32 devices in a mesh: band: 8 (over z, x), dx: 2 (over core), dy: 2 (over y).
Axes of the slice: x: 2, y: 2, z: 4, core: 2. Of those that a mesh axis runs over, the one named last changes fastest.
Arguments:
- waves: bfloat16 [512, 2, 2, 896], P('band', 'dx', 'dy'), may hold values from -6 to 6
- stiff: bfloat16 [343, 343], replicated, as said below
- cell_scale: float32 [2, 2, 4], P('dx', 'dy'), may hold values from 0.3 to 1
- cell_pot: float32 [2, 2, 4, 343], P('dx', 'dy'), may hold values from -1.5 to 1.5
- conn: int32 [2, 2, 4, 343], P('dx', 'dy'), may hold values from 0 to 895, as said below
- counts: int32 [2, 2], P('dx', 'dy'), may hold values from 1 to 4, as said below
- shared: int32 [2, 2, 4, 128], P('dx', 'dy'), may hold values from 0 to 895, as said below
- rotation: bfloat16 [512, 512], P('band'), may hold values from -0.25 to 0.25
Outputs:
- margin: float32 [512, 512], P('band', ('dx', 'dy'))
- rotated: bfloat16 [512, 2, 2, 896], P('band', 'dx', 'dy')
The draws below stay inside these ranges and needn't reach their ends.
Inputs may be any that keep to these rules, and one draw needn't show every extreme that they name: `conn`: each row lists 343 distinct local nodes of its partition. `counts`: cells in use of each partition; some partition uses all 4 cells, another only 1. `shared`: the four lists of a partition hold 512 distinct local nodes; entry k of a partition's upper list along dx (dy) and entry k of the lower list of the next partition along dx (dy) are the same mesh node. `stiff`: symmetric, with a dominant positive diagonal.
All inputs are finite; a program needn't handle non-finite values.
Results may differ from the reference program's by a relative error of at most 0.038.
Values may be sent and summed in bfloat16 or wider, within the bound.
No kernel may reach another device: no remote copies, remote signals or barrier semaphores. Data moves between devices by JAX's collectives and lax.ppermute only.
A program may use at most 64 MiB of HBM per device.

```python
import math
import jax
import jax.numpy as jnp
from jax import lax

NWF = 512
MAXC = 4
NODE_STEP = 224
NP = 343
DEGREE = 4
LN = 896
SHARE = 128
OWNED = 3072
N_DX = 2
N_DY = 2


def node_labels(key):
    base = jax.random.fold_in(key, 11)
    keys = jax.random.split(base, N_DX * N_DY)
    labels = jax.vmap(lambda single: jax.random.permutation(single, LN))(keys)
    return labels.reshape(N_DX, N_DY, LN).astype(jnp.int32)


def draw_conn(key, part):
    labels = node_labels(key)
    window = (jnp.arange(MAXC, dtype=jnp.int32)[:, None] * NODE_STEP + jnp.arange(NP, dtype=jnp.int32)[None, :]) % LN
    return labels[:, :, window]


def draw_shared(key, part):
    labels = node_labels(key)
    window = jnp.arange(4 * SHARE, dtype=jnp.int32).reshape(4, SHARE)
    return labels[:, :, window]


def draw_counts(key, part):
    domains = N_DX * N_DY
    drawn = jax.random.randint(jax.random.fold_in(key, 5), (domains,), MAXC // 4, MAXC + 1, dtype=jnp.int32)
    chosen = jax.random.randint(jax.random.fold_in(key, 6), (), 0, domains, dtype=jnp.int32)
    offset = jax.random.randint(jax.random.fold_in(key, 7), (), 1, domains, dtype=jnp.int32)
    lightest = (chosen + offset) % domains
    places = jnp.arange(domains, dtype=jnp.int32)
    filled = jnp.where(places == chosen, MAXC, drawn)
    filled = jnp.where(places == lightest, MAXC // 4, filled)
    return filled.reshape(N_DX, N_DY).astype(jnp.int32)


def draw_stiff(key, part):
    first = jax.random.fold_in(key, 1)
    second = jax.random.fold_in(key, 2)
    raw = jax.random.uniform(first, (NP, NP), jnp.float32, -1.0, 1.0)
    diagonal = jax.random.uniform(second, (NP,), jnp.float32, 2.1, 3.5)
    offdiag = (raw + raw.T) * (1.0 / NP)
    ident = jnp.arange(NP)[:, None] == jnp.arange(NP)[None, :]
    return jnp.where(ident, diagonal[:, None], offdiag).astype(jnp.bfloat16)


def shard_levels(key, dims, pieces, low, high):
    def one(dim, parts):
        heights = jax.random.uniform(jax.random.fold_in(jax.random.fold_in(key, 6), dim), (parts,), jnp.float32, low / len(pieces), high / len(pieces))
        return jnp.repeat(jnp.exp(heights), dims[dim] // parts).reshape((-1,) + (1,) * (len(dims) - dim - 1))

    level = one(*pieces[0])
    for cut in pieces[1:]:
        level = level * one(*cut)
    return level


def gaussian(rng, dims, scale, most, pieces=(), kind=jnp.bfloat16):
    array = jax.random.normal(rng, dims, jnp.float32) * scale
    if len(pieces) > 0:
        array = shard_levels(rng, dims, pieces, -0.22, 0.18) * array
    return jnp.clip(array, min=-most, max=most).astype(kind)


def setup_inputs(seed: int = 0) -> dict:
    streams_of = jax.random.split(jax.random.key(seed), 9)
    return {
        "waves": gaussian(streams_of[0], (NWF, N_DX, N_DY, LN), 1.0, 6.0, ((0, 8), (1, 2), (2, 2))),
        "stiff": draw_stiff(jax.random.fold_in(streams_of[8], 71), 0),
        "cell_scale": jnp.clip(jnp.exp(math.log(1.0) - 1.2039728 * jax.random.uniform(streams_of[2], (N_DX, N_DY, MAXC), jnp.float32) ** shard_levels(streams_of[2], (N_DX, N_DY, MAXC), ((0, 2), (1, 2)), -0.2, 0.2)), 0.3, 1.0),
        "cell_pot": jnp.clip(jax.random.uniform(streams_of[3], (N_DX, N_DY, MAXC, NP), jnp.float32, -1.5, 1.5) * shard_levels(streams_of[3], (N_DX, N_DY, MAXC, NP), ((0, 2), (1, 2)), -0.4, 0.0), -1.5, 1.5),
        "conn": draw_conn(jax.random.fold_in(streams_of[8], 71), 0),
        "counts": draw_counts(jax.random.fold_in(streams_of[8], 71), 0),
        "shared": draw_shared(jax.random.fold_in(streams_of[8], 71), 0),
        "rotation": gaussian(streams_of[7], (NWF, NWF), NWF ** -0.5, 0.25, ((0, 8),)),
    }


shift_center = 3.0
half_width = 6.0


def cell_local(values, stiff, scale, potential):
    product = jnp.einsum("wcq,pq->wcp", values.astype(jnp.float32), stiff.astype(jnp.float32))
    return product * scale[None, :, None] + potential[None] * values.astype(jnp.float32)


def assemble(fields, stiff, cell_scale, cell_pot, conn, counts, shared):
    domains = N_DX * N_DY
    width = fields.shape[1]

    def local_part(inputs):
        field, links, scale, potential, count = inputs
        active = (jnp.arange(MAXC, dtype=jnp.int32) < count).astype(jnp.float32)
        values = field[:, links]
        term = cell_local(values, stiff, scale * active, potential * active[:, None])
        return jnp.zeros((width, LN), jnp.float32).at[:, links].add(term)

    local = lax.map(local_part, (fields, conn.reshape(domains, MAXC, NP), cell_scale.reshape(domains, MAXC),
                                 cell_pot.reshape(domains, MAXC, NP), counts.reshape(domains)))
    lists = shared.reshape(domains, 4, SHARE)
    faces = jax.vmap(lambda part, index: part[:, index])(local, lists)
    faces = faces.reshape(N_DX, N_DY, width, 4, SHARE)
    zeros_x = jnp.zeros((1, N_DY, width, SHARE), jnp.float32)
    zeros_y = jnp.zeros((N_DX, 1, width, SHARE), jnp.float32)
    from_lower_x = jnp.concatenate([zeros_x, faces[:-1, :, :, 1]], axis=0)
    from_upper_x = jnp.concatenate([faces[1:, :, :, 0], zeros_x], axis=0)
    from_lower_y = jnp.concatenate([zeros_y, faces[:, :-1, :, 3]], axis=1)
    from_upper_y = jnp.concatenate([faces[:, 1:, :, 2], zeros_y], axis=1)
    received = jnp.stack([from_lower_x, from_upper_x, from_lower_y, from_upper_y], axis=3)
    received = received.reshape(domains, width, 4 * SHARE)
    return jax.vmap(lambda part, index, extra: part.at[:, index.reshape(-1)].add(extra))(local, lists, received)


def reference(waves, stiff, cell_scale, cell_pot, conn, counts, shared, rotation):
    domains = N_DX * N_DY
    width = waves.shape[0]
    initial = jnp.transpose(waves, (1, 2, 0, 3)).reshape(domains, width, LN).astype(jnp.float32)

    def operator(field):
        applied = assemble(field.astype(jnp.bfloat16), stiff, cell_scale, cell_pot, conn, counts, shared)
        return (applied - shift_center * field) / half_width

    previous = initial
    current = operator(initial)
    for degree_step in range(DEGREE - 1):
        previous, current = current, 2.0 * operator(current) - previous
    filtered = current.astype(jnp.bfloat16)

    lists = shared.reshape(domains, 4, SHARE)

    def owner_weight(index, domain):
        lower_x = (domain // N_DY) > 0
        lower_y = (domain % N_DY) > 0
        mask = jnp.ones((LN,), jnp.float32)
        mask = mask.at[index[0]].set(jnp.where(lower_x, 0.0, 1.0).astype(jnp.float32))
        mask = mask.at[index[2]].set(jnp.where(lower_y, 0.0, 1.0).astype(jnp.float32))
        return mask.astype(jnp.bfloat16)

    owners = jax.vmap(owner_weight)(lists, jnp.arange(domains, dtype=jnp.int32))

    def accumulate(total, inputs):
        block, mask = inputs
        weighted = (block * mask[None, :]).astype(jnp.float32)
        return total + jnp.dot(weighted, block.astype(jnp.float32).T, preferred_element_type=jnp.float32), None

    margin_sum, unused = lax.scan(accumulate, jnp.zeros((width, width), jnp.float32), (filtered, owners))
    margin = margin_sum * (1.0 / OWNED)
    rotated = lax.map(lambda block: jnp.dot(rotation.astype(jnp.float32), block.astype(jnp.float32),
                                            preferred_element_type=jnp.float32).astype(jnp.bfloat16), filtered)
    rotated = jnp.transpose(rotated.reshape(N_DX, N_DY, width, LN), (2, 0, 1, 3))
    return margin, rotated
```

```python
import functools

import jax
import jax.numpy as jnp
from jax import lax
from jax.experimental import pallas as pl
from jax.experimental.pallas import tpu as pltpu
from jax.sharding import PartitionSpec as P

DEGREE = 4
LANE = 128
SHIFT_CENTER = 3.0
HALF_WIDTH = 6.0
BF = jnp.bfloat16
F32 = jnp.float32
NT = (((1,), (1,)), ((), ()))
FACE = 4 * LANE

VMEM = pl.BlockSpec(memory_space=pltpu.VMEM)
HBM = pl.BlockSpec(memory_space=pltpu.HBM)


def iota(shape, dim):
    return lax.broadcasted_iota(jnp.int32, shape, dim)


def hot(mask):
    return mask.astype(F32).astype(BF)


def mm(a, b):
    return jnp.dot(a, b, preferred_element_type=F32)


def mm_nt(a, b):
    return lax.dot_general(a, b, NT, preferred_element_type=F32)


def apply_operator(field, matrix_ref, diagonal_ref):
    return mm(field.astype(BF), matrix_ref[...]) + field * diagonal_ref[0:1, :]


def build_kernel(
    spots, paired,
    counts_hbm, scale_hbm, conn_hbm, pot_hbm, shared_hbm, stiff_hbm, x_hbm,
    matrix_ref, diagonal_ref, perm_ref, y0_ref, rest_ref, *outs_and_scratch,
):
    sends = outs_and_scratch[: len(spots)]
    (count, scale, conn, pot, shared, stiff, x, tcat, vcat, off, table, links, sems) = outs_and_scratch[len(spots):]
    copies = [
        pltpu.make_async_copy(src, dst, sems.at[i])
        for i, (src, dst) in enumerate(
            ((counts_hbm, count), (scale_hbm, scale), (shared_hbm, shared), (conn_hbm, conn),
             (pot_hbm, pot), (stiff_hbm, stiff), (x_hbm, x))
        )
    ]
    for copy in copies:
        copy.start()
    cells, degree_nodes = conn.shape
    nodes = x.shape[1]
    wide = off.shape[0]
    off[...] = jnp.zeros_like(off)
    table[...] = jnp.zeros_like(table)
    links[...] = jnp.full(links.shape, -1, jnp.int32)
    for copy in copies:
        copy.wait()
    matrix = stiff[...]
    eye = iota(matrix.shape, 0) == iota(matrix.shape, 1)
    off[:degree_nodes, :degree_nodes] = jnp.where(eye, jnp.zeros_like(matrix), matrix)
    table[cells:cells + 1, :degree_nodes] = jnp.sum(
        jnp.where(eye, matrix.astype(F32), 0.0), axis=0, keepdims=True
    )
    table[:cells, :degree_nodes] = pot[...]
    links[:cells, :degree_nodes] = conn[...]
    if paired:
        first_x = 1 - lax.axis_index("dx")
        first_y = 1 - lax.axis_index("dy")
        order = (first_x, 1 - first_x, 2 + first_y, 3 - first_y)
    else:
        order = (0, 1, 2, 3)
    node = iota((nodes, LANE), 0)
    lane = iota((nodes, LANE), 1)
    for i in range(4):
        perm_ref[:, i * LANE:(i + 1) * LANE] = hot(node == shared[pl.ds(order[i], 1), :])
    on_face = mm(perm_ref[:, :FACE], jnp.ones((FACE, LANE), BF))
    inner = (1.0 - on_face).astype(BF)
    below = hot(iota((LANE, LANE), 1) < iota((LANE, LANE), 0))
    ranks = []
    seen = jnp.zeros((1, LANE), F32)
    for j in range(nodes // LANE):
        part = inner[j * LANE:(j + 1) * LANE]
        ranks.append(mm(below, part) + seen)
        seen = seen + jnp.sum(part.astype(F32), axis=0, keepdims=True)
    rank = jnp.concatenate(ranks, axis=0)
    rank = jnp.where(on_face > 0.5, -1.0, rank).astype(jnp.int32)
    for j in range((nodes - FACE) // LANE):
        perm_ref[:, FACE + j * LANE:FACE + (j + 1) * LANE] = hot(rank == lane + j * LANE)
    spot = iota((8, nodes), 1)
    digits = jnp.where(iota((8, nodes), 0) == 0, spot >> 4, spot & 15).astype(F32).astype(BF)
    place = mm_nt(digits, perm_ref[...]).astype(BF)
    y0 = mm(x[...], perm_ref[...])
    wide_node = iota((nodes, wide), 0)
    tail = degree_nodes + (-degree_nodes) % 16
    row = iota((16, wide), 0)
    diagonal = jnp.zeros((1, nodes), F32)
    for c in range(cells):
        used = c < count[0, 0]
        weight = jnp.where(used, scale[0, c], 0.0) * (2.0 / HALF_WIDTH)
        share = jnp.where(used, 2.0 / HALF_WIDTH, 0.0)
        link = links[c:c + 1, :]
        found = mm(place, hot(wide_node == link))
        where = jnp.where(link < 0, -1.0, found[0:1] * 16.0 + found[1:2]).astype(jnp.int32)
        select = hot(wide_node == where)
        tcat[:, c * wide:(c + 1) * wide] = select
        value = weight * table[cells:cells + 1, :] + share * table[c:c + 1, :]
        high = value.astype(BF).astype(F32)
        middle = (value - high).astype(BF).astype(F32)
        low = value - high - middle
        off[tail:tail + 16, :] = jnp.where(
            row == 0, high, jnp.where(row == 1, middle, jnp.where(row == 2, low, 0.0))
        ).astype(BF)
        moved = mm_nt(off[...], select)
        diagonal = diagonal + jnp.sum(moved[tail:tail + 16], axis=0, keepdims=True)
        vcat[c * wide:(c + 1) * wide, :] = (moved * weight).astype(BF)
    diagonal_ref[...] = jnp.broadcast_to(diagonal, diagonal_ref.shape)
    matrix_ref[...] = mm(tcat[...], vcat[...]).astype(BF)
    y0_ref[...] = y0
    applied = apply_operator(y0, matrix_ref, diagonal_ref)
    rest_ref[...] = 0.5 * (applied - y0)
    for send, at in zip(sends, spots):
        send[...] = applied[:, at:at + LANE].astype(BF)


def build(spots, paired, counts, scale, conn, pot, shared, stiff, x):
    cells, degree_nodes = conn.shape
    rows, nodes = x.shape
    wide = -(-(degree_nodes + 32) // LANE) * LANE
    f = lambda *s: jax.ShapeDtypeStruct(s, F32)
    b = lambda *s: jax.ShapeDtypeStruct(s, BF)
    outs = (b(nodes, nodes), f(8, nodes), b(nodes, nodes), f(rows, nodes), f(rows, nodes))
    outs += (b(rows, LANE),) * len(spots)
    return pl.pallas_call(
        functools.partial(build_kernel, spots, paired),
        out_shape=outs,
        in_specs=[HBM] * 7,
        out_specs=(VMEM,) * len(outs),
        scratch_shapes=[
            pltpu.SMEM(counts.shape, counts.dtype),
            pltpu.SMEM(scale.shape, F32),
            pltpu.VMEM(conn.shape, jnp.int32),
            pltpu.VMEM(pot.shape, F32),
            pltpu.VMEM(shared.shape, jnp.int32),
            pltpu.VMEM(stiff.shape, BF),
            pltpu.VMEM(x.shape, BF),
            pltpu.VMEM((nodes, cells * wide), BF),
            pltpu.VMEM((cells * wide, nodes), BF),
            pltpu.VMEM((wide, wide), BF),
            pltpu.VMEM((8, wide), F32),
            pltpu.VMEM((8, wide), jnp.int32),
            pltpu.SemaphoreType.DMA((7,)),
        ],
        compiler_params=pltpu.CompilerParams(vmem_limit_bytes=40 << 20),
        cost_estimate=pl.CostEstimate(flops=5_000_000_000, bytes_accessed=5_000_000, transcendentals=0),
        name="build",
    )(counts, scale, conn, pot, shared, stiff, x)


def step_kernel(spots, factor, last, matrix_ref, diagonal_ref, rest_ref, before_ref, *refs):
    count = len(spots)
    received = refs[:count]
    outs = refs[count:]
    field_ref = outs[0]
    field_ref[...] = rest_ref[...]
    for got, at in zip(received, spots):
        field_ref[:, at:at + LANE] += factor * got[...].astype(F32)
    field = field_ref[...]
    applied = apply_operator(field, matrix_ref, diagonal_ref)
    outs[1][...] = applied - field - before_ref[...]
    for send, at in zip(outs[2:], spots):
        send[...] = applied[:, at:at + LANE].astype(BF)


def step(spots, factor, matrix, diagonal, rest, before, received):
    rows, nodes = rest.shape
    field = jax.ShapeDtypeStruct((rows, nodes), F32)
    outs = (field, field) + (jax.ShapeDtypeStruct((rows, LANE), BF),) * len(spots)
    return pl.pallas_call(
        functools.partial(step_kernel, spots, factor, False),
        out_shape=outs,
        in_specs=[VMEM] * (4 + len(spots)),
        out_specs=(VMEM,) * len(outs),
        compiler_params=pltpu.CompilerParams(vmem_limit_bytes=16 << 20),
        cost_estimate=pl.CostEstimate(flops=110_000_000, bytes_accessed=3_000_000, transcendentals=0),
        name="step",
    )(matrix, diagonal, rest, before, *received)


def finish_kernel(spots, rest_ref, *refs):
    received, out_ref = refs[:-1], refs[-1]
    out_ref[...] = rest_ref[...].astype(BF)
    for got, at in zip(received, spots):
        out_ref[:, at:at + LANE] = (rest_ref[:, at:at + LANE] + got[...].astype(F32)).astype(BF)


def finish(spots, rest, received):
    return pl.pallas_call(
        functools.partial(finish_kernel, spots),
        out_shape=jax.ShapeDtypeStruct(rest.shape, BF),
        in_specs=[VMEM] * (1 + len(spots)),
        out_specs=VMEM,
        name="finish",
    )(rest, *received)


def owner_row(nodes, place_x, place_y):
    lane = iota((1, nodes), 1)
    hidden = ((lane < LANE) & (place_x > 0)) | ((lane >= 2 * LANE) & (lane < 3 * LANE) & (place_y > 0))
    return jnp.where(hidden, 0.0, 1.0)


def products_kernel(zs, own_ref, side_ref, mine_ref, other_ref, *refs):
    columns = refs[:zs - 1]
    rot_ref, turn_ref, keep_ref, give_ref, fields, pair, coef = refs[zs - 1:]
    width, nodes = own_ref.shape
    at = lax.axis_index("band")
    z, x = at // 2, at % 2
    fields[:, 1 - x] = jnp.zeros((zs, width, nodes), BF)
    fields[z, x] = own_ref[...]
    for k, column in enumerate(columns):
        fields[z ^ (k + 1), x] = column[...]
    coef[:width] = mine_ref[...]
    coef[width:] = other_ref[...]
    turned = mm(coef[...], fields[...].reshape(zs * 2 * width, nodes))
    rot_ref[...] = turned[:width]
    turn_ref[...] = turned[width:].astype(BF)
    owner = owner_row(nodes, lax.axis_index("dx"), lax.axis_index("dy"))
    pair[:width] = (own_ref[...].astype(F32) * owner).astype(BF)
    pair[width:] = (side_ref[...].astype(F32) * owner).astype(BF)
    p = lax.axis_index("dx") * 2 + lax.axis_index("dy")
    for j, ref in enumerate((keep_ref, keep_ref, give_ref, give_ref)):
        ref[j % 2] = mm_nt(fields[p ^ j, x], pair[...])


def products(zs, own, side, mine, other, columns):
    width, nodes = own.shape
    f = lambda *s: jax.ShapeDtypeStruct(s, F32)
    outs = (f(width, nodes), jax.ShapeDtypeStruct((width, nodes), BF),
            f(2, width, 2 * width), f(2, width, 2 * width))
    return pl.pallas_call(
        functools.partial(products_kernel, zs),
        out_shape=outs,
        in_specs=[VMEM] * (4 + len(columns)),
        out_specs=(VMEM,) * 4,
        scratch_shapes=[
            pltpu.VMEM((zs, 2, width, nodes), BF),
            pltpu.VMEM((2 * width, nodes), BF),
            pltpu.VMEM((2 * width, zs * 2 * width), BF),
        ],
        compiler_params=pltpu.CompilerParams(vmem_limit_bytes=16 << 20),
        cost_estimate=pl.CostEstimate(flops=200_000_000, bytes_accessed=2_000_000, transcendentals=0),
        name="products",
    )(own, side, mine, other, *columns)


def rotated_kernel(mine_ref, got_ref, perm_ref, out_ref):
    total = (mine_ref[...] + got_ref[...].astype(F32)).astype(BF)
    out_ref[...] = mm_nt(total, perm_ref[...]).astype(BF)


def rotated_of(mine, got, perm):
    return pl.pallas_call(
        rotated_kernel,
        out_shape=jax.ShapeDtypeStruct(mine.shape, BF),
        in_specs=[VMEM] * 3,
        out_specs=VMEM,
        compiler_params=pltpu.CompilerParams(vmem_limit_bytes=16 << 20),
        name="rotated",
    )(mine, got, perm)


def margin_kernel(owned, held_ref, got_ref, out_ref):
    width = held_ref.shape[0]
    x = lax.axis_index("band") % 2
    here = held_ref[...].T[:width] * (1.0 / owned)
    there = got_ref[...].T[:width] * (1.0 / owned)
    out_ref[:, :width] = jnp.where(x == 0, here, there)
    out_ref[:, width:] = jnp.where(x == 0, there, here)


def margin_of(owned, held, got):
    width = held.shape[0]
    return pl.pallas_call(
        functools.partial(margin_kernel, owned),
        out_shape=jax.ShapeDtypeStruct((width, 2 * width), F32),
        in_specs=[VMEM] * 2,
        out_specs=VMEM,
        name="margin",
    )(held, got)


def swap(value, axis):
    return lax.ppermute(value, axis, [(0, 1), (1, 0)])


def from_behind(block, axis, distance):
    devices = range(lax.axis_size(axis))
    route = [(i - distance, i) for i in devices if i - distance in devices]
    return lax.ppermute(block, axis, route)


def on_device(waves, stiff, cell_scale, cell_pot, conn, counts, shared, rotation):
    width, nodes = waves.shape[0], waves.shape[3]
    cells, degree_nodes = conn.shape[2:]
    share = shared.shape[3]
    count_x, count_y = lax.axis_size("dx"), lax.axis_size("dy")
    bands = lax.axis_size("band")
    owned = nodes * count_x * count_y - share * (2 * count_x * count_y - count_x - count_y)
    paired = count_x == 2 and count_y == 2 and bands == 2 * count_x * count_y
    x = waves.reshape(width, nodes)
    spots = (0, 2 * LANE) if paired else (0, LANE, 2 * LANE, 3 * LANE)

    def exchange(sends):
        if paired:
            return swap(sends[0], "dx"), swap(sends[1], "dy")
        return (
            from_behind(sends[1], "dx", 1), from_behind(sends[0], "dx", -1),
            from_behind(sends[3], "dy", 1), from_behind(sends[2], "dy", -1),
        )

    matrix, diagonal, perm, before, rest, *sends = build(
        spots, paired, counts.reshape(1, 1), cell_scale.reshape(1, cells),
        conn.reshape(cells, degree_nodes), cell_pot.reshape(cells, degree_nodes),
        shared.reshape(4, share), stiff, x,
    )
    for degree_step in range(DEGREE - 1):
        factor = 0.5 if degree_step == 0 else 1.0
        field, rest, *sends = step(spots, factor, matrix, diagonal, rest, before, exchange(sends))
        before = field
    filtered = finish(spots, rest, exchange(sends))

    if paired:
        across = [(i, i ^ 1) for i in range(bands)]
        other = lax.ppermute(rotation, "band", across)
        side = lax.ppermute(filtered, "band", across)
        zs = bands // 2
        columns = [
            lax.ppermute(filtered, "band", [(i, i ^ (2 * k)) for i in range(bands)])
            for k in range(1, zs)
        ]
        mine, turn, keep, give = products(zs, filtered, side, rotation, other, columns)
        got = lax.ppermute(turn, "band", across)
        half = keep + swap(give, "dx")
        block = half[0] + swap(half[1], "dy")
        margin = margin_of(owned, block, lax.ppermute(jnp.roll(block, width, axis=1), "band", across))
        rotated = rotated_of(mine, got, perm)
    else:
        gathered = lax.all_gather(filtered, "band", axis=0, tiled=True)
        owner = owner_row(nodes, lax.axis_index("dx"), lax.axis_index("dy")).astype(BF)
        block = mm_nt(filtered * owner, gathered)
        block = lax.psum_scatter(block, ("dx", "dy"), scatter_dimension=1, tiled=True)
        margin = block * (1.0 / owned)
        rotated = mm_nt(mm(rotation, gathered).astype(BF), perm).astype(BF)
    return margin, rotated.reshape(width, 1, 1, nodes)


def solution(mesh):
    return jax.shard_map(
        on_device,
        mesh=mesh,
        in_specs=(
            P("band", "dx", "dy", None),
            P(),
            P("dx", "dy", None),
            P("dx", "dy", None, None),
            P("dx", "dy", None, None),
            P("dx", "dy"),
            P("dx", "dy", None, None),
            P("band", None),
        ),
        out_specs=(P("band", ("dx", "dy")), P("band", "dx", "dy", None)),
        check_vma=False,
    )
```

```python
import functools

import jax
import jax.numpy as jnp
from jax import lax
from jax.experimental import pallas as pl
from jax.experimental.pallas import tpu as pltpu
from jax.sharding import PartitionSpec as P

DEGREE = 4
LANE = 128
SHIFT_CENTER = 3.0
HALF_WIDTH = 6.0
BF = jnp.bfloat16
F32 = jnp.float32
NT = (((1,), (1,)), ((), ()))
FACE = 4 * LANE

VMEM = pl.BlockSpec(memory_space=pltpu.VMEM)
HBM = pl.BlockSpec(memory_space=pltpu.HBM)


def iota(shape, dim):
    return lax.broadcasted_iota(jnp.int32, shape, dim)


def hot(mask):
    return mask.astype(F32).astype(BF)


def mm(a, b):
    return jnp.dot(a, b, preferred_element_type=F32)


def mm_nt(a, b):
    return lax.dot_general(a, b, NT, preferred_element_type=F32)


def apply_operator(field, matrix_ref, diagonal_ref):
    return mm(field.astype(BF), matrix_ref[...]) + field * diagonal_ref[0:1, :]


def build_kernel(
    spots, paired,
    counts_hbm, scale_hbm, conn_hbm, pot_hbm, shared_hbm, stiff_hbm, x_hbm,
    matrix_ref, diagonal_ref, perm_ref, y0_ref, rest_ref, *outs_and_scratch,
):
    sends = outs_and_scratch[: len(spots)]
    (count, scale, conn, pot, shared, stiff, x, tcat, vcat, off, table, links, sems) = outs_and_scratch[len(spots):]
    copies = [
        pltpu.make_async_copy(src, dst, sems.at[i])
        for i, (src, dst) in enumerate(
            ((counts_hbm, count), (scale_hbm, scale), (shared_hbm, shared), (conn_hbm, conn),
             (pot_hbm, pot), (stiff_hbm, stiff), (x_hbm, x))
        )
    ]
    for copy in copies:
        copy.start()
    cells, degree_nodes = conn.shape
    nodes = x.shape[1]
    wide = off.shape[0]
    off[...] = jnp.zeros_like(off)
    table[...] = jnp.zeros_like(table)
    links[...] = jnp.full(links.shape, -1, jnp.int32)
    for copy in copies:
        copy.wait()
    matrix = stiff[...]
    eye = iota(matrix.shape, 0) == iota(matrix.shape, 1)
    off[:degree_nodes, :degree_nodes] = jnp.where(eye, jnp.zeros_like(matrix), matrix)
    table[cells:cells + 1, :degree_nodes] = jnp.sum(
        jnp.where(eye, matrix.astype(F32), 0.0), axis=0, keepdims=True
    )
    table[:cells, :degree_nodes] = pot[...]
    links[:cells, :degree_nodes] = conn[...]
    if paired:
        first_x = 1 - lax.axis_index("dx")
        first_y = 1 - lax.axis_index("dy")
        order = (first_x, 1 - first_x, 2 + first_y, 3 - first_y)
    else:
        order = (0, 1, 2, 3)
    node = iota((nodes, LANE), 0)
    lane = iota((nodes, LANE), 1)
    for i in range(4):
        perm_ref[:, i * LANE:(i + 1) * LANE] = hot(node == shared[pl.ds(order[i], 1), :])
    on_face = mm(perm_ref[:, :FACE], jnp.ones((FACE, LANE), BF))
    inner = (1.0 - on_face).astype(BF)
    below = hot(iota((LANE, LANE), 1) < iota((LANE, LANE), 0))
    ranks = []
    seen = jnp.zeros((1, LANE), F32)
    for j in range(nodes // LANE):
        part = inner[j * LANE:(j + 1) * LANE]
        ranks.append(mm(below, part) + seen)
        seen = seen + jnp.sum(part.astype(F32), axis=0, keepdims=True)
    rank = jnp.concatenate(ranks, axis=0)
    rank = jnp.where(on_face > 0.5, -1.0, rank).astype(jnp.int32)
    for j in range((nodes - FACE) // LANE):
        perm_ref[:, FACE + j * LANE:FACE + (j + 1) * LANE] = hot(rank == lane + j * LANE)
    spot = iota((8, nodes), 1)
    digits = jnp.where(iota((8, nodes), 0) == 0, spot >> 4, spot & 15).astype(F32).astype(BF)
    place = mm_nt(digits, perm_ref[...]).astype(BF)
    y0 = mm(x[...], perm_ref[...])
    wide_node = iota((nodes, wide), 0)
    tail = degree_nodes + (-degree_nodes) % 16
    row = iota((16, wide), 0)
    diagonal = jnp.zeros((1, nodes), F32)
    for c in range(cells):
        share = jnp.where(c < count[0, 0], 2.0 / HALF_WIDTH, 0.0)
        weight = share * scale[0, c]
        link = links[c:c + 1, :]
        found = mm(place, hot(wide_node == link))
        where = jnp.where(link < 0, -1.0, found[0:1] * 16.0 + found[1:2]).astype(jnp.int32)
        select = hot(wide_node == where)
        tcat[:, c * wide:(c + 1) * wide] = select
        value = weight * table[cells:cells + 1, :] + share * table[c:c + 1, :]
        high = value.astype(BF).astype(F32)
        middle = (value - high).astype(BF).astype(F32)
        low = value - high - middle
        off[tail:tail + 16, :] = jnp.where(
            row == 0, high, jnp.where(row == 1, middle, jnp.where(row == 2, low, 0.0))
        ).astype(BF)
        moved = mm_nt(off[...], select)
        diagonal = diagonal + jnp.sum(moved[tail:tail + 16], axis=0, keepdims=True)
        vcat[c * wide:(c + 1) * wide, :] = (moved * weight).astype(BF)
    diagonal_ref[...] = jnp.broadcast_to(diagonal, diagonal_ref.shape)
    matrix_ref[...] = mm(tcat[...], vcat[...]).astype(BF)
    y0_ref[...] = y0
    applied = apply_operator(y0, matrix_ref, diagonal_ref)
    rest_ref[...] = 0.5 * (applied - y0)
    for send, at in zip(sends, spots):
        send[...] = applied[:, at:at + LANE].astype(BF)


def build(spots, paired, counts, scale, conn, pot, shared, stiff, x):
    cells, degree_nodes = conn.shape
    rows, nodes = x.shape
    wide = -(-(degree_nodes + 32) // LANE) * LANE
    f = lambda *s: jax.ShapeDtypeStruct(s, F32)
    b = lambda *s: jax.ShapeDtypeStruct(s, BF)
    outs = (b(nodes, nodes), f(8, nodes), b(nodes, nodes), f(rows, nodes), f(rows, nodes))
    outs += (b(rows, LANE),) * len(spots)
    return pl.pallas_call(
        functools.partial(build_kernel, spots, paired),
        out_shape=outs,
        in_specs=[HBM] * 7,
        out_specs=(VMEM,) * len(outs),
        scratch_shapes=[
            pltpu.SMEM(counts.shape, counts.dtype),
            pltpu.SMEM(scale.shape, F32),
            pltpu.VMEM(conn.shape, jnp.int32),
            pltpu.VMEM(pot.shape, F32),
            pltpu.VMEM(shared.shape, jnp.int32),
            pltpu.VMEM(stiff.shape, BF),
            pltpu.VMEM(x.shape, BF),
            pltpu.VMEM((nodes, cells * wide), BF),
            pltpu.VMEM((cells * wide, nodes), BF),
            pltpu.VMEM((wide, wide), BF),
            pltpu.VMEM((8, wide), F32),
            pltpu.VMEM((8, wide), jnp.int32),
            pltpu.SemaphoreType.DMA((7,)),
        ],
        compiler_params=pltpu.CompilerParams(vmem_limit_bytes=40 << 20),
        cost_estimate=pl.CostEstimate(flops=5_000_000_000, bytes_accessed=5_000_000, transcendentals=0),
        name="build",
    )(counts, *(pltpu.with_memory_space_constraint(v, pltpu.HBM) for v in (scale, conn, pot, shared, stiff, x)))


def step_kernel(spots, factor, matrix_ref, diagonal_ref, rest_ref, before_ref, *refs):
    count = len(spots)
    received = refs[:count]
    outs = refs[count:]
    field_ref = outs[0]
    field_ref[...] = rest_ref[...]
    for got, at in zip(received, spots):
        field_ref[:, at:at + LANE] += factor * got[...].astype(F32)
    field = field_ref[...]
    applied = apply_operator(field, matrix_ref, diagonal_ref)
    outs[1][...] = applied - field - before_ref[...]
    for send, at in zip(outs[2:], spots):
        send[...] = applied[:, at:at + LANE].astype(BF)


def step(spots, factor, matrix, diagonal, rest, before, received):
    rows, nodes = rest.shape
    field = jax.ShapeDtypeStruct((rows, nodes), F32)
    outs = (field, field) + (jax.ShapeDtypeStruct((rows, LANE), BF),) * len(spots)
    return pl.pallas_call(
        functools.partial(step_kernel, spots, factor),
        out_shape=outs,
        in_specs=[VMEM] * (4 + len(spots)),
        out_specs=(VMEM,) * len(outs),
        compiler_params=pltpu.CompilerParams(vmem_limit_bytes=16 << 20),
        cost_estimate=pl.CostEstimate(flops=110_000_000, bytes_accessed=3_000_000, transcendentals=0),
        name="step",
    )(matrix, diagonal, rest, before, *received)


def finish_kernel(spots, rest_ref, *refs):
    received, out_ref = refs[:-1], refs[-1]
    out_ref[...] = rest_ref[...].astype(BF)
    for got, at in zip(received, spots):
        out_ref[:, at:at + LANE] = (rest_ref[:, at:at + LANE] + got[...].astype(F32)).astype(BF)


def finish(spots, rest, received):
    return pl.pallas_call(
        functools.partial(finish_kernel, spots),
        out_shape=jax.ShapeDtypeStruct(rest.shape, BF),
        in_specs=[VMEM] * (1 + len(spots)),
        out_specs=VMEM,
        compiler_params=pltpu.CompilerParams(vmem_limit_bytes=8 << 20),
        name="finish",
    )(rest, *received)


def owner_row(nodes, place_x, place_y):
    lane = iota((1, nodes), 1)
    hidden = ((lane < LANE) & (place_x > 0)) | ((lane >= 2 * LANE) & (lane < 3 * LANE) & (place_y > 0))
    return jnp.where(hidden, 0.0, 1.0)


def products_kernel(hops, own_ref, side_ref, mine_ref, other_ref, *refs):
    zs = len(hops) + 1
    columns = refs[:zs - 1]
    rot_ref, turn_ref, mine_block_ref, other_block_ref, fields, pair, coef = refs[zs - 1:]
    width, nodes = own_ref.shape
    at = lax.axis_index("band")
    z, x = at // 2, at % 2
    fields[:, 1 - x] = jnp.zeros((zs, width, nodes), BF)
    fields[z, x] = own_ref[...]
    for k, column in zip(hops, columns):
        fields[z ^ k, x] = column[...]
    coef[:width] = mine_ref[...]
    coef[width:] = other_ref[...]
    turned = mm(coef[...], fields[...].reshape(zs * 2 * width, nodes))
    rot_ref[...] = turned[:width]
    turn_ref[...] = turned[width:].astype(BF)
    owner = owner_row(nodes, lax.axis_index("dx"), lax.axis_index("dy"))
    pair[:width] = (own_ref[...].astype(F32) * owner).astype(BF)
    pair[width:] = (side_ref[...].astype(F32) * owner).astype(BF)
    p = lax.axis_index("dx") * 2 + lax.axis_index("dy")
    for j in range(zs):
        block = mm_nt(pair[...], fields[p ^ j, x])
        mine_block_ref[j] = block[:width]
        other_block_ref[j] = block[width:]


def products(hops, own, side, mine, other, columns):
    width, nodes = own.shape
    zs = len(hops) + 1
    f = lambda *s: jax.ShapeDtypeStruct(s, F32)
    outs = (f(width, nodes), jax.ShapeDtypeStruct((width, nodes), BF),
            f(zs, width, width), f(zs, width, width))
    return pl.pallas_call(
        functools.partial(products_kernel, hops),
        out_shape=outs,
        in_specs=[VMEM] * (4 + len(columns)),
        out_specs=(VMEM,) * 4,
        scratch_shapes=[
            pltpu.VMEM((zs, 2, width, nodes), BF),
            pltpu.VMEM((2 * width, nodes), BF),
            pltpu.VMEM((2 * width, zs * 2 * width), BF),
        ],
        compiler_params=pltpu.CompilerParams(vmem_limit_bytes=16 << 20),
        cost_estimate=pl.CostEstimate(flops=200_000_000, bytes_accessed=2_000_000, transcendentals=0),
        name="products",
    )(own, side, mine, other, *columns)


def rotated_kernel(mine_ref, got_ref, perm_ref, out_ref):
    total = (mine_ref[...] + got_ref[...].astype(F32)).astype(BF)
    out_ref[...] = mm_nt(total, perm_ref[...]).astype(BF)


def rotated_of(mine, got, perm):
    return pl.pallas_call(
        rotated_kernel,
        out_shape=jax.ShapeDtypeStruct(mine.shape, BF),
        in_specs=[VMEM] * 3,
        out_specs=VMEM,
        compiler_params=pltpu.CompilerParams(vmem_limit_bytes=16 << 20),
        name="rotated",
    )(mine, got, perm)


def sides_kernel(mine_ref, got_ref, keep_ref, give_ref):
    width = mine_ref.shape[1]
    x = lax.axis_index("band") % 2
    for ref, base in ((keep_ref, 0), (give_ref, 2)):
        for j in range(2):
            here, there = mine_ref[base + j], got_ref[base + j]
            ref[j, :, :width] = jnp.where(x == 0, here, there)
            ref[j, :, width:] = jnp.where(x == 0, there, here)


def sides(mine, got):
    width = mine.shape[1]
    half = jax.ShapeDtypeStruct((2, width, 2 * width), F32)
    return pl.pallas_call(
        sides_kernel,
        out_shape=(half, half),
        in_specs=[VMEM] * 2,
        out_specs=(VMEM,) * 2,
        compiler_params=pltpu.CompilerParams(vmem_limit_bytes=8 << 20),
        name="sides",
    )(mine, got)


def swap(value, axis):
    return lax.ppermute(value, axis, [(0, 1), (1, 0)])


def from_behind(block, axis, distance):
    devices = range(lax.axis_size(axis))
    route = [(i - distance, i) for i in devices if i - distance in devices]
    return lax.ppermute(block, axis, route)


def on_device(waves, stiff, cell_scale, cell_pot, conn, counts, shared, rotation):
    width, nodes = waves.shape[0], waves.shape[3]
    cells, degree_nodes = conn.shape[2:]
    share = shared.shape[3]
    count_x, count_y = lax.axis_size("dx"), lax.axis_size("dy")
    bands = lax.axis_size("band")
    owned = nodes * count_x * count_y - share * (2 * count_x * count_y - count_x - count_y)
    paired = count_x == 2 and count_y == 2 and bands == 2 * count_x * count_y
    x = waves.reshape(width, nodes)
    spots = (0, 2 * LANE) if paired else (0, LANE, 2 * LANE, 3 * LANE)

    def exchange(sends):
        if paired:
            return swap(sends[0], "dx"), swap(sends[1], "dy")
        return (
            from_behind(sends[1], "dx", 1), from_behind(sends[0], "dx", -1),
            from_behind(sends[3], "dy", 1), from_behind(sends[2], "dy", -1),
        )

    matrix, diagonal, perm, before, rest, *sends = build(
        spots, paired, counts, cell_scale.reshape(1, cells),
        conn.reshape(cells, degree_nodes), cell_pot.reshape(cells, degree_nodes),
        shared.reshape(4, share), stiff, x,
    )
    for degree_step in range(DEGREE - 1):
        factor = 0.5 if degree_step == 0 else 1.0
        field, rest, *sends = step(spots, factor, matrix, diagonal, rest, before, exchange(sends))
        before = field
    filtered = finish(spots, rest, exchange(sends))

    if paired:
        across = [(i, i ^ 1) for i in range(bands)]
        other = lax.ppermute(rotation, "band", across)
        side = lax.ppermute(filtered, "band", across)
        zs = bands // 2
        hops = (2, 3, 1)
        columns = [
            lax.ppermute(filtered, "band", [(i, i ^ (2 * k)) for i in range(bands)])
            for k in hops
        ]
        mine, turn, mine_block, other_block = products(hops, filtered, side, rotation, other, columns)
        keep, give = sides(mine_block, lax.ppermute(other_block, "band", across))
        got = lax.ppermute(turn, "band", across)
        half = keep + swap(give, "dx")
        margin = (half[0] + swap(half[1], "dy")) * (1.0 / owned)
        rotated = rotated_of(mine, got, perm)
    else:
        gathered = lax.all_gather(filtered, "band", axis=0, tiled=True)
        owner = owner_row(nodes, lax.axis_index("dx"), lax.axis_index("dy")).astype(BF)
        block = mm_nt(filtered * owner, gathered)
        block = lax.psum_scatter(block, ("dx", "dy"), scatter_dimension=1, tiled=True)
        margin = block * (1.0 / owned)
        rotated = mm_nt(mm(rotation, gathered).astype(BF), perm).astype(BF)
    return margin, rotated.reshape(width, 1, 1, nodes)


def solution(mesh):
    return jax.shard_map(
        on_device,
        mesh=mesh,
        in_specs=(
            P("band", "dx", "dy", None),
            P(),
            P("dx", "dy", None),
            P("dx", "dy", None, None),
            P("dx", "dy", None, None),
            P("dx", "dy"),
            P("dx", "dy", None, None),
            P("band", None),
        ),
        out_specs=(P("band", ("dx", "dy")), P("band", "dx", "dy", None)),
        check_vma=False,
    )
```

```python
import functools

import jax
import jax.numpy as jnp
from jax import lax
from jax.experimental import pallas as pl
from jax.experimental.pallas import tpu as pltpu
from jax.sharding import PartitionSpec as P

DEGREE = 4
LANE = 128
SHIFT_CENTER = 3.0
HALF_WIDTH = 6.0
BF = jnp.bfloat16
F32 = jnp.float32
NT = (((1,), (1,)), ((), ()))
FACE = 4 * LANE

VMEM = pl.BlockSpec(memory_space=pltpu.VMEM)
HBM = pl.BlockSpec(memory_space=pltpu.HBM)


def iota(shape, dim):
    return lax.broadcasted_iota(jnp.int32, shape, dim)


def hot(mask):
    return mask.astype(F32).astype(BF)


def mm(a, b):
    return jnp.dot(a, b, preferred_element_type=F32)


def mm_nt(a, b):
    return lax.dot_general(a, b, NT, preferred_element_type=F32)


def apply_operator(field, matrix_ref, diagonal_ref):
    return mm(field.astype(BF), matrix_ref[...]) + field * diagonal_ref[0:1, :]


def build_kernel(
    spots, paired,
    counts_hbm, scale_hbm, conn_hbm, pot_hbm, shared_hbm, stiff_hbm, x_hbm,
    matrix_ref, diagonal_ref, perm_ref, y0_ref, rest_ref, *outs_and_scratch,
):
    sends = outs_and_scratch[: len(spots)]
    (count, scale, conn, pot, shared, stiff, x, tcat, vcat, off, table, links, sems) = outs_and_scratch[len(spots):]
    copies = [
        pltpu.make_async_copy(src, dst, sems.at[i])
        for i, (src, dst) in enumerate(
            ((counts_hbm, count), (scale_hbm, scale), (shared_hbm, shared), (conn_hbm, conn),
             (pot_hbm, pot), (stiff_hbm, stiff), (x_hbm, x))
        )
    ]
    for copy in copies:
        copy.start()
    cells, degree_nodes = conn.shape
    nodes = x.shape[1]
    wide = off.shape[0]
    off[...] = jnp.zeros_like(off)
    table[...] = jnp.zeros_like(table)
    links[...] = jnp.full(links.shape, -1, jnp.int32)
    for copy in copies:
        copy.wait()
    matrix = stiff[...]
    eye = iota(matrix.shape, 0) == iota(matrix.shape, 1)
    off[:degree_nodes, :degree_nodes] = jnp.where(eye, jnp.zeros_like(matrix), matrix)
    table[cells:cells + 1, :degree_nodes] = jnp.sum(
        jnp.where(eye, matrix.astype(F32), 0.0), axis=0, keepdims=True
    )
    table[:cells, :degree_nodes] = pot[...]
    links[:cells, :degree_nodes] = conn[...]
    if paired:
        first_x = 1 - lax.axis_index("dx")
        first_y = 1 - lax.axis_index("dy")
        order = (first_x, 1 - first_x, 2 + first_y, 3 - first_y)
    else:
        order = (0, 1, 2, 3)
    node = iota((nodes, LANE), 0)
    lane = iota((nodes, LANE), 1)
    for i in range(4):
        perm_ref[:, i * LANE:(i + 1) * LANE] = hot(node == shared[pl.ds(order[i], 1), :])
    on_face = mm(perm_ref[:, :FACE], jnp.ones((FACE, LANE), BF))
    inner = (1.0 - on_face).astype(BF)
    below = hot(iota((LANE, LANE), 1) < iota((LANE, LANE), 0))
    ranks = []
    seen = jnp.zeros((1, LANE), F32)
    for j in range(nodes // LANE):
        part = inner[j * LANE:(j + 1) * LANE]
        ranks.append(mm(below, part) + seen)
        seen = seen + jnp.sum(part.astype(F32), axis=0, keepdims=True)
    rank = jnp.concatenate(ranks, axis=0)
    rank = jnp.where(on_face > 0.5, -1.0, rank).astype(jnp.int32)
    for j in range((nodes - FACE) // LANE):
        perm_ref[:, FACE + j * LANE:FACE + (j + 1) * LANE] = hot(rank == lane + j * LANE)
    spot = iota((8, nodes), 1)
    digits = jnp.where(iota((8, nodes), 0) == 0, spot >> 4, spot & 15).astype(F32).astype(BF)
    place = mm_nt(digits, perm_ref[...]).astype(BF)
    y0 = mm(x[...], perm_ref[...])
    wide_node = iota((nodes, wide), 0)
    tail = degree_nodes + (-degree_nodes) % 16
    row = iota((16, wide), 0)
    diagonal = jnp.zeros((1, nodes), F32)
    for c in range(cells):
        share = jnp.where(c < count[0, 0], 2.0 / HALF_WIDTH, 0.0)
        weight = share * scale[0, c]
        link = links[c:c + 1, :]
        found = mm(place, hot(wide_node == link))
        where = jnp.where(link < 0, -1.0, found[0:1] * 16.0 + found[1:2]).astype(jnp.int32)
        select = hot(wide_node == where)
        tcat[:, c * wide:(c + 1) * wide] = select
        value = weight * table[cells:cells + 1, :] + share * table[c:c + 1, :]
        high = value.astype(BF).astype(F32)
        middle = (value - high).astype(BF).astype(F32)
        low = value - high - middle
        off[tail:tail + 16, :] = jnp.where(
            row == 0, high, jnp.where(row == 1, middle, jnp.where(row == 2, low, 0.0))
        ).astype(BF)
        moved = mm_nt(off[...], select)
        diagonal = diagonal + jnp.sum(moved[tail:tail + 16], axis=0, keepdims=True)
        vcat[c * wide:(c + 1) * wide, :] = (moved * weight).astype(BF)
    diagonal_ref[...] = jnp.broadcast_to(diagonal, diagonal_ref.shape)
    matrix_ref[:FACE, :] = mm(tcat[:FACE, :], vcat[...]).astype(BF)
    matrix_ref[FACE:, FACE:] = mm(tcat[FACE:, :], vcat[:, FACE:]).astype(BF)
    matrix_ref[FACE:, :FACE] = matrix_ref[:FACE, FACE:].T
    y0_ref[...] = y0
    applied = apply_operator(y0, matrix_ref, diagonal_ref)
    rest_ref[...] = 0.5 * (applied - y0)
    for send, at in zip(sends, spots):
        send[...] = applied[:, at:at + LANE].astype(BF)


def build(spots, paired, counts, scale, conn, pot, shared, stiff, x):
    cells, degree_nodes = conn.shape
    rows, nodes = x.shape
    wide = -(-(degree_nodes + 32) // LANE) * LANE
    f = lambda *s: jax.ShapeDtypeStruct(s, F32)
    b = lambda *s: jax.ShapeDtypeStruct(s, BF)
    outs = (b(nodes, nodes), f(8, nodes), b(nodes, nodes), f(rows, nodes), f(rows, nodes))
    outs += (b(rows, LANE),) * len(spots)
    return pl.pallas_call(
        functools.partial(build_kernel, spots, paired),
        out_shape=outs,
        in_specs=[HBM] * 7,
        out_specs=(VMEM,) * len(outs),
        scratch_shapes=[
            pltpu.SMEM(counts.shape, counts.dtype),
            pltpu.SMEM(scale.shape, F32),
            pltpu.VMEM(conn.shape, jnp.int32),
            pltpu.VMEM(pot.shape, F32),
            pltpu.VMEM(shared.shape, jnp.int32),
            pltpu.VMEM(stiff.shape, BF),
            pltpu.VMEM(x.shape, BF),
            pltpu.VMEM((nodes, cells * wide), BF),
            pltpu.VMEM((cells * wide, nodes), BF),
            pltpu.VMEM((wide, wide), BF),
            pltpu.VMEM((8, wide), F32),
            pltpu.VMEM((8, wide), jnp.int32),
            pltpu.SemaphoreType.DMA((7,)),
        ],
        compiler_params=pltpu.CompilerParams(vmem_limit_bytes=40 << 20),
        cost_estimate=pl.CostEstimate(flops=5_000_000_000, bytes_accessed=5_000_000, transcendentals=0),
        name="build",
    )(counts, *(pltpu.with_memory_space_constraint(v, pltpu.HBM) for v in (scale, conn, pot, shared, stiff, x)))


def step_kernel(spots, factor, last, matrix_ref, diagonal_ref, rest_ref, before_ref, *refs):
    count = len(spots)
    received = refs[:count]
    outs = refs[count:]
    field_ref, outs = (outs[-1], outs[:-1]) if last else (outs[0], outs[1:])
    field_ref[...] = rest_ref[...]
    for got, at in zip(received, spots):
        field_ref[:, at:at + LANE] += factor * got[...].astype(F32)
    field = field_ref[...]
    applied = apply_operator(field, matrix_ref, diagonal_ref)
    outs[0][...] = applied - field - before_ref[...]
    for send, at in zip(outs[1:], spots):
        send[...] = applied[:, at:at + LANE].astype(BF)


def step(spots, factor, last, matrix, diagonal, rest, before, received):
    rows, nodes = rest.shape
    field = jax.ShapeDtypeStruct((rows, nodes), F32)
    outs = (field,) * (1 if last else 2) + (jax.ShapeDtypeStruct((rows, LANE), BF),) * len(spots)
    return pl.pallas_call(
        functools.partial(step_kernel, spots, factor, last),
        out_shape=outs,
        in_specs=[VMEM] * (4 + len(spots)),
        out_specs=(VMEM,) * len(outs),
        scratch_shapes=[pltpu.VMEM((rows, nodes), F32)] if last else [],
        compiler_params=pltpu.CompilerParams(vmem_limit_bytes=16 << 20),
        cost_estimate=pl.CostEstimate(flops=110_000_000, bytes_accessed=3_000_000, transcendentals=0),
        name="step",
    )(matrix, diagonal, rest, before, *received)


def finish_kernel(spots, rest_ref, *refs):
    received, out_ref = refs[:-1], refs[-1]
    out_ref[...] = rest_ref[...].astype(BF)
    for got, at in zip(received, spots):
        out_ref[:, at:at + LANE] = (rest_ref[:, at:at + LANE] + got[...].astype(F32)).astype(BF)


def finish(spots, rest, received):
    return pl.pallas_call(
        functools.partial(finish_kernel, spots),
        out_shape=jax.ShapeDtypeStruct(rest.shape, BF),
        in_specs=[VMEM] * (1 + len(spots)),
        out_specs=VMEM,
        compiler_params=pltpu.CompilerParams(vmem_limit_bytes=8 << 20),
        name="finish",
    )(rest, *received)


def owner_row(nodes, place_x, place_y):
    lane = iota((1, nodes), 1)
    hidden = ((lane < LANE) & (place_x > 0)) | ((lane >= 2 * LANE) & (lane < 3 * LANE) & (place_y > 0))
    return jnp.where(hidden, 0.0, 1.0)


def products_kernel(hops, own_ref, side_ref, mine_ref, other_ref, *refs):
    zs = len(hops) + 1
    columns = refs[:zs - 1]
    rot_ref, turn_ref, keep_ref, give_ref, fields, pair, coef = refs[zs - 1:]
    width, nodes = own_ref.shape
    at = lax.axis_index("band")
    z, x = at // 2, at % 2
    fields[:, 1 - x] = jnp.zeros((zs, width, nodes), BF)
    fields[z, x] = own_ref[...]
    for k, column in zip(hops, columns):
        fields[z ^ k, x] = column[...]
    coef[:width] = mine_ref[...]
    coef[width:] = other_ref[...]
    turned = mm(coef[...], fields[...].reshape(zs * 2 * width, nodes))
    rot_ref[...] = turned[:width]
    turn_ref[...] = turned[width:].astype(BF)
    owner = owner_row(nodes, lax.axis_index("dx"), lax.axis_index("dy"))
    pair[:width] = (own_ref[...].astype(F32) * owner).astype(BF)
    pair[width:] = (side_ref[...].astype(F32) * owner).astype(BF)
    p = lax.axis_index("dx") * 2 + lax.axis_index("dy")
    for j, ref in enumerate((keep_ref, keep_ref, give_ref, give_ref)):
        ref[j % 2] = mm_nt(fields[p ^ j, x], pair[...])


def products(hops, own, side, mine, other, columns):
    width, nodes = own.shape
    zs = len(hops) + 1
    f = lambda *s: jax.ShapeDtypeStruct(s, F32)
    outs = (f(width, nodes), jax.ShapeDtypeStruct((width, nodes), BF),
            f(2, width, 2 * width), f(2, width, 2 * width))
    return pl.pallas_call(
        functools.partial(products_kernel, hops),
        out_shape=outs,
        in_specs=[VMEM] * (4 + len(columns)),
        out_specs=(VMEM,) * 4,
        scratch_shapes=[
            pltpu.VMEM((zs, 2, width, nodes), BF),
            pltpu.VMEM((2 * width, nodes), BF),
            pltpu.VMEM((2 * width, zs * 2 * width), BF),
        ],
        compiler_params=pltpu.CompilerParams(vmem_limit_bytes=16 << 20),
        cost_estimate=pl.CostEstimate(flops=200_000_000, bytes_accessed=2_000_000, transcendentals=0),
        name="products",
    )(own, side, mine, other, *columns)


def finale_kernel(owned, mine_ref, got_ref, perm_ref, held_ref, side_ref, margin_ref, rotated_ref):
    total = (mine_ref[...] + got_ref[...].astype(F32)).astype(BF)
    rotated_ref[...] = mm_nt(total, perm_ref[...]).astype(BF)
    width = held_ref.shape[0]
    x = lax.axis_index("band") % 2
    here = held_ref[...].T[:width] * (1.0 / owned)
    there = side_ref[...].T[width:] * (1.0 / owned)
    margin_ref[:, :width] = jnp.where(x == 0, here, there)
    margin_ref[:, width:] = jnp.where(x == 0, there, here)


def finale(owned, mine, got, perm, held, side):
    width = held.shape[0]
    return pl.pallas_call(
        functools.partial(finale_kernel, owned),
        out_shape=(jax.ShapeDtypeStruct((width, 2 * width), F32), jax.ShapeDtypeStruct(mine.shape, BF)),
        in_specs=[VMEM] * 5,
        out_specs=(VMEM,) * 2,
        compiler_params=pltpu.CompilerParams(vmem_limit_bytes=16 << 20),
        name="finale",
    )(mine, got, perm, held, side)


def swap(value, axis):
    return lax.ppermute(value, axis, [(0, 1), (1, 0)])


def from_behind(block, axis, distance):
    devices = range(lax.axis_size(axis))
    route = [(i - distance, i) for i in devices if i - distance in devices]
    return lax.ppermute(block, axis, route)


def on_device(waves, stiff, cell_scale, cell_pot, conn, counts, shared, rotation):
    width, nodes = waves.shape[0], waves.shape[3]
    cells, degree_nodes = conn.shape[2:]
    share = shared.shape[3]
    count_x, count_y = lax.axis_size("dx"), lax.axis_size("dy")
    bands = lax.axis_size("band")
    owned = nodes * count_x * count_y - share * (2 * count_x * count_y - count_x - count_y)
    paired = count_x == 2 and count_y == 2 and bands == 2 * count_x * count_y
    x = waves.reshape(width, nodes)
    spots = (0, 2 * LANE) if paired else (0, LANE, 2 * LANE, 3 * LANE)

    def exchange(sends):
        if paired:
            return swap(sends[0], "dx"), swap(sends[1], "dy")
        return (
            from_behind(sends[1], "dx", 1), from_behind(sends[0], "dx", -1),
            from_behind(sends[3], "dy", 1), from_behind(sends[2], "dy", -1),
        )

    matrix, diagonal, perm, before, rest, *sends = build(
        spots, paired, counts, cell_scale.reshape(1, cells),
        conn.reshape(cells, degree_nodes), cell_pot.reshape(cells, degree_nodes),
        shared.reshape(4, share), stiff, x,
    )
    for degree_step in range(DEGREE - 1):
        factor = 0.5 if degree_step == 0 else 1.0
        received = exchange(sends)
        if degree_step < DEGREE - 2:
            field, rest, *sends = step(spots, factor, False, matrix, diagonal, rest, before, received)
            before = field
        else:
            rest, *sends = step(spots, factor, True, matrix, diagonal, rest, before, received)
    filtered = finish(spots, rest, exchange(sends))

    if paired:
        across = [(i, i ^ 1) for i in range(bands)]
        other = lax.ppermute(rotation, "band", across)
        side = lax.ppermute(filtered, "band", across)
        zs = bands // 2
        hops = (2, 3, 1)
        columns = [
            lax.ppermute(filtered, "band", [(i, i ^ (2 * k)) for i in range(bands)])
            for k in hops
        ]
        mine, turn, keep, give = products(hops, filtered, side, rotation, other, columns)
        got = lax.ppermute(turn, "band", across)
        half = keep + swap(give, "dx")
        block = half[0] + swap(half[1], "dy")
        margin, rotated = finale(owned, mine, got, perm, block, lax.ppermute(block, "band", across))
    else:
        gathered = lax.all_gather(filtered, "band", axis=0, tiled=True)
        owner = owner_row(nodes, lax.axis_index("dx"), lax.axis_index("dy")).astype(BF)
        block = mm_nt(filtered * owner, gathered)
        block = lax.psum_scatter(block, ("dx", "dy"), scatter_dimension=1, tiled=True)
        margin = block * (1.0 / owned)
        rotated = mm_nt(mm(rotation, gathered).astype(BF), perm).astype(BF)
    return margin, rotated.reshape(width, 1, 1, nodes)


def solution(mesh):
    return jax.shard_map(
        on_device,
        mesh=mesh,
        in_specs=(
            P("band", "dx", "dy", None),
            P(),
            P("dx", "dy", None),
            P("dx", "dy", None, None),
            P("dx", "dy", None, None),
            P("dx", "dy"),
            P("dx", "dy", None, None),
            P("band", None),
        ),
        out_specs=(P("band", ("dx", "dy")), P("band", "dx", "dy", None)),
        check_vma=False,
    )
```

```python
import functools

import jax
import jax.numpy as jnp
from jax import lax
from jax.experimental import pallas as pl
from jax.experimental.pallas import tpu as pltpu
from jax.sharding import PartitionSpec as P

DEGREE = 4
LANE = 128
SHIFT_CENTER = 3.0
HALF_WIDTH = 6.0
BF = jnp.bfloat16
F32 = jnp.float32
NT = (((1,), (1,)), ((), ()))
FACE = 4 * LANE

VMEM = pl.BlockSpec(memory_space=pltpu.VMEM)
HBM = pl.BlockSpec(memory_space=pltpu.HBM)


def iota(shape, dim):
    return lax.broadcasted_iota(jnp.int32, shape, dim)


def hot(mask):
    return mask.astype(F32).astype(BF)


def mm(a, b):
    return jnp.dot(a, b, preferred_element_type=F32)


def mm_nt(a, b):
    return lax.dot_general(a, b, NT, preferred_element_type=F32)


def apply_operator(field, matrix_ref, diagonal_ref):
    return mm(field.astype(BF), matrix_ref[...]) + field * diagonal_ref[0:1, :]


def build_kernel(
    spots, paired,
    counts_hbm, scale_hbm, conn_hbm, pot_hbm, shared_hbm, stiff_hbm, x_hbm,
    matrix_ref, diagonal_ref, perm_ref, y0_ref, rest_ref, *outs_and_scratch,
):
    sends = outs_and_scratch[: len(spots)]
    (count, scale, conn, pot, shared, stiff, x, tcat, vcat, off, table, links, sems) = outs_and_scratch[len(spots):]
    copies = [
        pltpu.make_async_copy(src, dst, sems.at[i])
        for i, (src, dst) in enumerate(
            ((counts_hbm, count), (scale_hbm, scale), (shared_hbm, shared), (conn_hbm, conn),
             (pot_hbm, pot), (stiff_hbm, stiff), (x_hbm, x))
        )
    ]
    for copy in copies:
        copy.start()
    cells, degree_nodes = conn.shape
    nodes = x.shape[1]
    wide = off.shape[0]
    off[...] = jnp.zeros_like(off)
    table[...] = jnp.zeros_like(table)
    links[...] = jnp.full(links.shape, -1, jnp.int32)
    for copy in copies:
        copy.wait()
    matrix = stiff[...]
    eye = iota(matrix.shape, 0) == iota(matrix.shape, 1)
    off[:degree_nodes, :degree_nodes] = jnp.where(eye, jnp.zeros_like(matrix), matrix)
    table[cells:cells + 1, :degree_nodes] = jnp.sum(
        jnp.where(eye, matrix.astype(F32), 0.0), axis=0, keepdims=True
    )
    table[:cells, :degree_nodes] = pot[...]
    links[:cells, :degree_nodes] = conn[...]
    if paired:
        first_x = 1 - lax.axis_index("dx")
        first_y = 1 - lax.axis_index("dy")
        order = (first_x, 1 - first_x, 2 + first_y, 3 - first_y)
    else:
        order = (0, 1, 2, 3)
    node = iota((nodes, LANE), 0)
    lane = iota((nodes, LANE), 1)
    for i in range(4):
        perm_ref[:, i * LANE:(i + 1) * LANE] = hot(node == shared[pl.ds(order[i], 1), :])
    on_face = mm(perm_ref[:, :FACE], jnp.ones((FACE, LANE), BF))
    inner = (1.0 - on_face).astype(BF)
    below = hot(iota((LANE, LANE), 1) < iota((LANE, LANE), 0))
    ranks = []
    seen = jnp.zeros((1, LANE), F32)
    for j in range(nodes // LANE):
        part = inner[j * LANE:(j + 1) * LANE]
        ranks.append(mm(below, part) + seen)
        seen = seen + jnp.sum(part.astype(F32), axis=0, keepdims=True)
    rank = jnp.concatenate(ranks, axis=0)
    rank = jnp.where(on_face > 0.5, -1.0, rank).astype(jnp.int32)
    for j in range((nodes - FACE) // LANE):
        perm_ref[:, FACE + j * LANE:FACE + (j + 1) * LANE] = hot(rank == lane + j * LANE)
    spot = iota((8, nodes), 1)
    digits = jnp.where(iota((8, nodes), 0) == 0, spot >> 4, spot & 15).astype(F32).astype(BF)
    place = mm_nt(digits, perm_ref[...]).astype(BF)
    y0 = mm(x[...], perm_ref[...])
    wide_node = iota((nodes, wide), 0)
    tail = degree_nodes + (-degree_nodes) % 16
    row = iota((16, wide), 0)
    diagonal = jnp.zeros((1, nodes), F32)
    for c in range(cells):
        share = jnp.where(c < count[0, 0], 2.0 / HALF_WIDTH, 0.0)
        weight = share * scale[0, c]
        link = links[c:c + 1, :]
        found = mm(place, hot(wide_node == link))
        where = jnp.where(link < 0, -1.0, found[0:1] * 16.0 + found[1:2]).astype(jnp.int32)
        select = hot(wide_node == where)
        tcat[:, c * wide:(c + 1) * wide] = select
        value = weight * table[cells:cells + 1, :] + share * table[c:c + 1, :]
        high = value.astype(BF).astype(F32)
        middle = (value - high).astype(BF).astype(F32)
        low = value - high - middle
        off[tail:tail + 16, :] = jnp.where(
            row == 0, high, jnp.where(row == 1, middle, jnp.where(row == 2, low, 0.0))
        ).astype(BF)
        moved = mm_nt(off[...], select)
        diagonal = diagonal + jnp.sum(moved[tail:tail + 16], axis=0, keepdims=True)
        vcat[c * wide:(c + 1) * wide, :] = (moved * weight).astype(BF)
    diagonal_ref[...] = jnp.broadcast_to(diagonal, diagonal_ref.shape)
    matrix_ref[:FACE, :] = mm(tcat[:FACE, :], vcat[...]).astype(BF)
    matrix_ref[FACE:, FACE:] = mm(tcat[FACE:, :], vcat[:, FACE:]).astype(BF)
    matrix_ref[FACE:, :FACE] = matrix_ref[:FACE, FACE:].T
    y0_ref[...] = y0
    applied = apply_operator(y0, matrix_ref, diagonal_ref)
    rest_ref[...] = 0.5 * (applied - y0)
    for send, at in zip(sends, spots):
        send[...] = applied[:, at:at + LANE].astype(BF)


def build(spots, paired, counts, scale, conn, pot, shared, stiff, x):
    cells, degree_nodes = conn.shape
    rows, nodes = x.shape
    wide = -(-(degree_nodes + 32) // LANE) * LANE
    f = lambda *s: jax.ShapeDtypeStruct(s, F32)
    b = lambda *s: jax.ShapeDtypeStruct(s, BF)
    outs = (b(nodes, nodes), f(8, nodes), b(nodes, nodes), f(rows, nodes), f(rows, nodes))
    outs += (b(rows, LANE),) * len(spots)
    return pl.pallas_call(
        functools.partial(build_kernel, spots, paired),
        out_shape=outs,
        in_specs=[HBM] * 7,
        out_specs=(VMEM,) * len(outs),
        scratch_shapes=[
            pltpu.SMEM(counts.shape, counts.dtype),
            pltpu.SMEM(scale.shape, F32),
            pltpu.VMEM(conn.shape, jnp.int32),
            pltpu.VMEM(pot.shape, F32),
            pltpu.VMEM(shared.shape, jnp.int32),
            pltpu.VMEM(stiff.shape, BF),
            pltpu.VMEM(x.shape, BF),
            pltpu.VMEM((nodes, cells * wide), BF),
            pltpu.VMEM((cells * wide, nodes), BF),
            pltpu.VMEM((wide, wide), BF),
            pltpu.VMEM((8, wide), F32),
            pltpu.VMEM((8, wide), jnp.int32),
            pltpu.SemaphoreType.DMA((7,)),
        ],
        compiler_params=pltpu.CompilerParams(vmem_limit_bytes=40 << 20),
        cost_estimate=pl.CostEstimate(flops=5_000_000_000, bytes_accessed=5_000_000, transcendentals=0),
        name="build",
    )(counts, *(pltpu.with_memory_space_constraint(v, pltpu.HBM) for v in (scale, conn, pot, shared, stiff, x)))


def step_kernel(spots, factor, last, matrix_ref, diagonal_ref, rest_ref, before_ref, *refs):
    count = len(spots)
    received = refs[:count]
    outs = refs[count:]
    field_ref, outs = (outs[-1], outs[:-1]) if last else (outs[0], outs[1:])
    field_ref[...] = rest_ref[...]
    for got, at in zip(received, spots):
        field_ref[:, at:at + LANE] += factor * got[...].astype(F32)
    field = field_ref[...]
    applied = apply_operator(field, matrix_ref, diagonal_ref)
    outs[0][...] = applied - field - before_ref[...]
    for send, at in zip(outs[1:], spots):
        send[...] = applied[:, at:at + LANE].astype(BF)


def step(spots, factor, last, matrix, diagonal, rest, before, received):
    rows, nodes = rest.shape
    field = jax.ShapeDtypeStruct((rows, nodes), F32)
    outs = (field,) * (1 if last else 2) + (jax.ShapeDtypeStruct((rows, LANE), BF),) * len(spots)
    return pl.pallas_call(
        functools.partial(step_kernel, spots, factor, last),
        out_shape=outs,
        in_specs=[VMEM] * (4 + len(spots)),
        out_specs=(VMEM,) * len(outs),
        scratch_shapes=[pltpu.VMEM((rows, nodes), F32)] if last else [],
        compiler_params=pltpu.CompilerParams(vmem_limit_bytes=16 << 20),
        cost_estimate=pl.CostEstimate(flops=110_000_000, bytes_accessed=3_000_000, transcendentals=0),
        name="step",
    )(matrix, diagonal, rest, before, *received)


def finish_kernel(spots, rest_ref, *refs):
    received, out_ref = refs[:-1], refs[-1]
    out_ref[...] = rest_ref[...].astype(BF)
    for got, at in zip(received, spots):
        out_ref[:, at:at + LANE] = (rest_ref[:, at:at + LANE] + got[...].astype(F32)).astype(BF)


def finish(spots, rest, received):
    return pl.pallas_call(
        functools.partial(finish_kernel, spots),
        out_shape=jax.ShapeDtypeStruct(rest.shape, BF),
        in_specs=[VMEM] * (1 + len(spots)),
        out_specs=VMEM,
        compiler_params=pltpu.CompilerParams(vmem_limit_bytes=8 << 20),
        name="finish",
    )(rest, *received)


def owner_row(nodes, place_x, place_y):
    lane = iota((1, nodes), 1)
    hidden = ((lane < LANE) & (place_x > 0)) | ((lane >= 2 * LANE) & (lane < 3 * LANE) & (place_y > 0))
    return jnp.where(hidden, 0.0, 1.0)


def products_kernel(hops, own_ref, side_ref, mine_ref, other_ref, *refs):
    zs = len(hops) + 1
    columns = refs[:zs - 1]
    rot_ref, turn_ref, keep_ref, give_ref, fields, pair, coef = refs[zs - 1:]
    width, nodes = own_ref.shape
    at = lax.axis_index("band")
    z, x = at // 2, at % 2
    fields[:, 1 - x] = jnp.zeros((zs, width, nodes), BF)
    fields[z, x] = own_ref[...]
    for k, column in zip(hops, columns):
        fields[z ^ k, x] = column[...]
    coef[:width] = mine_ref[...]
    coef[width:] = other_ref[...]
    turned = mm(coef[...], fields[...].reshape(zs * 2 * width, nodes))
    rot_ref[...] = turned[:width]
    turn_ref[...] = turned[width:].astype(BF)
    owner = owner_row(nodes, lax.axis_index("dx"), lax.axis_index("dy"))
    pair[:width] = (own_ref[...].astype(F32) * owner).astype(BF)
    pair[width:] = (side_ref[...].astype(F32) * owner).astype(BF)
    p = lax.axis_index("dx") * 2 + lax.axis_index("dy")
    for j, ref in enumerate((keep_ref, keep_ref, give_ref, give_ref)):
        ref[j % 2] = mm_nt(fields[p ^ j, x], pair[...])


def products(hops, own, side, mine, other, columns):
    width, nodes = own.shape
    zs = len(hops) + 1
    f = lambda *s: jax.ShapeDtypeStruct(s, F32)
    outs = (f(width, nodes), jax.ShapeDtypeStruct((width, nodes), BF),
            f(2, width, 2 * width), f(2, width, 2 * width))
    return pl.pallas_call(
        functools.partial(products_kernel, hops),
        out_shape=outs,
        in_specs=[VMEM] * (4 + len(columns)),
        out_specs=(VMEM,) * 4,
        scratch_shapes=[
            pltpu.VMEM((zs, 2, width, nodes), BF),
            pltpu.VMEM((2 * width, nodes), BF),
            pltpu.VMEM((2 * width, zs * 2 * width), BF),
        ],
        compiler_params=pltpu.CompilerParams(vmem_limit_bytes=16 << 20),
        cost_estimate=pl.CostEstimate(flops=200_000_000, bytes_accessed=2_000_000, transcendentals=0),
        name="products",
    )(own, side, mine, other, *columns)


def finale_kernel(owned, mine_ref, got_ref, perm_ref, here_ref, below_ref, side_ref, corner_ref, margin_ref, rotated_ref):
    total = (mine_ref[...] + got_ref[...].astype(F32)).astype(BF)
    rotated_ref[...] = mm_nt(total, perm_ref[...]).astype(BF)
    width = here_ref.shape[0]
    x = lax.axis_index("band") % 2
    here = (here_ref[...] + below_ref[...]).T[:width] * (1.0 / owned)
    there = (side_ref[...] + corner_ref[...]).T[width:] * (1.0 / owned)
    margin_ref[:, :width] = jnp.where(x == 0, here, there)
    margin_ref[:, width:] = jnp.where(x == 0, there, here)


def finale(owned, mine, got, perm, parts):
    width = mine.shape[0]
    return pl.pallas_call(
        functools.partial(finale_kernel, owned),
        out_shape=(jax.ShapeDtypeStruct((width, 2 * width), F32), jax.ShapeDtypeStruct(mine.shape, BF)),
        in_specs=[VMEM] * (3 + len(parts)),
        out_specs=(VMEM,) * 2,
        compiler_params=pltpu.CompilerParams(vmem_limit_bytes=16 << 20),
        name="finale",
    )(mine, got, perm, *parts)


def swap(value, axis):
    return lax.ppermute(value, axis, [(0, 1), (1, 0)])


def from_behind(block, axis, distance):
    devices = range(lax.axis_size(axis))
    route = [(i - distance, i) for i in devices if i - distance in devices]
    return lax.ppermute(block, axis, route)


def on_device(waves, stiff, cell_scale, cell_pot, conn, counts, shared, rotation):
    width, nodes = waves.shape[0], waves.shape[3]
    cells, degree_nodes = conn.shape[2:]
    share = shared.shape[3]
    count_x, count_y = lax.axis_size("dx"), lax.axis_size("dy")
    bands = lax.axis_size("band")
    owned = nodes * count_x * count_y - share * (2 * count_x * count_y - count_x - count_y)
    paired = count_x == 2 and count_y == 2 and bands == 2 * count_x * count_y
    x = waves.reshape(width, nodes)
    spots = (0, 2 * LANE) if paired else (0, LANE, 2 * LANE, 3 * LANE)

    def exchange(sends):
        if paired:
            return swap(sends[0], "dx"), swap(sends[1], "dy")
        return (
            from_behind(sends[1], "dx", 1), from_behind(sends[0], "dx", -1),
            from_behind(sends[3], "dy", 1), from_behind(sends[2], "dy", -1),
        )

    matrix, diagonal, perm, before, rest, *sends = build(
        spots, paired, counts, cell_scale.reshape(1, cells),
        conn.reshape(cells, degree_nodes), cell_pot.reshape(cells, degree_nodes),
        shared.reshape(4, share), stiff, x,
    )
    for degree_step in range(DEGREE - 1):
        factor = 0.5 if degree_step == 0 else 1.0
        received = exchange(sends)
        if degree_step < DEGREE - 2:
            field, rest, *sends = step(spots, factor, False, matrix, diagonal, rest, before, received)
            before = field
        else:
            rest, *sends = step(spots, factor, True, matrix, diagonal, rest, before, received)
    filtered = finish(spots, rest, exchange(sends))

    if paired:
        across = [(i, i ^ 1) for i in range(bands)]
        other = lax.ppermute(rotation, "band", across)
        side = lax.ppermute(filtered, "band", across)
        zs = bands // 2
        hops = (2, 3, 1)
        columns = [
            lax.ppermute(filtered, "band", [(i, i ^ (2 * k)) for i in range(bands)])
            for k in hops
        ]
        mine, turn, keep, give = products(hops, filtered, side, rotation, other, columns)
        got = lax.ppermute(turn, "band", across)
        half = keep + swap(give, "dx")
        corner = [
            (2 * i + j, 2 * (i ^ 1) + (j ^ 1)) for i in range(bands) for j in range(count_y)
        ]
        parts = (
            half[0], swap(half[1], "dy"), lax.ppermute(half[0], "band", across),
            lax.ppermute(half[1], ("band", "dy"), corner),
        )
        margin, rotated = finale(owned, mine, got, perm, parts)
    else:
        gathered = lax.all_gather(filtered, "band", axis=0, tiled=True)
        owner = owner_row(nodes, lax.axis_index("dx"), lax.axis_index("dy")).astype(BF)
        block = mm_nt(filtered * owner, gathered)
        block = lax.psum_scatter(block, ("dx", "dy"), scatter_dimension=1, tiled=True)
        margin = block * (1.0 / owned)
        rotated = mm_nt(mm(rotation, gathered).astype(BF), perm).astype(BF)
    return margin, rotated.reshape(width, 1, 1, nodes)


def solution(mesh):
    return jax.shard_map(
        on_device,
        mesh=mesh,
        in_specs=(
            P("band", "dx", "dy", None),
            P(),
            P("dx", "dy", None),
            P("dx", "dy", None, None),
            P("dx", "dy", None, None),
            P("dx", "dy"),
            P("dx", "dy", None, None),
            P("band", None),
        ),
        out_specs=(P("band", ("dx", "dy")), P("band", "dx", "dy", None)),
        check_vma=False,
    )
```

```python
import functools

import jax
import jax.numpy as jnp
from jax import lax
from jax.experimental import pallas as pl
from jax.experimental.pallas import tpu as pltpu
from jax.sharding import PartitionSpec as P

DEGREE = 4
LANE = 128
SHIFT_CENTER = 3.0
HALF_WIDTH = 6.0
BF = jnp.bfloat16
F32 = jnp.float32
NT = (((1,), (1,)), ((), ()))
FACE = 4 * LANE
FX, FY = 0, 2 * LANE
SPLIT = 16

VMEM = pl.BlockSpec(memory_space=pltpu.VMEM)
HBM = pl.BlockSpec(memory_space=pltpu.HBM)


def iota(shape, dim):
    return lax.broadcasted_iota(jnp.int32, shape, dim)


def hot(mask):
    return mask.astype(F32).astype(BF)


def mm(a, b):
    return jnp.dot(a, b, preferred_element_type=F32)


def mm_nt(a, b):
    return lax.dot_general(a, b, NT, preferred_element_type=F32)


def apply_operator(field, matrix_ref, diagonal_ref):
    return mm(field.astype(BF), matrix_ref[...]) + field * diagonal_ref[0:1, :]


def build_kernel(
    spots, paired,
    counts_hbm, scale_hbm, conn_hbm, pot_hbm, shared_hbm, stiff_hbm, x_hbm,
    matrix_ref, diagonal_ref, perm_ref, y0_ref, rest_ref, *outs_and_scratch,
):
    count_out = 1 if paired else len(spots)
    sends = outs_and_scratch[:count_out]
    (count, scale, conn, pot, shared, stiff, x, tcat, vcat, off, table, links, sems) = outs_and_scratch[count_out:]
    copies = [
        pltpu.make_async_copy(src, dst, sems.at[i])
        for i, (src, dst) in enumerate(
            ((counts_hbm, count), (scale_hbm, scale), (shared_hbm, shared), (conn_hbm, conn),
             (pot_hbm, pot), (stiff_hbm, stiff), (x_hbm, x))
        )
    ]
    for copy in copies:
        copy.start()
    cells, degree_nodes = conn.shape
    nodes = x.shape[1]
    wide = off.shape[0]
    off[...] = jnp.zeros_like(off)
    table[...] = jnp.zeros_like(table)
    links[...] = jnp.full(links.shape, -1, jnp.int32)
    for copy in copies:
        copy.wait()
    matrix = stiff[...]
    eye = iota(matrix.shape, 0) == iota(matrix.shape, 1)
    off[:degree_nodes, :degree_nodes] = jnp.where(eye, jnp.zeros_like(matrix), matrix)
    table[cells:cells + 1, :degree_nodes] = jnp.sum(
        jnp.where(eye, matrix.astype(F32), 0.0), axis=0, keepdims=True
    )
    table[:cells, :degree_nodes] = pot[...]
    links[:cells, :degree_nodes] = conn[...]
    if paired:
        first_x = 1 - lax.axis_index("dx")
        first_y = 1 - lax.axis_index("dy")
        order = (first_x, 1 - first_x, 2 + first_y, 3 - first_y)
    else:
        order = (0, 1, 2, 3)
    node = iota((nodes, LANE), 0)
    lane = iota((nodes, LANE), 1)
    for i in range(4):
        perm_ref[:, i * LANE:(i + 1) * LANE] = hot(node == shared[pl.ds(order[i], 1), :])
    on_face = mm(perm_ref[:, :FACE], jnp.ones((FACE, LANE), BF))
    inner = (1.0 - on_face).astype(BF)
    below = hot(iota((LANE, LANE), 1) < iota((LANE, LANE), 0))
    ranks = []
    seen = jnp.zeros((1, LANE), F32)
    for j in range(nodes // LANE):
        part = inner[j * LANE:(j + 1) * LANE]
        ranks.append(mm(below, part) + seen)
        seen = seen + jnp.sum(part.astype(F32), axis=0, keepdims=True)
    rank = jnp.concatenate(ranks, axis=0)
    rank = jnp.where(on_face > 0.5, -1.0, rank).astype(jnp.int32)
    for j in range((nodes - FACE) // LANE):
        perm_ref[:, FACE + j * LANE:FACE + (j + 1) * LANE] = hot(rank == lane + j * LANE)
    spot = iota((8, nodes), 1)
    digits = jnp.where(iota((8, nodes), 0) == 0, spot >> 4, spot & 15).astype(F32).astype(BF)
    place = mm_nt(digits, perm_ref[...]).astype(BF)
    y0 = mm(x[...], perm_ref[...])
    wide_node = iota((nodes, wide), 0)
    tail = degree_nodes + (-degree_nodes) % 16
    row = iota((16, wide), 0)
    diagonal = jnp.zeros((1, nodes), F32)
    for c in range(cells):
        share = jnp.where(c < count[0, 0], 2.0 / HALF_WIDTH, 0.0)
        weight = share * scale[0, c]
        link = links[c:c + 1, :]
        found = mm(place, hot(wide_node == link))
        where = jnp.where(link < 0, -1.0, found[0:1] * 16.0 + found[1:2]).astype(jnp.int32)
        select = hot(wide_node == where)
        tcat[:, c * wide:(c + 1) * wide] = select
        value = weight * table[cells:cells + 1, :] + share * table[c:c + 1, :]
        high = value.astype(BF).astype(F32)
        middle = (value - high).astype(BF).astype(F32)
        low = value - high - middle
        off[tail:tail + 16, :] = jnp.where(
            row == 0, high, jnp.where(row == 1, middle, jnp.where(row == 2, low, 0.0))
        ).astype(BF)
        moved = mm_nt(off[...], select)
        diagonal = diagonal + jnp.sum(moved[tail:tail + 16], axis=0, keepdims=True)
        vcat[c * wide:(c + 1) * wide, :] = (moved * weight).astype(BF)
    diagonal_ref[...] = jnp.broadcast_to(diagonal, diagonal_ref.shape)
    matrix_ref[:FACE, :] = mm(tcat[:FACE, :], vcat[...]).astype(BF)
    matrix_ref[FACE:, FACE:] = mm(tcat[FACE:, :], vcat[:, FACE:]).astype(BF)
    matrix_ref[FACE:, :FACE] = matrix_ref[:FACE, FACE:].T
    y0_ref[...] = y0
    applied = apply_operator(y0, matrix_ref, diagonal_ref)
    if paired:
        rows = x.shape[0]
        rest_ref[...] = applied
        pack_faces(sends[0], applied)
        sends[0][2 * rows:, :] = matrix_ref[FY:FY + LANE, FX:FX + LANE]
    else:
        rest_ref[...] = 0.5 * (applied - y0)
        for send, at in zip(sends, spots):
            send[...] = applied[:, at:at + LANE].astype(BF)


def pack_faces(out_ref, applied):
    rows = applied.shape[0]
    out_ref[:rows, :] = applied[:, FX:FX + LANE].astype(BF)
    out_ref[rows:2 * rows, :] = applied[:, FY:FY + LANE].astype(BF)


def build(spots, paired, counts, scale, conn, pot, shared, stiff, x):
    cells, degree_nodes = conn.shape
    rows, nodes = x.shape
    wide = -(-(degree_nodes + 32) // LANE) * LANE
    f = lambda *s: jax.ShapeDtypeStruct(s, F32)
    b = lambda *s: jax.ShapeDtypeStruct(s, BF)
    outs = (b(nodes, nodes), f(8, nodes), b(nodes, nodes), f(rows, nodes), f(rows, nodes))
    outs += (b(2 * rows + LANE, LANE),) if paired else (b(rows, LANE),) * len(spots)
    return pl.pallas_call(
        functools.partial(build_kernel, spots, paired),
        out_shape=outs,
        in_specs=[HBM] * 7,
        out_specs=(VMEM,) * len(outs),
        scratch_shapes=[
            pltpu.SMEM(counts.shape, counts.dtype),
            pltpu.SMEM(scale.shape, F32),
            pltpu.VMEM(conn.shape, jnp.int32),
            pltpu.VMEM(pot.shape, F32),
            pltpu.VMEM(shared.shape, jnp.int32),
            pltpu.VMEM(stiff.shape, BF),
            pltpu.VMEM(x.shape, BF),
            pltpu.VMEM((nodes, cells * wide), BF),
            pltpu.VMEM((cells * wide, nodes), BF),
            pltpu.VMEM((wide, wide), BF),
            pltpu.VMEM((8, wide), F32),
            pltpu.VMEM((8, wide), jnp.int32),
            pltpu.SemaphoreType.DMA((7,)),
        ],
        compiler_params=pltpu.CompilerParams(vmem_limit_bytes=40 << 20),
        cost_estimate=pl.CostEstimate(flops=5_000_000_000, bytes_accessed=5_000_000, transcendentals=0),
        name="build",
    )(counts, *(pltpu.with_memory_space_constraint(v, pltpu.HBM) for v in (scale, conn, pot, shared, stiff, x)))


def step_kernel(spots, factor, last, matrix_ref, diagonal_ref, rest_ref, before_ref, *refs):
    count = len(spots)
    received = refs[:count]
    outs = refs[count:]
    field_ref, outs = (outs[-1], outs[:-1]) if last else (outs[0], outs[1:])
    field_ref[...] = rest_ref[...]
    for got, at in zip(received, spots):
        field_ref[:, at:at + LANE] += factor * got[...].astype(F32)
    field = field_ref[...]
    applied = apply_operator(field, matrix_ref, diagonal_ref)
    outs[0][...] = applied - field - before_ref[...]
    for send, at in zip(outs[1:], spots):
        send[...] = applied[:, at:at + LANE].astype(BF)


def step(spots, factor, last, matrix, diagonal, rest, before, received):
    rows, nodes = rest.shape
    field = jax.ShapeDtypeStruct((rows, nodes), F32)
    outs = (field,) * (1 if last else 2) + (jax.ShapeDtypeStruct((rows, LANE), BF),) * len(spots)
    return pl.pallas_call(
        functools.partial(step_kernel, spots, factor, last),
        out_shape=outs,
        in_specs=[VMEM] * (4 + len(spots)),
        out_specs=(VMEM,) * len(outs),
        scratch_shapes=[pltpu.VMEM((rows, nodes), F32)] if last else [],
        compiler_params=pltpu.CompilerParams(vmem_limit_bytes=16 << 20),
        cost_estimate=pl.CostEstimate(flops=110_000_000, bytes_accessed=3_000_000, transcendentals=0),
        name="step",
    )(matrix, diagonal, rest, before, *received)


def finish_kernel(spots, rest_ref, *refs):
    received, out_ref = refs[:-1], refs[-1]
    out_ref[...] = rest_ref[...].astype(BF)
    for got, at in zip(received, spots):
        out_ref[:, at:at + LANE] = (rest_ref[:, at:at + LANE] + got[...].astype(F32)).astype(BF)


def finish(spots, rest, received):
    return pl.pallas_call(
        functools.partial(finish_kernel, spots),
        out_shape=jax.ShapeDtypeStruct(rest.shape, BF),
        in_specs=[VMEM] * (1 + len(spots)),
        out_specs=VMEM,
        compiler_params=pltpu.CompilerParams(vmem_limit_bytes=8 << 20),
        name="finish",
    )(rest, *received)


def owner_row(nodes, place_x, place_y):
    lane = iota((1, nodes), 1)
    hidden = ((lane < LANE) & (place_x > 0)) | ((lane >= 2 * LANE) & (lane < 3 * LANE) & (place_y > 0))
    return jnp.where(hidden, 0.0, 1.0)


def products_kernel(hops, own_ref, side_ref, mine_ref, other_ref, *refs):
    zs = len(hops) + 1
    columns = refs[:zs - 1]
    rot_ref, turn_ref, keep_ref, give_ref, fields, pair, coef = refs[zs - 1:]
    width, nodes = own_ref.shape
    at = lax.axis_index("band")
    z, x = at // 2, at % 2
    fields[:, 1 - x] = jnp.zeros((zs, width, nodes), BF)
    fields[z, x] = own_ref[...]
    for k, column in zip(hops, columns):
        fields[z ^ k, x] = column[...]
    coef[:width] = mine_ref[...]
    coef[width:] = other_ref[...]
    turned = mm(coef[...], fields[...].reshape(zs * 2 * width, nodes))
    rot_ref[...] = turned[:width]
    turn_ref[...] = turned[width:].astype(BF)
    owner = owner_row(nodes, lax.axis_index("dx"), lax.axis_index("dy"))
    pair[:width] = (own_ref[...].astype(F32) * owner).astype(BF)
    pair[width:] = (side_ref[...].astype(F32) * owner).astype(BF)
    p = lax.axis_index("dx") * 2 + lax.axis_index("dy")
    for j, ref in enumerate((keep_ref, keep_ref, give_ref, give_ref)):
        ref[j % 2] = mm_nt(fields[p ^ j, x], pair[...])


def products(hops, own, side, mine, other, columns):
    width, nodes = own.shape
    zs = len(hops) + 1
    f = lambda *s: jax.ShapeDtypeStruct(s, F32)
    outs = (f(width, nodes), jax.ShapeDtypeStruct((width, nodes), BF),
            f(2, width, 2 * width), f(2, width, 2 * width))
    return pl.pallas_call(
        functools.partial(products_kernel, hops),
        out_shape=outs,
        in_specs=[VMEM] * (4 + len(columns)),
        out_specs=(VMEM,) * 4,
        scratch_shapes=[
            pltpu.VMEM((zs, 2, width, nodes), BF),
            pltpu.VMEM((2 * width, nodes), BF),
            pltpu.VMEM((2 * width, zs * 2 * width), BF),
        ],
        compiler_params=pltpu.CompilerParams(vmem_limit_bytes=16 << 20),
        cost_estimate=pl.CostEstimate(flops=200_000_000, bytes_accessed=2_000_000, transcendentals=0),
        name="products",
    )(own, side, mine, other, *columns)


def finale_kernel(owned, mine_ref, got_ref, perm_ref, here_ref, below_ref, side_ref, corner_ref, margin_ref, rotated_ref):
    total = (mine_ref[...] + got_ref[...].astype(F32)).astype(BF)
    rotated_ref[...] = mm_nt(total, perm_ref[...]).astype(BF)
    width = here_ref.shape[0]
    x = lax.axis_index("band") % 2
    here = (here_ref[...] + below_ref[...]).T[:width] * (1.0 / owned)
    there = (side_ref[...] + corner_ref[...]).T[width:] * (1.0 / owned)
    margin_ref[:, :width] = jnp.where(x == 0, here, there)
    margin_ref[:, width:] = jnp.where(x == 0, there, here)


def finale(owned, mine, got, perm, parts):
    width = mine.shape[0]
    return pl.pallas_call(
        functools.partial(finale_kernel, owned),
        out_shape=(jax.ShapeDtypeStruct((width, 2 * width), F32), jax.ShapeDtypeStruct(mine.shape, BF)),
        in_specs=[VMEM] * (3 + len(parts)),
        out_specs=(VMEM,) * 2,
        compiler_params=pltpu.CompilerParams(vmem_limit_bytes=16 << 20),
        name="finale",
    )(mine, got, perm, *parts)


def swap(value, axis):
    return lax.ppermute(value, axis, [(0, 1), (1, 0)])


def split3(value):
    high = value.astype(BF).astype(F32)
    middle = (value - high).astype(BF).astype(F32)
    return high, middle, value - high - middle


def advance_kernel(first, matrix_ref, diagonal_ref, applied_ref, field_ref, *refs):
    before_ref = None if first else refs[0]
    got_ref, next_ref, product_ref, to_x_ref, to_y_ref = refs[0 if first else 1:]
    rows = field_ref.shape[0]
    if first:
        next_ref[...] = 0.5 * (applied_ref[...] - field_ref[...])
        next_ref[:, FX:FX + LANE] += 0.5 * got_ref[:rows, :].astype(F32)
    else:
        next_ref[...] = applied_ref[...] - field_ref[...] - before_ref[...]
        next_ref[:, FX:FX + LANE] += got_ref[:rows, :].astype(F32)
    product = apply_operator(next_ref[...], matrix_ref, diagonal_ref)
    product_ref[...] = product
    to_x_ref[...] = product[:, FX:FX + LANE].astype(BF)
    to_y_ref[:rows, :] = applied_ref[:, FY:FY + LANE].astype(BF)
    to_y_ref[rows:2 * rows, :] = product[:, FY:FY + LANE].astype(BF)
    to_y_ref[2 * rows:3 * rows, :] = got_ref[rows:2 * rows, :]
    if first:
        to_y_ref[3 * rows:3 * rows + LANE, :] = matrix_ref[FY:FY + LANE, FY:FY + LANE]
        high, middle, low = split3(diagonal_ref[0:1, FY:FY + LANE])
        row = iota((SPLIT, LANE), 0)
        to_y_ref[3 * rows + LANE:, :] = jnp.where(
            row == 0, high, jnp.where(row == 1, middle, jnp.where(row == 2, low, 0.0))
        ).astype(BF)


def advance(matrix, diagonal, applied, field, before, got):
    first = before is None
    rows, nodes = field.shape
    f = jax.ShapeDtypeStruct((rows, nodes), F32)
    down = 3 * rows + (LANE + SPLIT if first else 0)
    args = (matrix, diagonal, applied, field) + (() if first else (before,)) + (got,)
    return pl.pallas_call(
        functools.partial(advance_kernel, first),
        out_shape=(f, f, jax.ShapeDtypeStruct((rows, LANE), BF), jax.ShapeDtypeStruct((down, LANE), BF)),
        in_specs=[VMEM] * len(args),
        out_specs=(VMEM,) * 4,
        compiler_params=pltpu.CompilerParams(vmem_limit_bytes=16 << 20),
        cost_estimate=pl.CostEstimate(flops=110_000_000, bytes_accessed=3_000_000, transcendentals=0),
        name="advance",
    )(*args)


def correct_kernel(
    first, matrix_ref, diagonal_ref, applied_ref, field_ref, next_ref, product_ref,
    from_x_ref, from_y_ref, block_x_ref, block_y_ref, *outs,
):
    rows = field_ref.shape[0]
    scale = 0.5 if first else 1.0
    total_ref = outs[-1]
    given = scale * from_y_ref[:rows, :].astype(F32)
    sent = scale * applied_ref[:, FY:FY + LANE].astype(BF).astype(F32)
    corner = scale * from_y_ref[2 * rows:3 * rows, :].astype(F32)
    tail = block_y_ref[3 * rows + LANE:3 * rows + LANE + 8, :].astype(F32)
    their_diagonal = tail[0:1] + tail[1:2] + tail[2:3]
    their_y = (
        from_y_ref[rows:2 * rows, :].astype(F32)
        + mm(sent.astype(BF), block_y_ref[3 * rows:3 * rows + LANE, :])
        + sent * their_diagonal
    )
    their_x = from_x_ref[...].astype(F32) + mm(corner.astype(BF), block_x_ref[2 * rows:2 * rows + LANE, :])
    total_ref[...] = (
        product_ref[...] + mm(given.astype(BF), matrix_ref[FY:FY + LANE, :])
        - next_ref[...] - field_ref[...]
    )
    total_ref[:, FX:FX + LANE] += their_x
    total_ref[:, FY:FY + LANE] += their_y + given * (diagonal_ref[0:1, FY:FY + LANE] - 1.0)
    if first:
        middle_ref, second_ref, again_ref, pack_ref = outs[:-1]
        middle_ref[...] = next_ref[...]
        middle_ref[:, FY:FY + LANE] += given
        second = total_ref[...]
        second_ref[...] = second
        applied = apply_operator(second, matrix_ref, diagonal_ref)
        again_ref[...] = applied
        pack_faces(pack_ref, applied)
    else:
        outs[0][...] = total_ref[...].astype(BF)


def correct(first, matrix, diagonal, applied, field, ahead, product, from_x, from_y, block_x, block_y):
    rows, nodes = field.shape
    f = jax.ShapeDtypeStruct((rows, nodes), F32)
    outs = (f, f, f, jax.ShapeDtypeStruct((2 * rows, LANE), BF)) if first else (jax.ShapeDtypeStruct((rows, nodes), BF),)
    return pl.pallas_call(
        functools.partial(correct_kernel, first),
        out_shape=outs,
        in_specs=[VMEM] * 10,
        out_specs=(VMEM,) * len(outs),
        scratch_shapes=[pltpu.VMEM((rows, nodes), F32)],
        compiler_params=pltpu.CompilerParams(vmem_limit_bytes=16 << 20),
        cost_estimate=pl.CostEstimate(flops=150_000_000, bytes_accessed=3_000_000, transcendentals=0),
        name="correct",
    )(matrix, diagonal, applied, field, ahead, product, from_x, from_y, block_x, block_y)


def filter_pairs(matrix, diagonal, field, applied, pack):
    block_x = got = swap(pack, "dx")
    ahead, product, to_x, to_y = advance(matrix, diagonal, applied, field, None, got)
    block_y = swap(to_y, "dy")
    field, second, applied, pack = correct(
        True, matrix, diagonal, applied, field, ahead, product, swap(to_x, "dx"), block_y, block_x, block_y
    )
    got = swap(pack, "dx")
    ahead, product, to_x, to_y = advance(matrix, diagonal, applied, second, field, got)
    return correct(
        False, matrix, diagonal, applied, second, ahead, product, swap(to_x, "dx"), swap(to_y, "dy"), block_x, block_y
    )[0]


def from_behind(block, axis, distance):
    devices = range(lax.axis_size(axis))
    route = [(i - distance, i) for i in devices if i - distance in devices]
    return lax.ppermute(block, axis, route)


def on_device(waves, stiff, cell_scale, cell_pot, conn, counts, shared, rotation):
    width, nodes = waves.shape[0], waves.shape[3]
    cells, degree_nodes = conn.shape[2:]
    share = shared.shape[3]
    count_x, count_y = lax.axis_size("dx"), lax.axis_size("dy")
    bands = lax.axis_size("band")
    owned = nodes * count_x * count_y - share * (2 * count_x * count_y - count_x - count_y)
    paired = count_x == 2 and count_y == 2 and bands == 2 * count_x * count_y
    x = waves.reshape(width, nodes)
    spots = (0, LANE, 2 * LANE, 3 * LANE)

    def exchange(sends):
        return (
            from_behind(sends[1], "dx", 1), from_behind(sends[0], "dx", -1),
            from_behind(sends[3], "dy", 1), from_behind(sends[2], "dy", -1),
        )

    matrix, diagonal, perm, before, rest, *sends = build(
        spots, paired, counts, cell_scale.reshape(1, cells),
        conn.reshape(cells, degree_nodes), cell_pot.reshape(cells, degree_nodes),
        shared.reshape(4, share), stiff, x,
    )
    if paired:
        filtered = filter_pairs(matrix, diagonal, before, rest, sends[0])
    else:
        for degree_step in range(DEGREE - 1):
            factor = 0.5 if degree_step == 0 else 1.0
            received = exchange(sends)
            if degree_step < DEGREE - 2:
                field, rest, *sends = step(spots, factor, False, matrix, diagonal, rest, before, received)
                before = field
            else:
                rest, *sends = step(spots, factor, True, matrix, diagonal, rest, before, received)
        filtered = finish(spots, rest, exchange(sends))

    if paired:
        across = [(i, i ^ 1) for i in range(bands)]
        other = lax.ppermute(rotation, "band", across)
        side = lax.ppermute(filtered, "band", across)
        zs = bands // 2
        hops = (2, 3, 1)
        columns = [
            lax.ppermute(filtered, "band", [(i, i ^ (2 * k)) for i in range(bands)])
            for k in hops
        ]
        mine, turn, keep, give = products(hops, filtered, side, rotation, other, columns)
        got = lax.ppermute(turn, "band", across)
        half = keep + swap(give, "dx")
        corner = [
            (2 * i + j, 2 * (i ^ 1) + (j ^ 1)) for i in range(bands) for j in range(count_y)
        ]
        parts = (
            half[0], swap(half[1], "dy"), lax.ppermute(half[0], "band", across),
            lax.ppermute(half[1], ("band", "dy"), corner),
        )
        margin, rotated = finale(owned, mine, got, perm, parts)
    else:
        gathered = lax.all_gather(filtered, "band", axis=0, tiled=True)
        owner = owner_row(nodes, lax.axis_index("dx"), lax.axis_index("dy")).astype(BF)
        block = mm_nt(filtered * owner, gathered)
        block = lax.psum_scatter(block, ("dx", "dy"), scatter_dimension=1, tiled=True)
        margin = block * (1.0 / owned)
        rotated = mm_nt(mm(rotation, gathered).astype(BF), perm).astype(BF)
    return margin, rotated.reshape(width, 1, 1, nodes)


def solution(mesh):
    return jax.shard_map(
        on_device,
        mesh=mesh,
        in_specs=(
            P("band", "dx", "dy", None),
            P(),
            P("dx", "dy", None),
            P("dx", "dy", None, None),
            P("dx", "dy", None, None),
            P("dx", "dy"),
            P("dx", "dy", None, None),
            P("band", None),
        ),
        out_specs=(P("band", ("dx", "dy")), P("band", "dx", "dy", None)),
        check_vma=False,
    )
```

```python
import functools

import jax
import jax.numpy as jnp
from jax import lax
from jax.experimental import pallas as pl
from jax.experimental.pallas import tpu as pltpu
from jax.sharding import PartitionSpec as P

DEGREE = 4
LANE = 128
SHIFT_CENTER = 3.0
HALF_WIDTH = 6.0
BF = jnp.bfloat16
F32 = jnp.float32
NT = (((1,), (1,)), ((), ()))
FACE = 4 * LANE
FX, FY = 0, 2 * LANE
SPLIT = 16

VMEM = pl.BlockSpec(memory_space=pltpu.VMEM)
HBM = pl.BlockSpec(memory_space=pltpu.HBM)


def iota(shape, dim):
    return lax.broadcasted_iota(jnp.int32, shape, dim)


def hot(mask):
    return mask.astype(F32).astype(BF)


def mm(a, b):
    return jnp.dot(a, b, preferred_element_type=F32)


def mm_nt(a, b):
    return lax.dot_general(a, b, NT, preferred_element_type=F32)


def apply_operator(field, matrix_ref, diagonal_ref):
    return mm(field.astype(BF), matrix_ref[...]) + field * diagonal_ref[0:1, :]


def build_kernel(
    spots, paired,
    counts_hbm, scale_hbm, conn_hbm, pot_hbm, shared_hbm, stiff_hbm, x_hbm,
    matrix_ref, diagonal_ref, perm_ref, y0_ref, rest_ref, *outs_and_scratch,
):
    count_out = 1 if paired else len(spots)
    sends = outs_and_scratch[:count_out]
    (count, scale, conn, pot, shared, stiff, x, tcat, vcat, off, table, links, sems) = outs_and_scratch[count_out:]
    copies = [
        pltpu.make_async_copy(src, dst, sems.at[i])
        for i, (src, dst) in enumerate(
            ((counts_hbm, count), (scale_hbm, scale), (shared_hbm, shared), (conn_hbm, conn),
             (pot_hbm, pot), (stiff_hbm, stiff), (x_hbm, x))
        )
    ]
    for copy in copies:
        copy.start()
    cells, degree_nodes = conn.shape
    nodes = x.shape[1]
    wide = off.shape[0]
    off[...] = jnp.zeros_like(off)
    table[...] = jnp.zeros_like(table)
    links[...] = jnp.full(links.shape, -1, jnp.int32)
    for copy in copies:
        copy.wait()
    matrix = stiff[...]
    eye = iota(matrix.shape, 0) == iota(matrix.shape, 1)
    off[:degree_nodes, :degree_nodes] = jnp.where(eye, jnp.zeros_like(matrix), matrix)
    table[cells:cells + 1, :degree_nodes] = jnp.sum(
        jnp.where(eye, matrix.astype(F32), 0.0), axis=0, keepdims=True
    )
    table[:cells, :degree_nodes] = pot[...]
    links[:cells, :degree_nodes] = conn[...]
    if paired:
        first_x = 1 - lax.axis_index("dx")
        first_y = 1 - lax.axis_index("dy")
        order = (first_x, 1 - first_x, 2 + first_y, 3 - first_y)
    else:
        order = (0, 1, 2, 3)
    node = iota((nodes, LANE), 0)
    lane = iota((nodes, LANE), 1)
    for i in range(4):
        perm_ref[:, i * LANE:(i + 1) * LANE] = hot(node == shared[pl.ds(order[i], 1), :])
    on_face = mm(perm_ref[:, :FACE], jnp.ones((FACE, LANE), BF))
    inner = (1.0 - on_face).astype(BF)
    below = hot(iota((LANE, LANE), 1) < iota((LANE, LANE), 0))
    ranks = []
    seen = jnp.zeros((1, LANE), F32)
    for j in range(nodes // LANE):
        part = inner[j * LANE:(j + 1) * LANE]
        ranks.append(mm(below, part) + seen)
        seen = seen + jnp.sum(part.astype(F32), axis=0, keepdims=True)
    rank = jnp.concatenate(ranks, axis=0)
    rank = jnp.where(on_face > 0.5, -1.0, rank).astype(jnp.int32)
    for j in range((nodes - FACE) // LANE):
        perm_ref[:, FACE + j * LANE:FACE + (j + 1) * LANE] = hot(rank == lane + j * LANE)
    spot = iota((8, nodes), 1)
    digits = jnp.where(iota((8, nodes), 0) == 0, spot >> 4, spot & 15).astype(F32).astype(BF)
    place = mm_nt(digits, perm_ref[...]).astype(BF)
    y0 = mm(x[...], perm_ref[...])
    wide_node = iota((nodes, wide), 0)
    tail = degree_nodes + (-degree_nodes) % 16
    row = iota((16, wide), 0)
    diagonal = jnp.zeros((1, nodes), F32)
    for c in range(cells):
        share = jnp.where(c < count[0, 0], 2.0 / HALF_WIDTH, 0.0)
        weight = share * scale[0, c]
        link = links[c:c + 1, :]
        found = mm(place, hot(wide_node == link))
        where = jnp.where(link < 0, -1.0, found[0:1] * 16.0 + found[1:2]).astype(jnp.int32)
        select = hot(wide_node == where)
        tcat[:, c * wide:(c + 1) * wide] = select
        value = weight * table[cells:cells + 1, :] + share * table[c:c + 1, :]
        high = value.astype(BF).astype(F32)
        middle = (value - high).astype(BF).astype(F32)
        low = value - high - middle
        off[tail:tail + 16, :] = jnp.where(
            row == 0, high, jnp.where(row == 1, middle, jnp.where(row == 2, low, 0.0))
        ).astype(BF)
        moved = mm_nt(off[...], select)
        diagonal = diagonal + jnp.sum(moved[tail:tail + 16], axis=0, keepdims=True)
        vcat[c * wide:(c + 1) * wide, :] = (moved * weight).astype(BF)
    diagonal_ref[...] = jnp.broadcast_to(diagonal, diagonal_ref.shape)
    matrix_ref[:FACE, :] = mm(tcat[:FACE, :], vcat[...]).astype(BF)
    matrix_ref[FACE:, FACE:] = mm(tcat[FACE:, :], vcat[:, FACE:]).astype(BF)
    matrix_ref[FACE:, :FACE] = matrix_ref[:FACE, FACE:].T
    y0_ref[...] = y0
    applied = apply_operator(y0, matrix_ref, diagonal_ref)
    if paired:
        rows = x.shape[0]
        rest_ref[...] = applied
        pack_faces(sends[0], applied)
        sends[0][2 * rows:, :] = matrix_ref[FY:FY + LANE, FX:FX + LANE]
    else:
        rest_ref[...] = 0.5 * (applied - y0)
        for send, at in zip(sends, spots):
            send[...] = applied[:, at:at + LANE].astype(BF)


def pack_faces(out_ref, applied):
    rows = applied.shape[0]
    out_ref[:rows, :] = applied[:, FX:FX + LANE].astype(BF)
    out_ref[rows:2 * rows, :] = applied[:, FY:FY + LANE].astype(BF)


def build(spots, paired, counts, scale, conn, pot, shared, stiff, x):
    cells, degree_nodes = conn.shape
    rows, nodes = x.shape
    wide = -(-(degree_nodes + 32) // LANE) * LANE
    f = lambda *s: jax.ShapeDtypeStruct(s, F32)
    b = lambda *s: jax.ShapeDtypeStruct(s, BF)
    outs = (b(nodes, nodes), f(8, nodes), b(nodes, nodes), f(rows, nodes), f(rows, nodes))
    outs += (b(2 * rows + LANE, LANE),) if paired else (b(rows, LANE),) * len(spots)
    return pl.pallas_call(
        functools.partial(build_kernel, spots, paired),
        out_shape=outs,
        in_specs=[HBM] * 7,
        out_specs=(VMEM,) * len(outs),
        scratch_shapes=[
            pltpu.SMEM(counts.shape, counts.dtype),
            pltpu.SMEM(scale.shape, F32),
            pltpu.VMEM(conn.shape, jnp.int32),
            pltpu.VMEM(pot.shape, F32),
            pltpu.VMEM(shared.shape, jnp.int32),
            pltpu.VMEM(stiff.shape, BF),
            pltpu.VMEM(x.shape, BF),
            pltpu.VMEM((nodes, cells * wide), BF),
            pltpu.VMEM((cells * wide, nodes), BF),
            pltpu.VMEM((wide, wide), BF),
            pltpu.VMEM((8, wide), F32),
            pltpu.VMEM((8, wide), jnp.int32),
            pltpu.SemaphoreType.DMA((7,)),
        ],
        compiler_params=pltpu.CompilerParams(vmem_limit_bytes=40 << 20),
        cost_estimate=pl.CostEstimate(flops=5_000_000_000, bytes_accessed=5_000_000, transcendentals=0),
        name="build",
    )(counts, *(pltpu.with_memory_space_constraint(v, pltpu.HBM) for v in (scale, conn, pot, shared, stiff, x)))


def step_kernel(spots, factor, last, matrix_ref, diagonal_ref, rest_ref, before_ref, *refs):
    count = len(spots)
    received = refs[:count]
    outs = refs[count:]
    field_ref, outs = (outs[-1], outs[:-1]) if last else (outs[0], outs[1:])
    field_ref[...] = rest_ref[...]
    for got, at in zip(received, spots):
        field_ref[:, at:at + LANE] += factor * got[...].astype(F32)
    field = field_ref[...]
    applied = apply_operator(field, matrix_ref, diagonal_ref)
    outs[0][...] = applied - field - before_ref[...]
    for send, at in zip(outs[1:], spots):
        send[...] = applied[:, at:at + LANE].astype(BF)


def step(spots, factor, last, matrix, diagonal, rest, before, received):
    rows, nodes = rest.shape
    field = jax.ShapeDtypeStruct((rows, nodes), F32)
    outs = (field,) * (1 if last else 2) + (jax.ShapeDtypeStruct((rows, LANE), BF),) * len(spots)
    return pl.pallas_call(
        functools.partial(step_kernel, spots, factor, last),
        out_shape=outs,
        in_specs=[VMEM] * (4 + len(spots)),
        out_specs=(VMEM,) * len(outs),
        scratch_shapes=[pltpu.VMEM((rows, nodes), F32)] if last else [],
        compiler_params=pltpu.CompilerParams(vmem_limit_bytes=16 << 20),
        cost_estimate=pl.CostEstimate(flops=110_000_000, bytes_accessed=3_000_000, transcendentals=0),
        name="step",
    )(matrix, diagonal, rest, before, *received)


def finish_kernel(spots, rest_ref, *refs):
    received, out_ref = refs[:-1], refs[-1]
    out_ref[...] = rest_ref[...].astype(BF)
    for got, at in zip(received, spots):
        out_ref[:, at:at + LANE] = (rest_ref[:, at:at + LANE] + got[...].astype(F32)).astype(BF)


def finish(spots, rest, received):
    return pl.pallas_call(
        functools.partial(finish_kernel, spots),
        out_shape=jax.ShapeDtypeStruct(rest.shape, BF),
        in_specs=[VMEM] * (1 + len(spots)),
        out_specs=VMEM,
        compiler_params=pltpu.CompilerParams(vmem_limit_bytes=8 << 20),
        name="finish",
    )(rest, *received)


def owner_row(nodes, place_x, place_y):
    lane = iota((1, nodes), 1)
    hidden = ((lane < LANE) & (place_x > 0)) | ((lane >= 2 * LANE) & (lane < 3 * LANE) & (place_y > 0))
    return jnp.where(hidden, 0.0, 1.0)


def products_kernel(hops, own_ref, side_ref, mine_ref, other_ref, *refs):
    zs = len(hops) + 1
    columns = refs[:zs - 1]
    rot_ref, turn_ref, keep_ref, give_ref, fields, pair, coef = refs[zs - 1:]
    width, nodes = own_ref.shape
    at = lax.axis_index("band")
    z, x = at // 2, at % 2
    fields[:, 1 - x] = jnp.zeros((zs, width, nodes), BF)
    fields[z, x] = own_ref[...]
    for k, column in zip(hops, columns):
        fields[z ^ k, x] = column[...]
    coef[:width] = mine_ref[...]
    coef[width:] = other_ref[...]
    turned = mm(coef[...], fields[...].reshape(zs * 2 * width, nodes))
    rot_ref[...] = turned[:width]
    turn_ref[...] = turned[width:].astype(BF)
    owner = owner_row(nodes, lax.axis_index("dx"), lax.axis_index("dy"))
    pair[:width] = (own_ref[...].astype(F32) * owner).astype(BF)
    pair[width:] = (side_ref[...].astype(F32) * owner).astype(BF)
    p = lax.axis_index("dx") * 2 + lax.axis_index("dy")
    for j, ref in enumerate((keep_ref, keep_ref, give_ref, give_ref)):
        ref[j % 2] = mm_nt(fields[p ^ j, x], pair[...])


def products(hops, own, side, mine, other, columns):
    width, nodes = own.shape
    zs = len(hops) + 1
    f = lambda *s: jax.ShapeDtypeStruct(s, F32)
    outs = (f(width, nodes), jax.ShapeDtypeStruct((width, nodes), BF),
            f(2, width, 2 * width), f(2, width, 2 * width))
    return pl.pallas_call(
        functools.partial(products_kernel, hops),
        out_shape=outs,
        in_specs=[VMEM] * (4 + len(columns)),
        out_specs=(VMEM,) * 4,
        scratch_shapes=[
            pltpu.VMEM((zs, 2, width, nodes), BF),
            pltpu.VMEM((2 * width, nodes), BF),
            pltpu.VMEM((2 * width, zs * 2 * width), BF),
        ],
        compiler_params=pltpu.CompilerParams(vmem_limit_bytes=16 << 20),
        cost_estimate=pl.CostEstimate(flops=200_000_000, bytes_accessed=2_000_000, transcendentals=0),
        name="products",
    )(own, side, mine, other, *columns)


def finale_kernel(owned, mine_ref, got_ref, perm_ref, here_ref, below_ref, side_ref, corner_ref, margin_ref, rotated_ref):
    total = (mine_ref[...] + got_ref[...].astype(F32)).astype(BF)
    rotated_ref[...] = mm_nt(total, perm_ref[...]).astype(BF)
    width = here_ref.shape[0]
    x = lax.axis_index("band") % 2
    here = (here_ref[...] + below_ref[...]).T[:width] * (1.0 / owned)
    there = (side_ref[...] + corner_ref[...]).T[width:] * (1.0 / owned)
    margin_ref[:, :width] = jnp.where(x == 0, here, there)
    margin_ref[:, width:] = jnp.where(x == 0, there, here)


def finale(owned, mine, got, perm, parts):
    width = mine.shape[0]
    return pl.pallas_call(
        functools.partial(finale_kernel, owned),
        out_shape=(jax.ShapeDtypeStruct((width, 2 * width), F32), jax.ShapeDtypeStruct(mine.shape, BF)),
        in_specs=[VMEM] * (3 + len(parts)),
        out_specs=(VMEM,) * 2,
        compiler_params=pltpu.CompilerParams(vmem_limit_bytes=16 << 20),
        name="finale",
    )(mine, got, perm, *parts)


def swap(value, axis):
    return lax.ppermute(value, axis, [(0, 1), (1, 0)])


def split3(value):
    high = value.astype(BF).astype(F32)
    middle = (value - high).astype(BF).astype(F32)
    return high, middle, value - high - middle


def advance_kernel(first, matrix_ref, diagonal_ref, applied_ref, field_ref, *refs):
    before_ref = None if first else refs[0]
    got_ref, next_ref, product_ref, to_x_ref, to_y_ref = refs[0 if first else 1:]
    rows = field_ref.shape[0]
    if first:
        next_ref[...] = 0.5 * (applied_ref[...] - field_ref[...])
        next_ref[:, FX:FX + LANE] += 0.5 * got_ref[:rows, :].astype(F32)
    else:
        next_ref[...] = applied_ref[...] - field_ref[...] - before_ref[...]
        next_ref[:, FX:FX + LANE] += got_ref[:rows, :].astype(F32)
    product = apply_operator(next_ref[...], matrix_ref, diagonal_ref)
    product_ref[...] = product
    to_x_ref[...] = product[:, FX:FX + LANE].astype(BF)
    to_y_ref[:rows, :] = applied_ref[:, FY:FY + LANE].astype(BF)
    to_y_ref[rows:2 * rows, :] = product[:, FY:FY + LANE].astype(BF)
    to_y_ref[2 * rows:3 * rows, :] = got_ref[rows:2 * rows, :]
    if first:
        to_y_ref[3 * rows:3 * rows + LANE, :] = matrix_ref[FY:FY + LANE, FY:FY + LANE]
        high, middle, low = split3(diagonal_ref[0:1, FY:FY + LANE])
        row = iota((SPLIT, LANE), 0)
        to_y_ref[3 * rows + LANE:, :] = jnp.where(
            row == 0, high, jnp.where(row == 1, middle, jnp.where(row == 2, low, 0.0))
        ).astype(BF)


def advance(matrix, diagonal, applied, field, before, got):
    first = before is None
    rows, nodes = field.shape
    f = jax.ShapeDtypeStruct((rows, nodes), F32)
    down = 3 * rows + (LANE + SPLIT if first else 0)
    args = (matrix, diagonal, applied, field) + (() if first else (before,)) + (got,)
    return pl.pallas_call(
        functools.partial(advance_kernel, first),
        out_shape=(f, f, jax.ShapeDtypeStruct((rows, LANE), BF), jax.ShapeDtypeStruct((down, LANE), BF)),
        in_specs=[VMEM] * len(args),
        out_specs=(VMEM,) * 4,
        compiler_params=pltpu.CompilerParams(vmem_limit_bytes=16 << 20),
        cost_estimate=pl.CostEstimate(flops=110_000_000, bytes_accessed=3_000_000, transcendentals=0),
        name="advance",
    )(*args)


def correct_kernel(
    first, matrix_ref, diagonal_ref, applied_ref, field_ref, next_ref, product_ref,
    from_x_ref, from_y_ref, block_x_ref, block_y_ref, *outs,
):
    rows = field_ref.shape[0]
    scale = 0.5 if first else 1.0
    total_ref = outs[-1]
    given = scale * from_y_ref[:rows, :].astype(F32)
    sent = scale * applied_ref[:, FY:FY + LANE].astype(BF).astype(F32)
    corner = scale * from_y_ref[2 * rows:3 * rows, :].astype(F32)
    tail = block_y_ref[3 * rows + LANE:3 * rows + LANE + 8, :].astype(F32)
    their_diagonal = tail[0:1] + tail[1:2] + tail[2:3]
    their_y = (
        from_y_ref[rows:2 * rows, :].astype(F32)
        + mm(sent.astype(BF), block_y_ref[3 * rows:3 * rows + LANE, :])
        + sent * their_diagonal
    )
    their_x = from_x_ref[...].astype(F32) + mm(corner.astype(BF), block_x_ref[2 * rows:2 * rows + LANE, :])
    total_ref[...] = (
        product_ref[...] + mm(given.astype(BF), matrix_ref[FY:FY + LANE, :])
        - next_ref[...] - field_ref[...]
    )
    total_ref[:, FX:FX + LANE] += their_x
    total_ref[:, FY:FY + LANE] += their_y + given * (diagonal_ref[0:1, FY:FY + LANE] - 1.0)
    if first:
        middle_ref, second_ref, again_ref, pack_ref = outs[:-1]
        middle_ref[...] = next_ref[...]
        middle_ref[:, FY:FY + LANE] += given
        second = total_ref[...]
        second_ref[...] = second
        applied = apply_operator(second, matrix_ref, diagonal_ref)
        again_ref[...] = applied
        pack_faces(pack_ref, applied)
    else:
        outs[0][...] = total_ref[...].astype(BF)


def correct(first, matrix, diagonal, applied, field, ahead, product, from_x, from_y, block_x, block_y):
    rows, nodes = field.shape
    f = jax.ShapeDtypeStruct((rows, nodes), F32)
    outs = (f, f, f, jax.ShapeDtypeStruct((2 * rows, LANE), BF)) if first else (jax.ShapeDtypeStruct((rows, nodes), BF),)
    return pl.pallas_call(
        functools.partial(correct_kernel, first),
        out_shape=outs,
        in_specs=[VMEM] * 10,
        out_specs=(VMEM,) * len(outs),
        scratch_shapes=[pltpu.VMEM((rows, nodes), F32)],
        compiler_params=pltpu.CompilerParams(vmem_limit_bytes=16 << 20),
        cost_estimate=pl.CostEstimate(flops=150_000_000, bytes_accessed=3_000_000, transcendentals=0),
        name="correct",
    )(matrix, diagonal, applied, field, ahead, product, from_x, from_y, block_x, block_y)


def filter_pairs(matrix, diagonal, field, applied, pack):
    block_x = got = swap(pack, "dx")
    ahead, product, to_x, to_y = advance(matrix, diagonal, applied, field, None, got)
    block_y = swap(to_y, "dy")
    field, second, applied, pack = correct(
        True, matrix, diagonal, applied, field, ahead, product, swap(to_x, "dx"), block_y, block_x, block_y
    )
    got = swap(pack, "dx")
    ahead, product, to_x, to_y = advance(matrix, diagonal, applied, second, field, got)
    return correct(
        False, matrix, diagonal, applied, second, ahead, product, swap(to_x, "dx"), swap(to_y, "dy"), block_x, block_y
    )[0]


def from_behind(block, axis, distance):
    devices = range(lax.axis_size(axis))
    route = [(i - distance, i) for i in devices if i - distance in devices]
    return lax.ppermute(block, axis, route)


def on_device(waves, stiff, cell_scale, cell_pot, conn, counts, shared, rotation):
    width, nodes = waves.shape[0], waves.shape[3]
    cells, degree_nodes = conn.shape[2:]
    share = shared.shape[3]
    count_x, count_y = lax.axis_size("dx"), lax.axis_size("dy")
    bands = lax.axis_size("band")
    owned = nodes * count_x * count_y - share * (2 * count_x * count_y - count_x - count_y)
    paired = count_x == 2 and count_y == 2 and bands == 2 * count_x * count_y
    x = waves.reshape(width, nodes)
    spots = (0, LANE, 2 * LANE, 3 * LANE)

    def exchange(sends):
        return (
            from_behind(sends[1], "dx", 1), from_behind(sends[0], "dx", -1),
            from_behind(sends[3], "dy", 1), from_behind(sends[2], "dy", -1),
        )

    matrix, diagonal, perm, before, rest, *sends = build(
        spots, paired, counts, cell_scale.reshape(1, cells),
        conn.reshape(cells, degree_nodes), cell_pot.reshape(cells, degree_nodes),
        shared.reshape(4, share), stiff, x,
    )
    if paired:
        filtered = filter_pairs(matrix, diagonal, before, rest, sends[0])
    else:
        for degree_step in range(DEGREE - 1):
            factor = 0.5 if degree_step == 0 else 1.0
            received = exchange(sends)
            if degree_step < DEGREE - 2:
                field, rest, *sends = step(spots, factor, False, matrix, diagonal, rest, before, received)
                before = field
            else:
                rest, *sends = step(spots, factor, True, matrix, diagonal, rest, before, received)
        filtered = finish(spots, rest, exchange(sends))

    if paired:
        across = [(i, i ^ 1) for i in range(bands)]
        other = lax.ppermute(rotation, "band", across)
        hops = (3, 1, 2)
        routes = [[(i, i ^ (2 * k)) for i in range(bands)] for k in hops]
        columns = [lax.ppermute(filtered, "band", route) for route in routes[:2]]
        side = lax.ppermute(filtered, "band", across)
        columns.append(lax.ppermute(filtered, "band", routes[2]))
        mine, turn, keep, give = products(hops, filtered, side, rotation, other, columns)
        got = lax.ppermute(turn, "band", across)
        half = keep + swap(give, "dx")
        corner = [
            (2 * i + j, 2 * (i ^ 1) + (j ^ 1)) for i in range(bands) for j in range(count_y)
        ]
        parts = (
            half[0], swap(half[1], "dy"), lax.ppermute(half[0], "band", across),
            lax.ppermute(half[1], ("band", "dy"), corner),
        )
        margin, rotated = finale(owned, mine, got, perm, parts)
    else:
        gathered = lax.all_gather(filtered, "band", axis=0, tiled=True)
        owner = owner_row(nodes, lax.axis_index("dx"), lax.axis_index("dy")).astype(BF)
        block = mm_nt(filtered * owner, gathered)
        block = lax.psum_scatter(block, ("dx", "dy"), scatter_dimension=1, tiled=True)
        margin = block * (1.0 / owned)
        rotated = mm_nt(mm(rotation, gathered).astype(BF), perm).astype(BF)
    return margin, rotated.reshape(width, 1, 1, nodes)


def solution(mesh):
    return jax.shard_map(
        on_device,
        mesh=mesh,
        in_specs=(
            P("band", "dx", "dy", None),
            P(),
            P("dx", "dy", None),
            P("dx", "dy", None, None),
            P("dx", "dy", None, None),
            P("dx", "dy"),
            P("dx", "dy", None, None),
            P("band", None),
        ),
        out_specs=(P("band", ("dx", "dy")), P("band", "dx", "dy", None)),
        check_vma=False,
    )
```

```python
import functools

import jax
import jax.numpy as jnp
from jax import lax
from jax.experimental import pallas as pl
from jax.experimental.pallas import tpu as pltpu
from jax.sharding import PartitionSpec as P

DEGREE = 4
LANE = 128
SHIFT_CENTER = 3.0
HALF_WIDTH = 6.0
BF = jnp.bfloat16
F32 = jnp.float32
NT = (((1,), (1,)), ((), ()))
FACE = 4 * LANE
FX, FY = 0, 2 * LANE
SPLIT = 16

VMEM = pl.BlockSpec(memory_space=pltpu.VMEM)
HBM = pl.BlockSpec(memory_space=pltpu.HBM)


def iota(shape, dim):
    return lax.broadcasted_iota(jnp.int32, shape, dim)


def hot(mask):
    return mask.astype(F32).astype(BF)


def mm(a, b):
    return jnp.dot(a, b, preferred_element_type=F32)


def mm_nt(a, b):
    return lax.dot_general(a, b, NT, preferred_element_type=F32)


def apply_operator(field, matrix_ref, diagonal_ref):
    return mm(field.astype(BF), matrix_ref[...]) + field * diagonal_ref[0:1, :]


def build_kernel(
    spots, paired,
    counts_hbm, scale_hbm, conn_hbm, pot_hbm, shared_hbm, stiff_hbm, x_hbm,
    matrix_ref, diagonal_ref, perm_ref, y0_ref, rest_ref, *outs_and_scratch,
):
    count_out = 1 if paired else len(spots)
    sends = outs_and_scratch[:count_out]
    (count, scale, conn, pot, shared, stiff, x, tcat, vcat, off, table, links, sems) = outs_and_scratch[count_out:]
    copies = [
        pltpu.make_async_copy(src, dst, sems.at[i])
        for i, (src, dst) in enumerate(
            ((counts_hbm, count), (scale_hbm, scale), (shared_hbm, shared), (conn_hbm, conn),
             (pot_hbm, pot), (stiff_hbm, stiff), (x_hbm, x))
        )
    ]
    for copy in copies:
        copy.start()
    cells, degree_nodes = conn.shape
    nodes = x.shape[1]
    wide = off.shape[0]
    off[...] = jnp.zeros_like(off)
    table[...] = jnp.zeros_like(table)
    links[...] = jnp.full(links.shape, -1, jnp.int32)
    for copy in copies:
        copy.wait()
    matrix = stiff[...]
    eye = iota(matrix.shape, 0) == iota(matrix.shape, 1)
    off[:degree_nodes, :degree_nodes] = jnp.where(eye, jnp.zeros_like(matrix), matrix)
    table[cells:cells + 1, :degree_nodes] = jnp.sum(
        jnp.where(eye, matrix.astype(F32), 0.0), axis=0, keepdims=True
    )
    table[:cells, :degree_nodes] = pot[...]
    links[:cells, :degree_nodes] = conn[...]
    if paired:
        first_x = 1 - lax.axis_index("dx")
        first_y = 1 - lax.axis_index("dy")
        order = (first_x, 1 - first_x, 2 + first_y, 3 - first_y)
    else:
        order = (0, 1, 2, 3)
    node = iota((nodes, LANE), 0)
    lane = iota((nodes, LANE), 1)
    for i in range(4):
        perm_ref[:, i * LANE:(i + 1) * LANE] = hot(node == shared[pl.ds(order[i], 1), :])
    on_face = mm(perm_ref[:, :FACE], jnp.ones((FACE, LANE), BF))
    inner = (1.0 - on_face).astype(BF)
    below = hot(iota((LANE, LANE), 1) < iota((LANE, LANE), 0))
    ranks = []
    seen = jnp.zeros((1, LANE), F32)
    for j in range(nodes // LANE):
        part = inner[j * LANE:(j + 1) * LANE]
        ranks.append(mm(below, part) + seen)
        seen = seen + jnp.sum(part.astype(F32), axis=0, keepdims=True)
    rank = jnp.concatenate(ranks, axis=0)
    rank = jnp.where(on_face > 0.5, -1.0, rank).astype(jnp.int32)
    for j in range((nodes - FACE) // LANE):
        perm_ref[:, FACE + j * LANE:FACE + (j + 1) * LANE] = hot(rank == lane + j * LANE)
    spot = iota((8, nodes), 1)
    digits = jnp.where(iota((8, nodes), 0) == 0, spot >> 4, spot & 15).astype(F32).astype(BF)
    place = mm_nt(digits, perm_ref[...]).astype(BF)
    y0 = mm(x[...], perm_ref[...])
    wide_node = iota((nodes, wide), 0)
    tail = degree_nodes + (-degree_nodes) % 16
    row = iota((16, wide), 0)
    diagonal = jnp.zeros((1, nodes), F32)
    for c in range(cells):
        share = jnp.where(c < count[0, 0], 2.0 / HALF_WIDTH, 0.0)
        weight = share * scale[0, c]
        link = links[c:c + 1, :]
        found = mm(place, hot(wide_node == link))
        where = jnp.where(link < 0, -1.0, found[0:1] * 16.0 + found[1:2]).astype(jnp.int32)
        select = hot(wide_node == where)
        tcat[:, c * wide:(c + 1) * wide] = select
        value = weight * table[cells:cells + 1, :] + share * table[c:c + 1, :]
        high = value.astype(BF).astype(F32)
        middle = (value - high).astype(BF).astype(F32)
        low = value - high - middle
        off[tail:tail + 16, :] = jnp.where(
            row == 0, high, jnp.where(row == 1, middle, jnp.where(row == 2, low, 0.0))
        ).astype(BF)
        moved = mm_nt(off[...], select)
        diagonal = diagonal + jnp.sum(moved[tail:tail + 16], axis=0, keepdims=True)
        vcat[c * wide:(c + 1) * wide, :] = (moved * weight).astype(BF)
    diagonal_ref[...] = jnp.broadcast_to(diagonal, diagonal_ref.shape)
    matrix_ref[:FACE, :] = mm(tcat[:FACE, :], vcat[...]).astype(BF)
    matrix_ref[FACE:, FACE:] = mm(tcat[FACE:, :], vcat[:, FACE:]).astype(BF)
    matrix_ref[FACE:, :FACE] = matrix_ref[:FACE, FACE:].T
    y0_ref[...] = y0
    applied = apply_operator(y0, matrix_ref, diagonal_ref)
    if paired:
        rows = x.shape[0]
        rest_ref[...] = applied
        pack_faces(sends[0], applied)
        sends[0][2 * rows:, :] = matrix_ref[FY:FY + LANE, FX:FX + LANE]
    else:
        rest_ref[...] = 0.5 * (applied - y0)
        for send, at in zip(sends, spots):
            send[...] = applied[:, at:at + LANE].astype(BF)


def pack_faces(out_ref, applied):
    rows = applied.shape[0]
    out_ref[:rows, :] = applied[:, FX:FX + LANE].astype(BF)
    out_ref[rows:2 * rows, :] = applied[:, FY:FY + LANE].astype(BF)


def build(spots, paired, counts, scale, conn, pot, shared, stiff, x):
    cells, degree_nodes = conn.shape
    rows, nodes = x.shape
    wide = -(-(degree_nodes + 32) // LANE) * LANE
    f = lambda *s: jax.ShapeDtypeStruct(s, F32)
    b = lambda *s: jax.ShapeDtypeStruct(s, BF)
    outs = (b(nodes, nodes), f(8, nodes), b(nodes, nodes), f(rows, nodes), f(rows, nodes))
    outs += (b(2 * rows + LANE, LANE),) if paired else (b(rows, LANE),) * len(spots)
    return pl.pallas_call(
        functools.partial(build_kernel, spots, paired),
        out_shape=outs,
        in_specs=[HBM] * 7,
        out_specs=(VMEM,) * len(outs),
        scratch_shapes=[
            pltpu.SMEM(counts.shape, counts.dtype),
            pltpu.SMEM(scale.shape, F32),
            pltpu.VMEM(conn.shape, jnp.int32),
            pltpu.VMEM(pot.shape, F32),
            pltpu.VMEM(shared.shape, jnp.int32),
            pltpu.VMEM(stiff.shape, BF),
            pltpu.VMEM(x.shape, BF),
            pltpu.VMEM((nodes, cells * wide), BF),
            pltpu.VMEM((cells * wide, nodes), BF),
            pltpu.VMEM((wide, wide), BF),
            pltpu.VMEM((8, wide), F32),
            pltpu.VMEM((8, wide), jnp.int32),
            pltpu.SemaphoreType.DMA((7,)),
        ],
        compiler_params=pltpu.CompilerParams(vmem_limit_bytes=40 << 20),
        cost_estimate=pl.CostEstimate(flops=5_000_000_000, bytes_accessed=5_000_000, transcendentals=0),
        name="build",
    )(counts, *(pltpu.with_memory_space_constraint(v, pltpu.HBM) for v in (scale, conn, pot, shared, stiff, x)))


def step_kernel(spots, factor, last, matrix_ref, diagonal_ref, rest_ref, before_ref, *refs):
    count = len(spots)
    received = refs[:count]
    outs = refs[count:]
    field_ref, outs = (outs[-1], outs[:-1]) if last else (outs[0], outs[1:])
    field_ref[...] = rest_ref[...]
    for got, at in zip(received, spots):
        field_ref[:, at:at + LANE] += factor * got[...].astype(F32)
    field = field_ref[...]
    applied = apply_operator(field, matrix_ref, diagonal_ref)
    outs[0][...] = applied - field - before_ref[...]
    for send, at in zip(outs[1:], spots):
        send[...] = applied[:, at:at + LANE].astype(BF)


def step(spots, factor, last, matrix, diagonal, rest, before, received):
    rows, nodes = rest.shape
    field = jax.ShapeDtypeStruct((rows, nodes), F32)
    outs = (field,) * (1 if last else 2) + (jax.ShapeDtypeStruct((rows, LANE), BF),) * len(spots)
    return pl.pallas_call(
        functools.partial(step_kernel, spots, factor, last),
        out_shape=outs,
        in_specs=[VMEM] * (4 + len(spots)),
        out_specs=(VMEM,) * len(outs),
        scratch_shapes=[pltpu.VMEM((rows, nodes), F32)] if last else [],
        compiler_params=pltpu.CompilerParams(vmem_limit_bytes=16 << 20),
        cost_estimate=pl.CostEstimate(flops=110_000_000, bytes_accessed=3_000_000, transcendentals=0),
        name="step",
    )(matrix, diagonal, rest, before, *received)


def finish_kernel(spots, rest_ref, *refs):
    received, out_ref = refs[:-1], refs[-1]
    out_ref[...] = rest_ref[...].astype(BF)
    for got, at in zip(received, spots):
        out_ref[:, at:at + LANE] = (rest_ref[:, at:at + LANE] + got[...].astype(F32)).astype(BF)


def finish(spots, rest, received):
    return pl.pallas_call(
        functools.partial(finish_kernel, spots),
        out_shape=jax.ShapeDtypeStruct(rest.shape, BF),
        in_specs=[VMEM] * (1 + len(spots)),
        out_specs=VMEM,
        compiler_params=pltpu.CompilerParams(vmem_limit_bytes=8 << 20),
        name="finish",
    )(rest, *received)


def owner_row(nodes, place_x, place_y):
    lane = iota((1, nodes), 1)
    hidden = ((lane < LANE) & (place_x > 0)) | ((lane >= 2 * LANE) & (lane < 3 * LANE) & (place_y > 0))
    return jnp.where(hidden, 0.0, 1.0)


def products_kernel(hops, own_ref, side_ref, mine_ref, other_ref, *refs):
    zs = len(hops) + 1
    columns = refs[:zs - 1]
    rot_ref, turn_ref, keep_ref, give_ref, fields, pair, coef = refs[zs - 1:]
    width, nodes = own_ref.shape
    at = lax.axis_index("band")
    z, x = at // 2, at % 2
    fields[:, 1 - x] = jnp.zeros((zs, width, nodes), BF)
    fields[z, x] = own_ref[...]
    for k, column in zip(hops, columns):
        fields[z ^ k, x] = column[...]
    coef[:width] = mine_ref[...]
    coef[width:] = other_ref[...]
    turned = mm(coef[...], fields[...].reshape(zs * 2 * width, nodes))
    rot_ref[...] = turned[:width]
    turn_ref[...] = turned[width:].astype(BF)
    owner = owner_row(nodes, lax.axis_index("dx"), lax.axis_index("dy"))
    pair[:width] = (own_ref[...].astype(F32) * owner).astype(BF)
    pair[width:] = (side_ref[...].astype(F32) * owner).astype(BF)
    p = lax.axis_index("dx") * 2 + lax.axis_index("dy")
    for j, ref in enumerate((keep_ref, keep_ref, give_ref, give_ref)):
        ref[j % 2] = mm_nt(fields[p ^ j, x], pair[...])


def products(hops, own, side, mine, other, columns):
    width, nodes = own.shape
    zs = len(hops) + 1
    f = lambda *s: jax.ShapeDtypeStruct(s, F32)
    outs = (f(width, nodes), jax.ShapeDtypeStruct((width, nodes), BF),
            f(2, width, 2 * width), f(2, width, 2 * width))
    return pl.pallas_call(
        functools.partial(products_kernel, hops),
        out_shape=outs,
        in_specs=[VMEM] * (4 + len(columns)),
        out_specs=(VMEM,) * 4,
        scratch_shapes=[
            pltpu.VMEM((zs, 2, width, nodes), BF),
            pltpu.VMEM((2 * width, nodes), BF),
            pltpu.VMEM((2 * width, zs * 2 * width), BF),
        ],
        compiler_params=pltpu.CompilerParams(vmem_limit_bytes=16 << 20),
        cost_estimate=pl.CostEstimate(flops=200_000_000, bytes_accessed=2_000_000, transcendentals=0),
        name="products",
    )(own, side, mine, other, *columns)


def rotated_kernel(mine_ref, got_ref, perm_ref, out_ref):
    total = (mine_ref[...] + got_ref[...].astype(F32)).astype(BF)
    out_ref[...] = mm_nt(total, perm_ref[...]).astype(BF)


def rotated_of(mine, got, perm):
    return pl.pallas_call(
        rotated_kernel,
        out_shape=jax.ShapeDtypeStruct(mine.shape, BF),
        in_specs=[VMEM] * 3,
        out_specs=VMEM,
        compiler_params=pltpu.CompilerParams(vmem_limit_bytes=16 << 20),
        cost_estimate=pl.CostEstimate(flops=110_000_000, bytes_accessed=3_000_000, transcendentals=0),
        name="rotated",
    )(mine, got, perm)


def margin_kernel(owned, own_ref, below_ref, side_ref, corner_ref, out_ref):
    width = own_ref.shape[0]
    x = lax.axis_index("band") % 2
    here = (own_ref[...] + below_ref[...].astype(F32)).T[:width] * (1.0 / owned)
    there = (side_ref[...].astype(F32) + corner_ref[...].astype(F32)).T[width:] * (1.0 / owned)
    out_ref[:, :width] = jnp.where(x == 0, here, there)
    out_ref[:, width:] = jnp.where(x == 0, there, here)


def margin_of(owned, *parts):
    width = parts[0].shape[0]
    return pl.pallas_call(
        functools.partial(margin_kernel, owned),
        out_shape=jax.ShapeDtypeStruct((width, 2 * width), F32),
        in_specs=[VMEM] * len(parts),
        out_specs=VMEM,
        compiler_params=pltpu.CompilerParams(vmem_limit_bytes=8 << 20),
        name="margin",
    )(*parts)


def swap(value, axis):
    return lax.ppermute(value, axis, [(0, 1), (1, 0)])


def split3(value):
    high = value.astype(BF).astype(F32)
    middle = (value - high).astype(BF).astype(F32)
    return high, middle, value - high - middle


def advance_kernel(first, matrix_ref, diagonal_ref, applied_ref, field_ref, *refs):
    before_ref = None if first else refs[0]
    got_ref, next_ref, product_ref, to_x_ref, to_y_ref = refs[0 if first else 1:]
    rows = field_ref.shape[0]
    if first:
        next_ref[...] = 0.5 * (applied_ref[...] - field_ref[...])
        next_ref[:, FX:FX + LANE] += 0.5 * got_ref[:rows, :].astype(F32)
    else:
        next_ref[...] = applied_ref[...] - field_ref[...] - before_ref[...]
        next_ref[:, FX:FX + LANE] += got_ref[:rows, :].astype(F32)
    product = apply_operator(next_ref[...], matrix_ref, diagonal_ref)
    product_ref[...] = product
    to_x_ref[...] = product[:, FX:FX + LANE].astype(BF)
    to_y_ref[:rows, :] = applied_ref[:, FY:FY + LANE].astype(BF)
    to_y_ref[rows:2 * rows, :] = product[:, FY:FY + LANE].astype(BF)
    to_y_ref[2 * rows:3 * rows, :] = got_ref[rows:2 * rows, :]
    if first:
        to_y_ref[3 * rows:3 * rows + LANE, :] = matrix_ref[FY:FY + LANE, FY:FY + LANE]
        high, middle, low = split3(diagonal_ref[0:1, FY:FY + LANE])
        row = iota((SPLIT, LANE), 0)
        to_y_ref[3 * rows + LANE:, :] = jnp.where(
            row == 0, high, jnp.where(row == 1, middle, jnp.where(row == 2, low, 0.0))
        ).astype(BF)


def advance(matrix, diagonal, applied, field, before, got):
    first = before is None
    rows, nodes = field.shape
    f = jax.ShapeDtypeStruct((rows, nodes), F32)
    down = 3 * rows + (LANE + SPLIT if first else 0)
    args = (matrix, diagonal, applied, field) + (() if first else (before,)) + (got,)
    return pl.pallas_call(
        functools.partial(advance_kernel, first),
        out_shape=(f, f, jax.ShapeDtypeStruct((rows, LANE), BF), jax.ShapeDtypeStruct((down, LANE), BF)),
        in_specs=[VMEM] * len(args),
        out_specs=(VMEM,) * 4,
        compiler_params=pltpu.CompilerParams(vmem_limit_bytes=16 << 20),
        cost_estimate=pl.CostEstimate(flops=110_000_000, bytes_accessed=3_000_000, transcendentals=0),
        name="advance",
    )(*args)


def correct_kernel(
    first, matrix_ref, diagonal_ref, applied_ref, field_ref, next_ref, product_ref,
    from_x_ref, from_y_ref, block_x_ref, block_y_ref, *outs,
):
    rows = field_ref.shape[0]
    scale = 0.5 if first else 1.0
    total_ref = outs[-1]
    given = scale * from_y_ref[:rows, :].astype(F32)
    sent = scale * applied_ref[:, FY:FY + LANE].astype(BF).astype(F32)
    corner = scale * from_y_ref[2 * rows:3 * rows, :].astype(F32)
    tail = block_y_ref[3 * rows + LANE:3 * rows + LANE + 8, :].astype(F32)
    their_diagonal = tail[0:1] + tail[1:2] + tail[2:3]
    their_y = (
        from_y_ref[rows:2 * rows, :].astype(F32)
        + mm(sent.astype(BF), block_y_ref[3 * rows:3 * rows + LANE, :])
        + sent * their_diagonal
    )
    their_x = from_x_ref[...].astype(F32) + mm(corner.astype(BF), block_x_ref[2 * rows:2 * rows + LANE, :])
    total_ref[...] = (
        product_ref[...] + mm(given.astype(BF), matrix_ref[FY:FY + LANE, :])
        - next_ref[...] - field_ref[...]
    )
    total_ref[:, FX:FX + LANE] += their_x
    total_ref[:, FY:FY + LANE] += their_y + given * (diagonal_ref[0:1, FY:FY + LANE] - 1.0)
    if first:
        middle_ref, second_ref, again_ref, pack_ref = outs[:-1]
        middle_ref[...] = next_ref[...]
        middle_ref[:, FY:FY + LANE] += given
        second = total_ref[...]
        second_ref[...] = second
        applied = apply_operator(second, matrix_ref, diagonal_ref)
        again_ref[...] = applied
        pack_faces(pack_ref, applied)
    else:
        outs[0][...] = total_ref[...].astype(BF)


def correct(first, matrix, diagonal, applied, field, ahead, product, from_x, from_y, block_x, block_y):
    rows, nodes = field.shape
    f = jax.ShapeDtypeStruct((rows, nodes), F32)
    outs = (f, f, f, jax.ShapeDtypeStruct((2 * rows, LANE), BF)) if first else (jax.ShapeDtypeStruct((rows, nodes), BF),)
    return pl.pallas_call(
        functools.partial(correct_kernel, first),
        out_shape=outs,
        in_specs=[VMEM] * 10,
        out_specs=(VMEM,) * len(outs),
        scratch_shapes=[pltpu.VMEM((rows, nodes), F32)],
        compiler_params=pltpu.CompilerParams(vmem_limit_bytes=16 << 20),
        cost_estimate=pl.CostEstimate(flops=150_000_000, bytes_accessed=3_000_000, transcendentals=0),
        name="correct",
    )(matrix, diagonal, applied, field, ahead, product, from_x, from_y, block_x, block_y)


def filter_pairs(matrix, diagonal, field, applied, pack):
    block_x = got = swap(pack, "dx")
    ahead, product, to_x, to_y = advance(matrix, diagonal, applied, field, None, got)
    block_y = swap(to_y, "dy")
    field, second, applied, pack = correct(
        True, matrix, diagonal, applied, field, ahead, product, swap(to_x, "dx"), block_y, block_x, block_y
    )
    got = swap(pack, "dx")
    ahead, product, to_x, to_y = advance(matrix, diagonal, applied, second, field, got)
    return correct(
        False, matrix, diagonal, applied, second, ahead, product, swap(to_x, "dx"), swap(to_y, "dy"), block_x, block_y
    )[0]


def from_behind(block, axis, distance):
    devices = range(lax.axis_size(axis))
    route = [(i - distance, i) for i in devices if i - distance in devices]
    return lax.ppermute(block, axis, route)


def on_device(waves, stiff, cell_scale, cell_pot, conn, counts, shared, rotation):
    width, nodes = waves.shape[0], waves.shape[3]
    cells, degree_nodes = conn.shape[2:]
    share = shared.shape[3]
    count_x, count_y = lax.axis_size("dx"), lax.axis_size("dy")
    bands = lax.axis_size("band")
    owned = nodes * count_x * count_y - share * (2 * count_x * count_y - count_x - count_y)
    paired = count_x == 2 and count_y == 2 and bands == 2 * count_x * count_y
    x = waves.reshape(width, nodes)
    spots = (0, LANE, 2 * LANE, 3 * LANE)

    def exchange(sends):
        return (
            from_behind(sends[1], "dx", 1), from_behind(sends[0], "dx", -1),
            from_behind(sends[3], "dy", 1), from_behind(sends[2], "dy", -1),
        )

    matrix, diagonal, perm, before, rest, *sends = build(
        spots, paired, counts, cell_scale.reshape(1, cells),
        conn.reshape(cells, degree_nodes), cell_pot.reshape(cells, degree_nodes),
        shared.reshape(4, share), stiff, x,
    )
    if paired:
        filtered = filter_pairs(matrix, diagonal, before, rest, sends[0])
    else:
        for degree_step in range(DEGREE - 1):
            factor = 0.5 if degree_step == 0 else 1.0
            received = exchange(sends)
            if degree_step < DEGREE - 2:
                field, rest, *sends = step(spots, factor, False, matrix, diagonal, rest, before, received)
                before = field
            else:
                rest, *sends = step(spots, factor, True, matrix, diagonal, rest, before, received)
        filtered = finish(spots, rest, exchange(sends))

    if paired:
        across = [(i, i ^ 1) for i in range(bands)]
        other = lax.ppermute(rotation, "band", across)
        hops = (3, 1, 2)
        routes = [[(i, i ^ (2 * k)) for i in range(bands)] for k in hops]
        columns = [lax.ppermute(filtered, "band", route) for route in routes[:2]]
        side = lax.ppermute(filtered, "band", across)
        columns.append(lax.ppermute(filtered, "band", routes[2]))
        mine, turn, keep, give = products(hops, filtered, side, rotation, other, columns)
        got = lax.ppermute(turn, "band", across)
        corner = [
            (2 * i + j, 2 * (i ^ 1) + (j ^ 1)) for i in range(bands) for j in range(count_y)
        ]
        half = keep + swap(give, "dx")
        own, below = half[0], half[1].astype(BF)
        aside, away = own.astype(BF), below
        rotated = rotated_of(mine, got, perm)
        below = swap(below, "dy")
        aside = lax.ppermute(aside, "band", across)
        away = lax.ppermute(away, ("band", "dy"), corner)
        own, rotated = lax.optimization_barrier((own, rotated))
        margin = margin_of(owned, own, below, aside, away)
    else:
        gathered = lax.all_gather(filtered, "band", axis=0, tiled=True)
        owner = owner_row(nodes, lax.axis_index("dx"), lax.axis_index("dy")).astype(BF)
        block = mm_nt(filtered * owner, gathered)
        block = lax.psum_scatter(block, ("dx", "dy"), scatter_dimension=1, tiled=True)
        margin = block * (1.0 / owned)
        rotated = mm_nt(mm(rotation, gathered).astype(BF), perm).astype(BF)
    return margin, rotated.reshape(width, 1, 1, nodes)


def solution(mesh):
    return jax.shard_map(
        on_device,
        mesh=mesh,
        in_specs=(
            P("band", "dx", "dy", None),
            P(),
            P("dx", "dy", None),
            P("dx", "dy", None, None),
            P("dx", "dy", None, None),
            P("dx", "dy"),
            P("dx", "dy", None, None),
            P("band", None),
        ),
        out_specs=(P("band", ("dx", "dy")), P("band", "dx", "dy", None)),
        check_vma=False,
    )
```

```python
import functools

import jax
import jax.numpy as jnp
from jax import lax
from jax.experimental import pallas as pl
from jax.experimental.pallas import tpu as pltpu
from jax.sharding import PartitionSpec as P

DEGREE = 4
LANE = 128
SHIFT_CENTER = 3.0
HALF_WIDTH = 6.0
BF = jnp.bfloat16
F32 = jnp.float32
NT = (((1,), (1,)), ((), ()))
FACE = 4 * LANE
FX, FY = 0, 2 * LANE
SPLIT = 16

VMEM = pl.BlockSpec(memory_space=pltpu.VMEM)
HBM = pl.BlockSpec(memory_space=pltpu.HBM)


def iota(shape, dim):
    return lax.broadcasted_iota(jnp.int32, shape, dim)


def hot(mask):
    return mask.astype(F32).astype(BF)


def mm(a, b):
    return jnp.dot(a, b, preferred_element_type=F32)


def mm_nt(a, b):
    return lax.dot_general(a, b, NT, preferred_element_type=F32)


def apply_operator(field, matrix_ref, diagonal_ref):
    return mm(field.astype(BF), matrix_ref[...]) + field * diagonal_ref[0:1, :]


def build_kernel(
    spots, paired,
    counts_hbm, scale_hbm, conn_hbm, pot_hbm, shared_hbm, stiff_hbm, x_hbm,
    matrix_ref, diagonal_ref, perm_ref, y0_ref, rest_ref, *outs_and_scratch,
):
    count_out = 1 if paired else len(spots)
    sends = outs_and_scratch[:count_out]
    (count, scale, conn, pot, shared, stiff, x, tcat, vcat, off, table, links, sems) = outs_and_scratch[count_out:]
    copies = [
        pltpu.make_async_copy(src, dst, sems.at[i])
        for i, (src, dst) in enumerate(
            ((counts_hbm, count), (scale_hbm, scale), (shared_hbm, shared), (conn_hbm, conn),
             (pot_hbm, pot), (stiff_hbm, stiff), (x_hbm, x))
        )
    ]
    for copy in copies:
        copy.start()
    cells, degree_nodes = conn.shape
    nodes = x.shape[1]
    wide = off.shape[0]
    off[...] = jnp.zeros_like(off)
    table[...] = jnp.zeros_like(table)
    links[...] = jnp.full(links.shape, -1, jnp.int32)
    copies[2].wait()
    if paired:
        first_x = 1 - lax.axis_index("dx")
        first_y = 1 - lax.axis_index("dy")
        order = (first_x, 1 - first_x, 2 + first_y, 3 - first_y)
    else:
        order = (0, 1, 2, 3)
    node = iota((nodes, LANE), 0)
    lane = iota((nodes, LANE), 1)
    spot = jnp.zeros((nodes, LANE), F32)
    for i in range(4):
        hit = node == shared[pl.ds(order[i], 1), :]
        perm_ref[:, i * LANE:(i + 1) * LANE] = hot(hit)
        spot = spot + jnp.where(hit, (lane + (i * LANE + 1)).astype(F32), 0.0)
    spot = jnp.broadcast_to(jnp.sum(spot, axis=1, keepdims=True), (nodes, LANE))
    on_face = (spot > 0.0).astype(F32)
    inner = (1.0 - on_face).astype(BF)
    below = hot(iota((LANE, LANE), 1) < iota((LANE, LANE), 0))
    ranks = []
    seen = jnp.zeros((1, LANE), F32)
    for j in range(nodes // LANE):
        part = inner[j * LANE:(j + 1) * LANE]
        ranks.append(mm(below, part) + seen)
        seen = seen + jnp.sum(part.astype(F32), axis=0, keepdims=True)
    rank = jnp.concatenate(ranks, axis=0)
    spot = jnp.where(on_face > 0.5, spot, rank + (FACE + 1))
    rank = jnp.where(on_face > 0.5, -1.0, rank).astype(jnp.int32)
    for j in range((nodes - FACE) // LANE):
        perm_ref[:, FACE + j * LANE:FACE + (j + 1) * LANE] = hot(rank == lane + j * LANE)
    for i in (0, 1, 3, 4, 5, 6):
        copies[i].wait()
    matrix = stiff[...]
    eye = iota(matrix.shape, 0) == iota(matrix.shape, 1)
    off[:degree_nodes, :degree_nodes] = jnp.where(eye, jnp.zeros_like(matrix), matrix)
    table[cells:cells + 1, :degree_nodes] = jnp.sum(
        jnp.where(eye, matrix.astype(F32), 0.0), axis=0, keepdims=True
    )
    table[:cells, :degree_nodes] = pot[...]
    links[:cells, :degree_nodes] = conn[...]
    y0 = mm(x[...], perm_ref[...])
    wide_node = iota((nodes, wide), 0)
    wide_spot = jnp.concatenate([spot] * (wide // LANE), axis=1)
    tail = degree_nodes + (-degree_nodes) % 16
    row = iota((16, wide), 0)
    diagonal = jnp.zeros((1, nodes), F32)
    for c in range(cells):
        share = jnp.where(c < count[0, 0], 2.0 / HALF_WIDTH, 0.0)
        weight = share * scale[0, c]
        link = links[c:c + 1, :]
        found = jnp.sum(jnp.where(wide_node == link, wide_spot, 0.0), axis=0, keepdims=True)
        where = found.astype(jnp.int32) - 1
        select = hot(wide_node == where)
        tcat[:, c * wide:(c + 1) * wide] = select
        value = weight * table[cells:cells + 1, :] + share * table[c:c + 1, :]
        high = value.astype(BF).astype(F32)
        middle = (value - high).astype(BF).astype(F32)
        low = value - high - middle
        off[tail:tail + 16, :] = jnp.where(
            row == 0, high, jnp.where(row == 1, middle, jnp.where(row == 2, low, 0.0))
        ).astype(BF)
        moved = mm_nt(off[...], select)
        diagonal = diagonal + jnp.sum(moved[tail:tail + 16], axis=0, keepdims=True)
        vcat[c * wide:(c + 1) * wide, :] = (moved * weight).astype(BF)
    diagonal_ref[...] = jnp.broadcast_to(diagonal, diagonal_ref.shape)
    for low in range(0, nodes, 2 * LANE):
        high = min(low + 2 * LANE, nodes)
        matrix_ref[low:high, low:] = mm(tcat[low:high, :], vcat[:, low:]).astype(BF)
        if high < nodes:
            matrix_ref[high:, low:high] = matrix_ref[low:high, high:].T
    y0_ref[...] = y0
    applied = apply_operator(y0, matrix_ref, diagonal_ref)
    if paired:
        rows = x.shape[0]
        rest_ref[...] = applied
        pack_faces(sends[0], applied)
        sends[0][2 * rows:, :] = matrix_ref[FY:FY + LANE, FX:FX + LANE]
    else:
        rest_ref[...] = 0.5 * (applied - y0)
        for send, at in zip(sends, spots):
            send[...] = applied[:, at:at + LANE].astype(BF)


def pack_faces(out_ref, applied):
    rows = applied.shape[0]
    out_ref[:rows, :] = applied[:, FX:FX + LANE].astype(BF)
    out_ref[rows:2 * rows, :] = applied[:, FY:FY + LANE].astype(BF)


def build(spots, paired, counts, scale, conn, pot, shared, stiff, x):
    cells, degree_nodes = conn.shape
    rows, nodes = x.shape
    wide = -(-(degree_nodes + 32) // LANE) * LANE
    f = lambda *s: jax.ShapeDtypeStruct(s, F32)
    b = lambda *s: jax.ShapeDtypeStruct(s, BF)
    outs = (b(nodes, nodes), f(8, nodes), b(nodes, nodes), f(rows, nodes), f(rows, nodes))
    outs += (b(2 * rows + LANE, LANE),) if paired else (b(rows, LANE),) * len(spots)
    return pl.pallas_call(
        functools.partial(build_kernel, spots, paired),
        out_shape=outs,
        in_specs=[HBM] * 7,
        out_specs=(VMEM,) * len(outs),
        scratch_shapes=[
            pltpu.SMEM(counts.shape, counts.dtype),
            pltpu.SMEM(scale.shape, F32),
            pltpu.VMEM(conn.shape, jnp.int32),
            pltpu.VMEM(pot.shape, F32),
            pltpu.VMEM(shared.shape, jnp.int32),
            pltpu.VMEM(stiff.shape, BF),
            pltpu.VMEM(x.shape, BF),
            pltpu.VMEM((nodes, cells * wide), BF),
            pltpu.VMEM((cells * wide, nodes), BF),
            pltpu.VMEM((wide, wide), BF),
            pltpu.VMEM((8, wide), F32),
            pltpu.VMEM((8, wide), jnp.int32),
            pltpu.SemaphoreType.DMA((7,)),
        ],
        compiler_params=pltpu.CompilerParams(vmem_limit_bytes=40 << 20),
        cost_estimate=pl.CostEstimate(flops=5_000_000_000, bytes_accessed=5_000_000, transcendentals=0),
        name="build",
    )(counts, *(pltpu.with_memory_space_constraint(v, pltpu.HBM) for v in (scale, conn, pot, shared, stiff, x)))


def step_kernel(spots, factor, last, matrix_ref, diagonal_ref, rest_ref, before_ref, *refs):
    count = len(spots)
    received = refs[:count]
    outs = refs[count:]
    field_ref, outs = (outs[-1], outs[:-1]) if last else (outs[0], outs[1:])
    field_ref[...] = rest_ref[...]
    for got, at in zip(received, spots):
        field_ref[:, at:at + LANE] += factor * got[...].astype(F32)
    field = field_ref[...]
    applied = apply_operator(field, matrix_ref, diagonal_ref)
    outs[0][...] = applied - field - before_ref[...]
    for send, at in zip(outs[1:], spots):
        send[...] = applied[:, at:at + LANE].astype(BF)


def step(spots, factor, last, matrix, diagonal, rest, before, received):
    rows, nodes = rest.shape
    field = jax.ShapeDtypeStruct((rows, nodes), F32)
    outs = (field,) * (1 if last else 2) + (jax.ShapeDtypeStruct((rows, LANE), BF),) * len(spots)
    return pl.pallas_call(
        functools.partial(step_kernel, spots, factor, last),
        out_shape=outs,
        in_specs=[VMEM] * (4 + len(spots)),
        out_specs=(VMEM,) * len(outs),
        scratch_shapes=[pltpu.VMEM((rows, nodes), F32)] if last else [],
        compiler_params=pltpu.CompilerParams(vmem_limit_bytes=16 << 20),
        cost_estimate=pl.CostEstimate(flops=110_000_000, bytes_accessed=3_000_000, transcendentals=0),
        name="step",
    )(matrix, diagonal, rest, before, *received)


def finish_kernel(spots, rest_ref, *refs):
    received, out_ref = refs[:-1], refs[-1]
    out_ref[...] = rest_ref[...].astype(BF)
    for got, at in zip(received, spots):
        out_ref[:, at:at + LANE] = (rest_ref[:, at:at + LANE] + got[...].astype(F32)).astype(BF)


def finish(spots, rest, received):
    return pl.pallas_call(
        functools.partial(finish_kernel, spots),
        out_shape=jax.ShapeDtypeStruct(rest.shape, BF),
        in_specs=[VMEM] * (1 + len(spots)),
        out_specs=VMEM,
        compiler_params=pltpu.CompilerParams(vmem_limit_bytes=8 << 20),
        name="finish",
    )(rest, *received)


def owner_row(nodes, place_x, place_y):
    lane = iota((1, nodes), 1)
    hidden = ((lane < LANE) & (place_x > 0)) | ((lane >= 2 * LANE) & (lane < 3 * LANE) & (place_y > 0))
    return jnp.where(hidden, 0.0, 1.0)


def products_kernel(hops, own_ref, side_ref, mine_ref, other_ref, *refs):
    zs = len(hops) + 1
    columns = refs[:zs - 1]
    rot_ref, turn_ref, keep_ref, give_ref, fields, pair, coef = refs[zs - 1:]
    width, nodes = own_ref.shape
    at = lax.axis_index("band")
    z, x = at // 2, at % 2
    fields[:, 1 - x] = jnp.zeros((zs, width, nodes), BF)
    fields[z, x] = own_ref[...]
    for k, column in zip(hops, columns):
        fields[z ^ k, x] = column[...]
    coef[:width] = mine_ref[...]
    coef[width:] = other_ref[...]
    turned = mm(coef[...], fields[...].reshape(zs * 2 * width, nodes))
    rot_ref[...] = turned[:width]
    turn_ref[...] = turned[width:].astype(BF)
    owner = owner_row(nodes, lax.axis_index("dx"), lax.axis_index("dy"))
    pair[:width] = (own_ref[...].astype(F32) * owner).astype(BF)
    pair[width:] = (side_ref[...].astype(F32) * owner).astype(BF)
    p = lax.axis_index("dx") * 2 + lax.axis_index("dy")
    for j, ref in enumerate((keep_ref, keep_ref, give_ref, give_ref)):
        ref[j % 2] = mm_nt(fields[p ^ j, x], pair[...])


def products(hops, own, side, mine, other, columns):
    width, nodes = own.shape
    zs = len(hops) + 1
    f = lambda *s: jax.ShapeDtypeStruct(s, F32)
    outs = (f(width, nodes), jax.ShapeDtypeStruct((width, nodes), BF),
            f(2, width, 2 * width), f(2, width, 2 * width))
    return pl.pallas_call(
        functools.partial(products_kernel, hops),
        out_shape=outs,
        in_specs=[VMEM] * (4 + len(columns)),
        out_specs=(VMEM,) * 4,
        scratch_shapes=[
            pltpu.VMEM((zs, 2, width, nodes), BF),
            pltpu.VMEM((2 * width, nodes), BF),
            pltpu.VMEM((2 * width, zs * 2 * width), BF),
        ],
        compiler_params=pltpu.CompilerParams(vmem_limit_bytes=16 << 20),
        cost_estimate=pl.CostEstimate(flops=200_000_000, bytes_accessed=2_000_000, transcendentals=0),
        name="products",
    )(own, side, mine, other, *columns)


def rotated_kernel(mine_ref, got_ref, perm_ref, out_ref):
    total = (mine_ref[...] + got_ref[...].astype(F32)).astype(BF)
    out_ref[...] = mm_nt(total, perm_ref[...]).astype(BF)


def rotated_of(mine, got, perm):
    return pl.pallas_call(
        rotated_kernel,
        out_shape=jax.ShapeDtypeStruct(mine.shape, BF),
        in_specs=[VMEM] * 3,
        out_specs=VMEM,
        compiler_params=pltpu.CompilerParams(vmem_limit_bytes=16 << 20),
        cost_estimate=pl.CostEstimate(flops=110_000_000, bytes_accessed=3_000_000, transcendentals=0),
        name="rotated",
    )(mine, got, perm)


def margin_kernel(owned, own_ref, below_ref, side_ref, corner_ref, out_ref):
    width = own_ref.shape[0]
    x = lax.axis_index("band") % 2
    here = (own_ref[...] + below_ref[...].astype(F32)).T[:width] * (1.0 / owned)
    there = (side_ref[...].astype(F32) + corner_ref[...].astype(F32)).T[width:] * (1.0 / owned)
    out_ref[:, :width] = jnp.where(x == 0, here, there)
    out_ref[:, width:] = jnp.where(x == 0, there, here)


def margin_of(owned, *parts):
    width = parts[0].shape[0]
    return pl.pallas_call(
        functools.partial(margin_kernel, owned),
        out_shape=jax.ShapeDtypeStruct((width, 2 * width), F32),
        in_specs=[VMEM] * len(parts),
        out_specs=VMEM,
        compiler_params=pltpu.CompilerParams(vmem_limit_bytes=8 << 20),
        name="margin",
    )(*parts)


def swap(value, axis):
    return lax.ppermute(value, axis, [(0, 1), (1, 0)])


def split3(value):
    high = value.astype(BF).astype(F32)
    middle = (value - high).astype(BF).astype(F32)
    return high, middle, value - high - middle


def advance_kernel(first, matrix_ref, diagonal_ref, applied_ref, field_ref, *refs):
    before_ref = None if first else refs[0]
    got_ref, next_ref, product_ref, to_x_ref, to_y_ref = refs[0 if first else 1:]
    rows = field_ref.shape[0]
    if first:
        next_ref[...] = 0.5 * (applied_ref[...] - field_ref[...])
        next_ref[:, FX:FX + LANE] += 0.5 * got_ref[:rows, :].astype(F32)
    else:
        next_ref[...] = applied_ref[...] - field_ref[...] - before_ref[...]
        next_ref[:, FX:FX + LANE] += got_ref[:rows, :].astype(F32)
    product = apply_operator(next_ref[...], matrix_ref, diagonal_ref)
    product_ref[...] = product
    to_x_ref[...] = product[:, FX:FX + LANE].astype(BF)
    to_y_ref[:rows, :] = applied_ref[:, FY:FY + LANE].astype(BF)
    to_y_ref[rows:2 * rows, :] = product[:, FY:FY + LANE].astype(BF)
    to_y_ref[2 * rows:3 * rows, :] = got_ref[rows:2 * rows, :]
    if first:
        to_y_ref[3 * rows:3 * rows + LANE, :] = matrix_ref[FY:FY + LANE, FY:FY + LANE]
        high, middle, low = split3(diagonal_ref[0:1, FY:FY + LANE])
        row = iota((SPLIT, LANE), 0)
        to_y_ref[3 * rows + LANE:, :] = jnp.where(
            row == 0, high, jnp.where(row == 1, middle, jnp.where(row == 2, low, 0.0))
        ).astype(BF)


def advance(matrix, diagonal, applied, field, before, got):
    first = before is None
    rows, nodes = field.shape
    f = jax.ShapeDtypeStruct((rows, nodes), F32)
    down = 3 * rows + (LANE + SPLIT if first else 0)
    args = (matrix, diagonal, applied, field) + (() if first else (before,)) + (got,)
    return pl.pallas_call(
        functools.partial(advance_kernel, first),
        out_shape=(f, f, jax.ShapeDtypeStruct((rows, LANE), BF), jax.ShapeDtypeStruct((down, LANE), BF)),
        in_specs=[VMEM] * len(args),
        out_specs=(VMEM,) * 4,
        compiler_params=pltpu.CompilerParams(vmem_limit_bytes=16 << 20),
        cost_estimate=pl.CostEstimate(flops=110_000_000, bytes_accessed=3_000_000, transcendentals=0),
        name="advance",
    )(*args)


def correct_kernel(
    first, matrix_ref, diagonal_ref, applied_ref, field_ref, next_ref, product_ref,
    from_x_ref, from_y_ref, block_x_ref, block_y_ref, *outs,
):
    rows = field_ref.shape[0]
    scale = 0.5 if first else 1.0
    total_ref = outs[-1]
    given = scale * from_y_ref[:rows, :].astype(F32)
    sent = scale * applied_ref[:, FY:FY + LANE].astype(BF).astype(F32)
    corner = scale * from_y_ref[2 * rows:3 * rows, :].astype(F32)
    tail = block_y_ref[3 * rows + LANE:3 * rows + LANE + 8, :].astype(F32)
    their_diagonal = tail[0:1] + tail[1:2] + tail[2:3]
    their_y = (
        from_y_ref[rows:2 * rows, :].astype(F32)
        + mm(sent.astype(BF), block_y_ref[3 * rows:3 * rows + LANE, :])
        + sent * their_diagonal
    )
    their_x = from_x_ref[...].astype(F32) + mm(corner.astype(BF), block_x_ref[2 * rows:2 * rows + LANE, :])
    total_ref[...] = (
        product_ref[...] + mm(given.astype(BF), matrix_ref[FY:FY + LANE, :])
        - next_ref[...] - field_ref[...]
    )
    total_ref[:, FX:FX + LANE] += their_x
    total_ref[:, FY:FY + LANE] += their_y + given * (diagonal_ref[0:1, FY:FY + LANE] - 1.0)
    if first:
        middle_ref, second_ref, again_ref, pack_ref = outs[:-1]
        middle_ref[...] = next_ref[...]
        middle_ref[:, FY:FY + LANE] += given
        second = total_ref[...]
        second_ref[...] = second
        applied = apply_operator(second, matrix_ref, diagonal_ref)
        again_ref[...] = applied
        pack_faces(pack_ref, applied)
    else:
        outs[0][...] = total_ref[...].astype(BF)


def correct(first, matrix, diagonal, applied, field, ahead, product, from_x, from_y, block_x, block_y):
    rows, nodes = field.shape
    f = jax.ShapeDtypeStruct((rows, nodes), F32)
    outs = (f, f, f, jax.ShapeDtypeStruct((2 * rows, LANE), BF)) if first else (jax.ShapeDtypeStruct((rows, nodes), BF),)
    return pl.pallas_call(
        functools.partial(correct_kernel, first),
        out_shape=outs,
        in_specs=[VMEM] * 10,
        out_specs=(VMEM,) * len(outs),
        scratch_shapes=[pltpu.VMEM((rows, nodes), F32)],
        compiler_params=pltpu.CompilerParams(vmem_limit_bytes=16 << 20),
        cost_estimate=pl.CostEstimate(flops=150_000_000, bytes_accessed=3_000_000, transcendentals=0),
        name="correct",
    )(matrix, diagonal, applied, field, ahead, product, from_x, from_y, block_x, block_y)


def filter_pairs(matrix, diagonal, field, applied, pack):
    block_x = got = swap(pack, "dx")
    ahead, product, to_x, to_y = advance(matrix, diagonal, applied, field, None, got)
    block_y = swap(to_y, "dy")
    field, second, applied, pack = correct(
        True, matrix, diagonal, applied, field, ahead, product, swap(to_x, "dx"), block_y, block_x, block_y
    )
    got = swap(pack, "dx")
    ahead, product, to_x, to_y = advance(matrix, diagonal, applied, second, field, got)
    return correct(
        False, matrix, diagonal, applied, second, ahead, product, swap(to_x, "dx"), swap(to_y, "dy"), block_x, block_y
    )[0]


def from_behind(block, axis, distance):
    devices = range(lax.axis_size(axis))
    route = [(i - distance, i) for i in devices if i - distance in devices]
    return lax.ppermute(block, axis, route)


def on_device(waves, stiff, cell_scale, cell_pot, conn, counts, shared, rotation):
    width, nodes = waves.shape[0], waves.shape[3]
    cells, degree_nodes = conn.shape[2:]
    share = shared.shape[3]
    count_x, count_y = lax.axis_size("dx"), lax.axis_size("dy")
    bands = lax.axis_size("band")
    owned = nodes * count_x * count_y - share * (2 * count_x * count_y - count_x - count_y)
    paired = count_x == 2 and count_y == 2 and bands == 2 * count_x * count_y
    x = waves.reshape(width, nodes)
    spots = (0, LANE, 2 * LANE, 3 * LANE)

    def exchange(sends):
        return (
            from_behind(sends[1], "dx", 1), from_behind(sends[0], "dx", -1),
            from_behind(sends[3], "dy", 1), from_behind(sends[2], "dy", -1),
        )

    matrix, diagonal, perm, before, rest, *sends = build(
        spots, paired, counts, cell_scale.reshape(1, cells),
        conn.reshape(cells, degree_nodes), cell_pot.reshape(cells, degree_nodes),
        shared.reshape(4, share), stiff, x,
    )
    if paired:
        filtered = filter_pairs(matrix, diagonal, before, rest, sends[0])
    else:
        for degree_step in range(DEGREE - 1):
            factor = 0.5 if degree_step == 0 else 1.0
            received = exchange(sends)
            if degree_step < DEGREE - 2:
                field, rest, *sends = step(spots, factor, False, matrix, diagonal, rest, before, received)
                before = field
            else:
                rest, *sends = step(spots, factor, True, matrix, diagonal, rest, before, received)
        filtered = finish(spots, rest, exchange(sends))

    if paired:
        across = [(i, i ^ 1) for i in range(bands)]
        other = lax.ppermute(rotation, "band", across)
        hops = (3, 1, 2)
        routes = [[(i, i ^ (2 * k)) for i in range(bands)] for k in hops]
        columns = [lax.ppermute(filtered, "band", route) for route in routes[:2]]
        side = lax.ppermute(filtered, "band", across)
        columns.append(lax.ppermute(filtered, "band", routes[2]))
        mine, turn, keep, give = products(hops, filtered, side, rotation, other, columns)
        got = lax.ppermute(turn, "band", across)
        corner = [
            (2 * i + j, 2 * (i ^ 1) + (j ^ 1)) for i in range(bands) for j in range(count_y)
        ]
        half = keep + swap(give, "dx")
        own, below = half[0], half[1].astype(BF)
        aside, away = own.astype(BF), below
        rotated = rotated_of(mine, got, perm)
        below = swap(below, "dy")
        aside = lax.ppermute(aside, "band", across)
        away = lax.ppermute(away, ("band", "dy"), corner)
        own, rotated = lax.optimization_barrier((own, rotated))
        margin = margin_of(owned, own, below, aside, away)
    else:
        gathered = lax.all_gather(filtered, "band", axis=0, tiled=True)
        owner = owner_row(nodes, lax.axis_index("dx"), lax.axis_index("dy")).astype(BF)
        block = mm_nt(filtered * owner, gathered)
        block = lax.psum_scatter(block, ("dx", "dy"), scatter_dimension=1, tiled=True)
        margin = block * (1.0 / owned)
        rotated = mm_nt(mm(rotation, gathered).astype(BF), perm).astype(BF)
    return margin, rotated.reshape(width, 1, 1, nodes)


def solution(mesh):
    return jax.shard_map(
        on_device,
        mesh=mesh,
        in_specs=(
            P("band", "dx", "dy", None),
            P(),
            P("dx", "dy", None),
            P("dx", "dy", None, None),
            P("dx", "dy", None, None),
            P("dx", "dy"),
            P("dx", "dy", None, None),
            P("band", None),
        ),
        out_specs=(P("band", ("dx", "dy")), P("band", "dx", "dy", None)),
        check_vma=False,
    )
```

```python
import functools

import jax
import jax.numpy as jnp
from jax import lax
from jax.experimental import pallas as pl
from jax.experimental.pallas import tpu as pltpu
from jax.sharding import PartitionSpec as P

DEGREE = 4
LANE = 128
SHIFT_CENTER = 3.0
HALF_WIDTH = 6.0
BF = jnp.bfloat16
F32 = jnp.float32
NT = (((1,), (1,)), ((), ()))
FACE = 4 * LANE
FX, FY = 0, 2 * LANE
SPLIT = 16

VMEM = pl.BlockSpec(memory_space=pltpu.VMEM)
HBM = pl.BlockSpec(memory_space=pltpu.HBM)


def iota(shape, dim):
    return lax.broadcasted_iota(jnp.int32, shape, dim)


def hot(mask):
    return jnp.where(mask, 1.0, 0.0).astype(BF)


def hot16(mask):
    return jnp.where(mask, jnp.ones((), BF), jnp.zeros((), BF))


def mm(a, b):
    return jnp.dot(a, b, preferred_element_type=F32)


def mm_nt(a, b):
    return lax.dot_general(a, b, NT, preferred_element_type=F32)


def apply_operator(field, matrix_ref, diagonal_ref):
    return mm(field.astype(BF), matrix_ref[...]) + field * diagonal_ref[0:1, :]


def build_kernel(
    spots, paired,
    counts_hbm, scale_hbm, conn_hbm, pot_hbm, shared_hbm, stiff_hbm, x_hbm,
    matrix_ref, diagonal_ref, perm_ref, y0_ref, rest_ref, *outs_and_scratch,
):
    count_out = 1 if paired else len(spots)
    sends = outs_and_scratch[:count_out]
    (count, scale, conn, pot, shared, stiff, x, tcat, vcat, off, table, links, sems) = outs_and_scratch[count_out:]
    copies = [
        pltpu.make_async_copy(src, dst, sems.at[i])
        for i, (src, dst) in enumerate(
            ((counts_hbm, count), (scale_hbm, scale), (shared_hbm, shared), (conn_hbm, conn),
             (pot_hbm, pot), (stiff_hbm, stiff), (x_hbm, x))
        )
    ]
    for copy in copies:
        copy.start()
    cells, degree_nodes = conn.shape
    nodes = x.shape[1]
    wide = off.shape[0]
    off[...] = jnp.zeros_like(off)
    table[...] = jnp.zeros_like(table)
    links[...] = jnp.full(links.shape, -1, jnp.int32)
    copies[2].wait()
    if paired:
        first_x = 1 - lax.axis_index("dx")
        first_y = 1 - lax.axis_index("dy")
        order = (first_x, 1 - first_x, 2 + first_y, 3 - first_y)
    else:
        order = (0, 1, 2, 3)
    node = iota((nodes, LANE), 0)
    lane = iota((nodes, LANE), 1)
    spot = jnp.zeros((nodes, LANE), F32)
    for i in range(4):
        hit = node == shared[pl.ds(order[i], 1), :]
        perm_ref[:, i * LANE:(i + 1) * LANE] = hot(hit)
        spot = spot + jnp.where(hit, (lane + (i * LANE + 1)).astype(F32), 0.0)
    spot = jnp.broadcast_to(jnp.sum(spot, axis=1, keepdims=True), (nodes, LANE))
    on_face = (spot > 0.0).astype(F32)
    inner = (1.0 - on_face).astype(BF)
    below = hot(iota((LANE, LANE), 1) < iota((LANE, LANE), 0))
    ranks = []
    seen = jnp.zeros((1, LANE), F32)
    for j in range(nodes // LANE):
        part = inner[j * LANE:(j + 1) * LANE]
        ranks.append(mm(below, part) + seen)
        seen = seen + jnp.sum(part.astype(F32), axis=0, keepdims=True)
    rank = jnp.concatenate(ranks, axis=0)
    spot = jnp.where(on_face > 0.5, spot, rank + (FACE + 1))
    rank = jnp.where(on_face > 0.5, -1.0, rank).astype(jnp.int32).astype(jnp.int16)
    narrow_lane = lane.astype(jnp.int16)
    for j in range((nodes - FACE) // LANE):
        perm_ref[:, FACE + j * LANE:FACE + (j + 1) * LANE] = hot16(rank == narrow_lane + jnp.int16(j * LANE))
    for i in (0, 1, 3, 4, 5, 6):
        copies[i].wait()
    matrix = stiff[...]
    eye = iota(matrix.shape, 0) == iota(matrix.shape, 1)
    off[:degree_nodes, :degree_nodes] = jnp.where(eye, jnp.zeros_like(matrix), matrix)
    table[cells:cells + 1, :degree_nodes] = jnp.sum(
        jnp.where(eye, matrix.astype(F32), 0.0), axis=0, keepdims=True
    )
    table[:cells, :degree_nodes] = pot[...]
    links[:cells, :degree_nodes] = conn[...]
    y0 = mm(x[...], perm_ref[...])
    wide_node = iota((nodes, wide), 0)
    narrow_node = wide_node.astype(jnp.int16)
    wide_spot = jnp.concatenate([spot] * (wide // LANE), axis=1)
    tail = degree_nodes + (-degree_nodes) % 16
    row = iota((16, wide), 0)
    diagonal = jnp.zeros((1, nodes), F32)
    for c in range(cells):
        share = jnp.where(c < count[0, 0], 2.0 / HALF_WIDTH, 0.0)
        weight = share * scale[0, c]
        link = links[c:c + 1, :]
        found = jnp.sum(jnp.where(wide_node == link, wide_spot, 0.0), axis=0, keepdims=True)
        where = found.astype(jnp.int32) - 1
        select = hot16(narrow_node == where.astype(jnp.int16))
        tcat[:, c * wide:(c + 1) * wide] = select
        value = weight * table[cells:cells + 1, :] + share * table[c:c + 1, :]
        high = value.astype(BF).astype(F32)
        middle = (value - high).astype(BF).astype(F32)
        low = value - high - middle
        off[tail:tail + 16, :] = jnp.where(
            row == 0, high, jnp.where(row == 1, middle, jnp.where(row == 2, low, 0.0))
        ).astype(BF)
        moved = mm_nt(off[...], select)
        diagonal = diagonal + jnp.sum(moved[tail:tail + 16], axis=0, keepdims=True)
        vcat[c * wide:(c + 1) * wide, :] = (moved * weight).astype(BF)
    diagonal_ref[...] = jnp.broadcast_to(diagonal, diagonal_ref.shape)
    for low in range(0, nodes, 2 * LANE):
        high = min(low + 2 * LANE, nodes)
        matrix_ref[low:high, low:] = mm(tcat[low:high, :], vcat[:, low:]).astype(BF)
        if high < nodes:
            matrix_ref[high:, low:high] = matrix_ref[low:high, high:].T
    y0_ref[...] = y0
    applied = apply_operator(y0, matrix_ref, diagonal_ref)
    if paired:
        rows = x.shape[0]
        rest_ref[...] = applied
        pack_faces(sends[0], applied)
        sends[0][2 * rows:, :] = matrix_ref[FY:FY + LANE, FX:FX + LANE]
    else:
        rest_ref[...] = 0.5 * (applied - y0)
        for send, at in zip(sends, spots):
            send[...] = applied[:, at:at + LANE].astype(BF)


def pack_faces(out_ref, applied):
    rows = applied.shape[0]
    out_ref[:rows, :] = applied[:, FX:FX + LANE].astype(BF)
    out_ref[rows:2 * rows, :] = applied[:, FY:FY + LANE].astype(BF)


def build(spots, paired, counts, scale, conn, pot, shared, stiff, x):
    cells, degree_nodes = conn.shape
    rows, nodes = x.shape
    wide = -(-(degree_nodes + 32) // LANE) * LANE
    f = lambda *s: jax.ShapeDtypeStruct(s, F32)
    b = lambda *s: jax.ShapeDtypeStruct(s, BF)
    outs = (b(nodes, nodes), f(8, nodes), b(nodes, nodes), f(rows, nodes), f(rows, nodes))
    outs += (b(2 * rows + LANE, LANE),) if paired else (b(rows, LANE),) * len(spots)
    return pl.pallas_call(
        functools.partial(build_kernel, spots, paired),
        out_shape=outs,
        in_specs=[HBM] * 7,
        out_specs=(VMEM,) * len(outs),
        scratch_shapes=[
            pltpu.SMEM(counts.shape, counts.dtype),
            pltpu.SMEM(scale.shape, F32),
            pltpu.VMEM(conn.shape, jnp.int32),
            pltpu.VMEM(pot.shape, F32),
            pltpu.VMEM(shared.shape, jnp.int32),
            pltpu.VMEM(stiff.shape, BF),
            pltpu.VMEM(x.shape, BF),
            pltpu.VMEM((nodes, cells * wide), BF),
            pltpu.VMEM((cells * wide, nodes), BF),
            pltpu.VMEM((wide, wide), BF),
            pltpu.VMEM((8, wide), F32),
            pltpu.VMEM((8, wide), jnp.int32),
            pltpu.SemaphoreType.DMA((7,)),
        ],
        compiler_params=pltpu.CompilerParams(vmem_limit_bytes=40 << 20),
        cost_estimate=pl.CostEstimate(flops=5_000_000_000, bytes_accessed=5_000_000, transcendentals=0),
        name="build",
    )(counts, *(pltpu.with_memory_space_constraint(v, pltpu.HBM) for v in (scale, conn, pot, shared, stiff, x)))


def step_kernel(spots, factor, last, matrix_ref, diagonal_ref, rest_ref, before_ref, *refs):
    count = len(spots)
    received = refs[:count]
    outs = refs[count:]
    field_ref, outs = (outs[-1], outs[:-1]) if last else (outs[0], outs[1:])
    field_ref[...] = rest_ref[...]
    for got, at in zip(received, spots):
        field_ref[:, at:at + LANE] += factor * got[...].astype(F32)
    field = field_ref[...]
    applied = apply_operator(field, matrix_ref, diagonal_ref)
    outs[0][...] = applied - field - before_ref[...]
    for send, at in zip(outs[1:], spots):
        send[...] = applied[:, at:at + LANE].astype(BF)


def step(spots, factor, last, matrix, diagonal, rest, before, received):
    rows, nodes = rest.shape
    field = jax.ShapeDtypeStruct((rows, nodes), F32)
    outs = (field,) * (1 if last else 2) + (jax.ShapeDtypeStruct((rows, LANE), BF),) * len(spots)
    return pl.pallas_call(
        functools.partial(step_kernel, spots, factor, last),
        out_shape=outs,
        in_specs=[VMEM] * (4 + len(spots)),
        out_specs=(VMEM,) * len(outs),
        scratch_shapes=[pltpu.VMEM((rows, nodes), F32)] if last else [],
        compiler_params=pltpu.CompilerParams(vmem_limit_bytes=16 << 20),
        cost_estimate=pl.CostEstimate(flops=110_000_000, bytes_accessed=3_000_000, transcendentals=0),
        name="step",
    )(matrix, diagonal, rest, before, *received)


def finish_kernel(spots, rest_ref, *refs):
    received, out_ref = refs[:-1], refs[-1]
    out_ref[...] = rest_ref[...].astype(BF)
    for got, at in zip(received, spots):
        out_ref[:, at:at + LANE] = (rest_ref[:, at:at + LANE] + got[...].astype(F32)).astype(BF)


def finish(spots, rest, received):
    return pl.pallas_call(
        functools.partial(finish_kernel, spots),
        out_shape=jax.ShapeDtypeStruct(rest.shape, BF),
        in_specs=[VMEM] * (1 + len(spots)),
        out_specs=VMEM,
        compiler_params=pltpu.CompilerParams(vmem_limit_bytes=8 << 20),
        name="finish",
    )(rest, *received)


def owner_row(nodes, place_x, place_y):
    lane = iota((1, nodes), 1)
    hidden = ((lane < LANE) & (place_x > 0)) | ((lane >= 2 * LANE) & (lane < 3 * LANE) & (place_y > 0))
    return jnp.where(hidden, 0.0, 1.0)


def products_kernel(hops, own_ref, side_ref, mine_ref, other_ref, *refs):
    zs = len(hops) + 1
    columns = refs[:zs - 1]
    rot_ref, turn_ref, keep_ref, give_ref, fields, pair, coef = refs[zs - 1:]
    width, nodes = own_ref.shape
    at = lax.axis_index("band")
    z, x = at // 2, at % 2
    fields[:, 1 - x] = jnp.zeros((zs, width, nodes), BF)
    fields[z, x] = own_ref[...]
    for k, column in zip(hops, columns):
        fields[z ^ k, x] = column[...]
    coef[:width] = mine_ref[...]
    coef[width:] = other_ref[...]
    turned = mm(coef[...], fields[...].reshape(zs * 2 * width, nodes))
    rot_ref[...] = turned[:width]
    turn_ref[...] = turned[width:].astype(BF)
    owner = owner_row(nodes, lax.axis_index("dx"), lax.axis_index("dy"))
    pair[:width] = (own_ref[...].astype(F32) * owner).astype(BF)
    pair[width:] = (side_ref[...].astype(F32) * owner).astype(BF)
    p = lax.axis_index("dx") * 2 + lax.axis_index("dy")
    for j, ref in enumerate((keep_ref, keep_ref, give_ref, give_ref)):
        ref[j % 2] = mm_nt(fields[p ^ j, x], pair[...])


def products(hops, own, side, mine, other, columns):
    width, nodes = own.shape
    zs = len(hops) + 1
    f = lambda *s: jax.ShapeDtypeStruct(s, F32)
    outs = (f(width, nodes), jax.ShapeDtypeStruct((width, nodes), BF),
            f(2, width, 2 * width), f(2, width, 2 * width))
    return pl.pallas_call(
        functools.partial(products_kernel, hops),
        out_shape=outs,
        in_specs=[VMEM] * (4 + len(columns)),
        out_specs=(VMEM,) * 4,
        scratch_shapes=[
            pltpu.VMEM((zs, 2, width, nodes), BF),
            pltpu.VMEM((2 * width, nodes), BF),
            pltpu.VMEM((2 * width, zs * 2 * width), BF),
        ],
        compiler_params=pltpu.CompilerParams(vmem_limit_bytes=16 << 20),
        cost_estimate=pl.CostEstimate(flops=200_000_000, bytes_accessed=2_000_000, transcendentals=0),
        name="products",
    )(own, side, mine, other, *columns)


def rotated_kernel(mine_ref, got_ref, perm_ref, out_ref):
    total = (mine_ref[...] + got_ref[...].astype(F32)).astype(BF)
    out_ref[...] = mm_nt(total, perm_ref[...]).astype(BF)


def rotated_of(mine, got, perm):
    return pl.pallas_call(
        rotated_kernel,
        out_shape=jax.ShapeDtypeStruct(mine.shape, BF),
        in_specs=[VMEM] * 3,
        out_specs=VMEM,
        compiler_params=pltpu.CompilerParams(vmem_limit_bytes=16 << 20),
        cost_estimate=pl.CostEstimate(flops=110_000_000, bytes_accessed=3_000_000, transcendentals=0),
        name="rotated",
    )(mine, got, perm)


def margin_kernel(owned, own_ref, corner_ref, side_ref, below_ref, out_ref):
    width = own_ref.shape[0]
    x = lax.axis_index("band") % 2
    here = (own_ref[...] + below_ref[...].astype(F32)).T[:width] * (1.0 / owned)
    there = (side_ref[...].astype(F32) + corner_ref[...].astype(F32)).T[width:] * (1.0 / owned)
    out_ref[:, :width] = jnp.where(x == 0, here, there)
    out_ref[:, width:] = jnp.where(x == 0, there, here)


def margin_of(owned, *parts):
    width = parts[0].shape[0]
    return pl.pallas_call(
        functools.partial(margin_kernel, owned),
        out_shape=jax.ShapeDtypeStruct((width, 2 * width), F32),
        in_specs=[VMEM] * len(parts),
        out_specs=VMEM,
        compiler_params=pltpu.CompilerParams(vmem_limit_bytes=8 << 20),
        name="margin",
    )(*parts)


def swap(value, axis):
    return lax.ppermute(value, axis, [(0, 1), (1, 0)])


def split3(value):
    high = value.astype(BF).astype(F32)
    middle = (value - high).astype(BF).astype(F32)
    return high, middle, value - high - middle


def advance_kernel(first, matrix_ref, diagonal_ref, applied_ref, field_ref, *refs):
    before_ref = None if first else refs[0]
    got_ref, next_ref, product_ref, to_x_ref, to_y_ref = refs[0 if first else 1:]
    rows = field_ref.shape[0]
    if first:
        next_ref[...] = 0.5 * (applied_ref[...] - field_ref[...])
        next_ref[:, FX:FX + LANE] += 0.5 * got_ref[:rows, :].astype(F32)
    else:
        next_ref[...] = applied_ref[...] - field_ref[...] - before_ref[...]
        next_ref[:, FX:FX + LANE] += got_ref[:rows, :].astype(F32)
    product = apply_operator(next_ref[...], matrix_ref, diagonal_ref)
    product_ref[...] = product
    to_x_ref[...] = product[:, FX:FX + LANE].astype(BF)
    to_y_ref[:rows, :] = applied_ref[:, FY:FY + LANE].astype(BF)
    to_y_ref[rows:2 * rows, :] = product[:, FY:FY + LANE].astype(BF)
    to_y_ref[2 * rows:3 * rows, :] = got_ref[rows:2 * rows, :]
    if first:
        to_y_ref[3 * rows:3 * rows + LANE, :] = matrix_ref[FY:FY + LANE, FY:FY + LANE]
        high, middle, low = split3(diagonal_ref[0:1, FY:FY + LANE])
        row = iota((SPLIT, LANE), 0)
        to_y_ref[3 * rows + LANE:, :] = jnp.where(
            row == 0, high, jnp.where(row == 1, middle, jnp.where(row == 2, low, 0.0))
        ).astype(BF)


def advance(matrix, diagonal, applied, field, before, got):
    first = before is None
    rows, nodes = field.shape
    f = jax.ShapeDtypeStruct((rows, nodes), F32)
    down = 3 * rows + (LANE + SPLIT if first else 0)
    args = (matrix, diagonal, applied, field) + (() if first else (before,)) + (got,)
    return pl.pallas_call(
        functools.partial(advance_kernel, first),
        out_shape=(f, f, jax.ShapeDtypeStruct((rows, LANE), BF), jax.ShapeDtypeStruct((down, LANE), BF)),
        in_specs=[VMEM] * len(args),
        out_specs=(VMEM,) * 4,
        compiler_params=pltpu.CompilerParams(vmem_limit_bytes=16 << 20),
        cost_estimate=pl.CostEstimate(flops=110_000_000, bytes_accessed=3_000_000, transcendentals=0),
        name="advance",
    )(*args)


def correct_kernel(
    first, matrix_ref, diagonal_ref, applied_ref, field_ref, next_ref, product_ref,
    from_x_ref, from_y_ref, block_x_ref, block_y_ref, *outs,
):
    rows = field_ref.shape[0]
    scale = 0.5 if first else 1.0
    total_ref = outs[-1]
    given = scale * from_y_ref[:rows, :].astype(F32)
    sent = scale * applied_ref[:, FY:FY + LANE].astype(BF).astype(F32)
    corner = scale * from_y_ref[2 * rows:3 * rows, :].astype(F32)
    tail = block_y_ref[3 * rows + LANE:3 * rows + LANE + 8, :].astype(F32)
    their_diagonal = tail[0:1] + tail[1:2] + tail[2:3]
    their_y = (
        from_y_ref[rows:2 * rows, :].astype(F32)
        + mm(sent.astype(BF), block_y_ref[3 * rows:3 * rows + LANE, :])
        + sent * their_diagonal
    )
    their_x = from_x_ref[...].astype(F32) + mm(corner.astype(BF), block_x_ref[2 * rows:2 * rows + LANE, :])
    total_ref[...] = (
        product_ref[...] + mm(given.astype(BF), matrix_ref[FY:FY + LANE, :])
        - next_ref[...] - field_ref[...]
    )
    total_ref[:, FX:FX + LANE] += their_x
    total_ref[:, FY:FY + LANE] += their_y + given * (diagonal_ref[0:1, FY:FY + LANE] - 1.0)
    if first:
        middle_ref, second_ref, again_ref, pack_ref = outs[:-1]
        middle_ref[...] = next_ref[...]
        middle_ref[:, FY:FY + LANE] += given
        second = total_ref[...]
        second_ref[...] = second
        applied = apply_operator(second, matrix_ref, diagonal_ref)
        again_ref[...] = applied
        pack_faces(pack_ref, applied)
    else:
        outs[0][...] = total_ref[...].astype(BF)


def correct(first, matrix, diagonal, applied, field, ahead, product, from_x, from_y, block_x, block_y):
    rows, nodes = field.shape
    f = jax.ShapeDtypeStruct((rows, nodes), F32)
    outs = (f, f, f, jax.ShapeDtypeStruct((2 * rows, LANE), BF)) if first else (jax.ShapeDtypeStruct((rows, nodes), BF),)
    return pl.pallas_call(
        functools.partial(correct_kernel, first),
        out_shape=outs,
        in_specs=[VMEM] * 10,
        out_specs=(VMEM,) * len(outs),
        scratch_shapes=[pltpu.VMEM((rows, nodes), F32)],
        compiler_params=pltpu.CompilerParams(vmem_limit_bytes=16 << 20),
        cost_estimate=pl.CostEstimate(flops=150_000_000, bytes_accessed=3_000_000, transcendentals=0),
        name="correct",
    )(matrix, diagonal, applied, field, ahead, product, from_x, from_y, block_x, block_y)


def filter_pairs(matrix, diagonal, field, applied, pack):
    block_x = got = swap(pack, "dx")
    ahead, product, to_x, to_y = advance(matrix, diagonal, applied, field, None, got)
    block_y = swap(to_y, "dy")
    field, second, applied, pack = correct(
        True, matrix, diagonal, applied, field, ahead, product, swap(to_x, "dx"), block_y, block_x, block_y
    )
    got = swap(pack, "dx")
    ahead, product, to_x, to_y = advance(matrix, diagonal, applied, second, field, got)
    return correct(
        False, matrix, diagonal, applied, second, ahead, product, swap(to_x, "dx"), swap(to_y, "dy"), block_x, block_y
    )[0]


def from_behind(block, axis, distance):
    devices = range(lax.axis_size(axis))
    route = [(i - distance, i) for i in devices if i - distance in devices]
    return lax.ppermute(block, axis, route)


def on_device(waves, stiff, cell_scale, cell_pot, conn, counts, shared, rotation):
    width, nodes = waves.shape[0], waves.shape[3]
    cells, degree_nodes = conn.shape[2:]
    share = shared.shape[3]
    count_x, count_y = lax.axis_size("dx"), lax.axis_size("dy")
    bands = lax.axis_size("band")
    owned = nodes * count_x * count_y - share * (2 * count_x * count_y - count_x - count_y)
    paired = count_x == 2 and count_y == 2 and bands == 2 * count_x * count_y
    x = waves.reshape(width, nodes)
    spots = (0, LANE, 2 * LANE, 3 * LANE)

    def exchange(sends):
        return (
            from_behind(sends[1], "dx", 1), from_behind(sends[0], "dx", -1),
            from_behind(sends[3], "dy", 1), from_behind(sends[2], "dy", -1),
        )

    matrix, diagonal, perm, before, rest, *sends = build(
        spots, paired, counts, cell_scale.reshape(1, cells),
        conn.reshape(cells, degree_nodes), cell_pot.reshape(cells, degree_nodes),
        shared.reshape(4, share), stiff, x,
    )
    if paired:
        filtered = filter_pairs(matrix, diagonal, before, rest, sends[0])
    else:
        for degree_step in range(DEGREE - 1):
            factor = 0.5 if degree_step == 0 else 1.0
            received = exchange(sends)
            if degree_step < DEGREE - 2:
                field, rest, *sends = step(spots, factor, False, matrix, diagonal, rest, before, received)
                before = field
            else:
                rest, *sends = step(spots, factor, True, matrix, diagonal, rest, before, received)
        filtered = finish(spots, rest, exchange(sends))

    if paired:
        across = [(i, i ^ 1) for i in range(bands)]
        other = lax.ppermute(rotation, "band", across)
        hops = (3, 1, 2)
        routes = [[(i, i ^ (2 * k)) for i in range(bands)] for k in hops]
        columns = [lax.ppermute(filtered, "band", route) for route in routes[:2]]
        side = lax.ppermute(filtered, "band", across)
        columns.append(lax.ppermute(filtered, "band", routes[2]))
        mine, turn, keep, give = products(hops, filtered, side, rotation, other, columns)
        got = lax.ppermute(turn, "band", across)
        corner = [
            (2 * i + j, 2 * (i ^ 1) + (j ^ 1)) for i in range(bands) for j in range(count_y)
        ]
        half = keep + swap(give, "dx")
        own, below = half[0], half[1].astype(BF)
        aside, away = own.astype(BF), below
        rotated = rotated_of(mine, got, perm)
        below = swap(below, "dy")
        aside = lax.ppermute(aside, "band", across)
        away = lax.ppermute(away, ("band", "dy"), corner)
        own, rotated = lax.optimization_barrier((own, rotated))
        margin = margin_of(owned, own, away, aside, below)
    else:
        gathered = lax.all_gather(filtered, "band", axis=0, tiled=True)
        owner = owner_row(nodes, lax.axis_index("dx"), lax.axis_index("dy")).astype(BF)
        block = mm_nt(filtered * owner, gathered)
        block = lax.psum_scatter(block, ("dx", "dy"), scatter_dimension=1, tiled=True)
        margin = block * (1.0 / owned)
        rotated = mm_nt(mm(rotation, gathered).astype(BF), perm).astype(BF)
    return margin, rotated.reshape(width, 1, 1, nodes)


def solution(mesh):
    return jax.shard_map(
        on_device,
        mesh=mesh,
        in_specs=(
            P("band", "dx", "dy", None),
            P(),
            P("dx", "dy", None),
            P("dx", "dy", None, None),
            P("dx", "dy", None, None),
            P("dx", "dy"),
            P("dx", "dy", None, None),
            P("band", None),
        ),
        out_specs=(P("band", ("dx", "dy")), P("band", "dx", "dy", None)),
        check_vma=False,
    )
```

```python
import functools

import jax
import jax.numpy as jnp
from jax import lax
from jax.experimental import pallas as pl
from jax.experimental.pallas import tpu as pltpu
from jax.sharding import PartitionSpec as P

DEGREE = 4
LANE = 128
SHIFT_CENTER = 3.0
HALF_WIDTH = 6.0
BF = jnp.bfloat16
F32 = jnp.float32
NT = (((1,), (1,)), ((), ()))
FACE = 4 * LANE
FX, FY = 0, 2 * LANE
SPLIT = 16

VMEM = pl.BlockSpec(memory_space=pltpu.VMEM)
HBM = pl.BlockSpec(memory_space=pltpu.HBM)


def iota(shape, dim):
    return lax.broadcasted_iota(jnp.int32, shape, dim)


def hot(mask):
    return jnp.where(mask, 1.0, 0.0).astype(BF)


def hot16(mask):
    return jnp.where(mask, jnp.ones((), BF), jnp.zeros((), BF))


def mm(a, b):
    return jnp.dot(a, b, preferred_element_type=F32)


def mm_nt(a, b):
    return lax.dot_general(a, b, NT, preferred_element_type=F32)


def apply_operator(field, matrix_ref, diagonal_ref):
    return mm(field.astype(BF), matrix_ref[...]) + field * diagonal_ref[0:1, :]


def build_kernel(
    spots, paired,
    counts_hbm, scale_hbm, conn_hbm, pot_hbm, shared_hbm, stiff_hbm, x_hbm,
    matrix_ref, diagonal_ref, perm_ref, y0_ref, rest_ref, *outs_and_scratch,
):
    count_out = 1 if paired else len(spots)
    sends = outs_and_scratch[:count_out]
    (count, scale, conn, pot, shared, stiff, x, tcat, vcat, off, table, links, sems) = outs_and_scratch[count_out:]
    copies = [
        pltpu.make_async_copy(src, dst, sems.at[i])
        for i, (src, dst) in enumerate(
            ((counts_hbm, count), (scale_hbm, scale), (shared_hbm, shared), (conn_hbm, conn),
             (pot_hbm, pot), (stiff_hbm, stiff), (x_hbm, x))
        )
    ]
    for copy in copies:
        copy.start()
    cells, degree_nodes = conn.shape
    nodes = x.shape[1]
    wide = off.shape[0]
    off[...] = jnp.zeros_like(off)
    table[...] = jnp.zeros_like(table)
    links[...] = jnp.full(links.shape, -1, jnp.int32)
    copies[2].wait()
    if paired:
        first_x = 1 - lax.axis_index("dx")
        first_y = 1 - lax.axis_index("dy")
        order = (first_x, 1 - first_x, 2 + first_y, 3 - first_y)
    else:
        order = (0, 1, 2, 3)
    node = iota((nodes, LANE), 0)
    lane = iota((nodes, LANE), 1)
    spot = jnp.zeros((nodes, LANE), F32)
    for i in range(4):
        hit = node == shared[pl.ds(order[i], 1), :]
        perm_ref[:, i * LANE:(i + 1) * LANE] = hot(hit)
        spot = spot + jnp.where(hit, (lane + (i * LANE + 1)).astype(F32), 0.0)
    spot = jnp.broadcast_to(jnp.sum(spot, axis=1, keepdims=True), (nodes, LANE))
    on_face = (spot > 0.0).astype(F32)
    inner = (1.0 - on_face).astype(BF)
    below = hot(iota((LANE, LANE), 1) < iota((LANE, LANE), 0))
    ranks = []
    seen = jnp.zeros((1, LANE), F32)
    for j in range(nodes // LANE):
        part = inner[j * LANE:(j + 1) * LANE]
        ranks.append(mm(below, part) + seen)
        seen = seen + jnp.sum(part.astype(F32), axis=0, keepdims=True)
    rank = jnp.concatenate(ranks, axis=0)
    spot = jnp.where(on_face > 0.5, spot, rank + (FACE + 1))
    rank = jnp.where(on_face > 0.5, -1.0, rank).astype(jnp.int32).astype(jnp.int16)
    narrow_lane = lane.astype(jnp.int16)
    for j in range((nodes - FACE) // LANE):
        perm_ref[:, FACE + j * LANE:FACE + (j + 1) * LANE] = hot16(rank == narrow_lane + jnp.int16(j * LANE))
    for i in (0, 1, 3, 4, 5, 6):
        copies[i].wait()
    matrix = stiff[...]
    eye = iota(matrix.shape, 0) == iota(matrix.shape, 1)
    off[:degree_nodes, :degree_nodes] = jnp.where(eye, jnp.zeros_like(matrix), matrix)
    table[cells:cells + 1, :degree_nodes] = jnp.sum(
        jnp.where(eye, matrix.astype(F32), 0.0), axis=0, keepdims=True
    )
    table[:cells, :degree_nodes] = pot[...]
    links[:cells, :degree_nodes] = conn[...]
    y0 = mm(x[...], perm_ref[...])
    wide_node = iota((nodes, wide), 0)
    narrow_node = wide_node.astype(jnp.int16)
    wide_spot = jnp.concatenate([spot] * (wide // LANE), axis=1)
    tail = degree_nodes + (-degree_nodes) % 16
    row = iota((16, wide), 0)
    diagonal = jnp.zeros((1, nodes), F32)
    for c in range(cells):
        share = jnp.where(c < count[0, 0], 2.0 / HALF_WIDTH, 0.0)
        weight = share * scale[0, c]
        link = links[c:c + 1, :]
        found = jnp.sum(jnp.where(wide_node == link, wide_spot, 0.0), axis=0, keepdims=True)
        where = found.astype(jnp.int32) - 1
        select = hot16(narrow_node == where.astype(jnp.int16))
        tcat[:, c * wide:(c + 1) * wide] = select
        value = weight * table[cells:cells + 1, :] + share * table[c:c + 1, :]
        high = value.astype(BF).astype(F32)
        middle = (value - high).astype(BF).astype(F32)
        low = value - high - middle
        off[tail:tail + 16, :] = jnp.where(
            row == 0, high, jnp.where(row == 1, middle, jnp.where(row == 2, low, 0.0))
        ).astype(BF)
        moved = mm_nt(off[...], select)
        diagonal = diagonal + jnp.sum(moved[tail:tail + 16], axis=0, keepdims=True)
        vcat[c * wide:(c + 1) * wide, :] = (moved * weight).astype(BF)
    diagonal_ref[...] = jnp.broadcast_to(diagonal, diagonal_ref.shape)
    for low in range(0, nodes, 2 * LANE):
        high = min(low + 2 * LANE, nodes)
        matrix_ref[low:high, low:] = mm(tcat[low:high, :], vcat[:, low:]).astype(BF)
        if high < nodes:
            matrix_ref[high:, low:high] = matrix_ref[low:high, high:].T
    y0_ref[...] = y0
    applied = apply_operator(y0, matrix_ref, diagonal_ref)
    if paired:
        rows = x.shape[0]
        rest_ref[...] = applied
        pack_faces(sends[0], applied)
        sends[0][2 * rows:, :] = matrix_ref[FY:FY + LANE, FX:FX + LANE]
    else:
        rest_ref[...] = 0.5 * (applied - y0)
        for send, at in zip(sends, spots):
            send[...] = applied[:, at:at + LANE].astype(BF)


def pack_faces(out_ref, applied):
    rows = applied.shape[0]
    out_ref[:rows, :] = applied[:, FX:FX + LANE].astype(BF)
    out_ref[rows:2 * rows, :] = applied[:, FY:FY + LANE].astype(BF)


def build(spots, paired, counts, scale, conn, pot, shared, stiff, x):
    cells, degree_nodes = conn.shape
    rows, nodes = x.shape
    wide = -(-(degree_nodes + 32) // LANE) * LANE
    f = lambda *s: jax.ShapeDtypeStruct(s, F32)
    b = lambda *s: jax.ShapeDtypeStruct(s, BF)
    outs = (b(nodes, nodes), f(8, nodes), b(nodes, nodes), f(rows, nodes), f(rows, nodes))
    outs += (b(2 * rows + LANE, LANE),) if paired else (b(rows, LANE),) * len(spots)
    return pl.pallas_call(
        functools.partial(build_kernel, spots, paired),
        out_shape=outs,
        in_specs=[HBM] * 7,
        out_specs=(VMEM,) * len(outs),
        scratch_shapes=[
            pltpu.SMEM(counts.shape, counts.dtype),
            pltpu.SMEM(scale.shape, F32),
            pltpu.VMEM(conn.shape, jnp.int32),
            pltpu.VMEM(pot.shape, F32),
            pltpu.VMEM(shared.shape, jnp.int32),
            pltpu.VMEM(stiff.shape, BF),
            pltpu.VMEM(x.shape, BF),
            pltpu.VMEM((nodes, cells * wide), BF),
            pltpu.VMEM((cells * wide, nodes), BF),
            pltpu.VMEM((wide, wide), BF),
            pltpu.VMEM((8, wide), F32),
            pltpu.VMEM((8, wide), jnp.int32),
            pltpu.SemaphoreType.DMA((7,)),
        ],
        compiler_params=pltpu.CompilerParams(vmem_limit_bytes=40 << 20),
        cost_estimate=pl.CostEstimate(flops=5_000_000_000, bytes_accessed=5_000_000, transcendentals=0),
        name="build",
    )(counts, *(pltpu.with_memory_space_constraint(v, pltpu.HBM) for v in (scale, conn, pot, shared, stiff, x)))


def step_kernel(spots, factor, last, matrix_ref, diagonal_ref, rest_ref, before_ref, *refs):
    count = len(spots)
    received = refs[:count]
    outs = refs[count:]
    field_ref, outs = (outs[-1], outs[:-1]) if last else (outs[0], outs[1:])
    field_ref[...] = rest_ref[...]
    for got, at in zip(received, spots):
        field_ref[:, at:at + LANE] += factor * got[...].astype(F32)
    field = field_ref[...]
    applied = apply_operator(field, matrix_ref, diagonal_ref)
    outs[0][...] = applied - field - before_ref[...]
    for send, at in zip(outs[1:], spots):
        send[...] = applied[:, at:at + LANE].astype(BF)


def step(spots, factor, last, matrix, diagonal, rest, before, received):
    rows, nodes = rest.shape
    field = jax.ShapeDtypeStruct((rows, nodes), F32)
    outs = (field,) * (1 if last else 2) + (jax.ShapeDtypeStruct((rows, LANE), BF),) * len(spots)
    return pl.pallas_call(
        functools.partial(step_kernel, spots, factor, last),
        out_shape=outs,
        in_specs=[VMEM] * (4 + len(spots)),
        out_specs=(VMEM,) * len(outs),
        scratch_shapes=[pltpu.VMEM((rows, nodes), F32)] if last else [],
        compiler_params=pltpu.CompilerParams(vmem_limit_bytes=16 << 20),
        cost_estimate=pl.CostEstimate(flops=110_000_000, bytes_accessed=3_000_000, transcendentals=0),
        name="step",
    )(matrix, diagonal, rest, before, *received)


def finish_kernel(spots, rest_ref, *refs):
    received, out_ref = refs[:-1], refs[-1]
    out_ref[...] = rest_ref[...].astype(BF)
    for got, at in zip(received, spots):
        out_ref[:, at:at + LANE] = (rest_ref[:, at:at + LANE] + got[...].astype(F32)).astype(BF)


def finish(spots, rest, received):
    return pl.pallas_call(
        functools.partial(finish_kernel, spots),
        out_shape=jax.ShapeDtypeStruct(rest.shape, BF),
        in_specs=[VMEM] * (1 + len(spots)),
        out_specs=VMEM,
        compiler_params=pltpu.CompilerParams(vmem_limit_bytes=8 << 20),
        name="finish",
    )(rest, *received)


def owner_row(nodes, place_x, place_y):
    lane = iota((1, nodes), 1)
    hidden = ((lane < LANE) & (place_x > 0)) | ((lane >= 2 * LANE) & (lane < 3 * LANE) & (place_y > 0))
    return jnp.where(hidden, 0.0, 1.0)


def products_kernel(hops, own_ref, side_ref, mine_ref, other_ref, *refs):
    zs = len(hops) + 1
    columns = refs[:zs - 1]
    rot_ref, turn_ref, keep_ref, give_ref, fields, pair, coef = refs[zs - 1:]
    width, nodes = own_ref.shape
    at = lax.axis_index("band")
    z, x = at // 2, at % 2
    fields[:, 1 - x] = jnp.zeros((zs, width, nodes), BF)
    fields[z, x] = own_ref[...]
    for k, column in zip(hops, columns):
        fields[z ^ k, x] = column[...]
    coef[:width] = mine_ref[...]
    coef[width:] = other_ref[...]
    turned = mm(coef[...], fields[...].reshape(zs * 2 * width, nodes))
    rot_ref[...] = turned[:width]
    turn_ref[...] = turned[width:].astype(BF)
    owner = owner_row(nodes, lax.axis_index("dx"), lax.axis_index("dy"))
    pair[:width] = (own_ref[...].astype(F32) * owner).astype(BF)
    pair[width:] = (side_ref[...].astype(F32) * owner).astype(BF)
    p = lax.axis_index("dx") * 2 + lax.axis_index("dy")
    for j, ref in enumerate((keep_ref, keep_ref, give_ref, give_ref)):
        ref[j % 2] = mm_nt(fields[p ^ j, x], pair[...])


def products(hops, own, side, mine, other, columns):
    width, nodes = own.shape
    zs = len(hops) + 1
    f = lambda *s: jax.ShapeDtypeStruct(s, F32)
    outs = (f(width, nodes), jax.ShapeDtypeStruct((width, nodes), BF),
            f(2, width, 2 * width), f(2, width, 2 * width))
    return pl.pallas_call(
        functools.partial(products_kernel, hops),
        out_shape=outs,
        in_specs=[VMEM] * (4 + len(columns)),
        out_specs=(VMEM,) * 4,
        scratch_shapes=[
            pltpu.VMEM((zs, 2, width, nodes), BF),
            pltpu.VMEM((2 * width, nodes), BF),
            pltpu.VMEM((2 * width, zs * 2 * width), BF),
        ],
        compiler_params=pltpu.CompilerParams(vmem_limit_bytes=16 << 20),
        cost_estimate=pl.CostEstimate(flops=200_000_000, bytes_accessed=2_000_000, transcendentals=0),
        name="products",
    )(own, side, mine, other, *columns)


def rotated_kernel(mine_ref, got_ref, perm_ref, out_ref):
    total = (mine_ref[...] + got_ref[...].astype(F32)).astype(BF)
    out_ref[...] = mm_nt(total, perm_ref[...]).astype(BF)


def rotated_of(mine, got, perm):
    return pl.pallas_call(
        rotated_kernel,
        out_shape=jax.ShapeDtypeStruct(mine.shape, BF),
        in_specs=[VMEM] * 3,
        out_specs=VMEM,
        compiler_params=pltpu.CompilerParams(vmem_limit_bytes=16 << 20),
        cost_estimate=pl.CostEstimate(flops=110_000_000, bytes_accessed=3_000_000, transcendentals=0),
        name="rotated",
    )(mine, got, perm)


def margin_kernel(owned, own_ref, corner_ref, side_ref, below_ref, out_ref):
    width = own_ref.shape[0]
    x = lax.axis_index("band") % 2
    here = (own_ref[...] + below_ref[...].astype(F32)).T[:width] * (1.0 / owned)
    there = (side_ref[...].astype(F32) + corner_ref[...].astype(F32)).T[width:] * (1.0 / owned)
    out_ref[:, :width] = jnp.where(x == 0, here, there)
    out_ref[:, width:] = jnp.where(x == 0, there, here)


def margin_of(owned, *parts):
    width = parts[0].shape[0]
    return pl.pallas_call(
        functools.partial(margin_kernel, owned),
        out_shape=jax.ShapeDtypeStruct((width, 2 * width), F32),
        in_specs=[VMEM] * len(parts),
        out_specs=VMEM,
        compiler_params=pltpu.CompilerParams(vmem_limit_bytes=8 << 20),
        name="margin",
    )(*parts)


def swap(value, axis):
    return lax.ppermute(value, axis, [(0, 1), (1, 0)])


def split3(value):
    high = value.astype(BF).astype(F32)
    middle = (value - high).astype(BF).astype(F32)
    return high, middle, value - high - middle


def advance_kernel(first, matrix_ref, diagonal_ref, applied_ref, field_ref, *refs):
    before_ref = None if first else refs[0]
    got_ref, next_ref, product_ref, to_x_ref, to_y_ref = refs[0 if first else 1:]
    rows = field_ref.shape[0]
    if first:
        next_ref[...] = 0.5 * (applied_ref[...] - field_ref[...])
        next_ref[:, FX:FX + LANE] += 0.5 * got_ref[:rows, :].astype(F32)
    else:
        next_ref[...] = applied_ref[...] - field_ref[...] - before_ref[...]
        next_ref[:, FX:FX + LANE] += got_ref[:rows, :].astype(F32)
    product = apply_operator(next_ref[...], matrix_ref, diagonal_ref)
    product_ref[...] = product
    to_x_ref[...] = product[:, FX:FX + LANE].astype(BF)
    to_y_ref[:rows, :] = applied_ref[:, FY:FY + LANE].astype(BF)
    to_y_ref[rows:2 * rows, :] = product[:, FY:FY + LANE].astype(BF)
    to_y_ref[2 * rows:3 * rows, :] = got_ref[rows:2 * rows, :]
    if first:
        to_y_ref[3 * rows:3 * rows + LANE, :] = matrix_ref[FY:FY + LANE, FY:FY + LANE]
        high, middle, low = split3(diagonal_ref[0:1, FY:FY + LANE])
        row = iota((SPLIT, LANE), 0)
        to_y_ref[3 * rows + LANE:, :] = jnp.where(
            row == 0, high, jnp.where(row == 1, middle, jnp.where(row == 2, low, 0.0))
        ).astype(BF)


def advance(matrix, diagonal, applied, field, before, got):
    first = before is None
    rows, nodes = field.shape
    f = jax.ShapeDtypeStruct((rows, nodes), F32)
    down = 3 * rows + (LANE + SPLIT if first else 0)
    args = (matrix, diagonal, applied, field) + (() if first else (before,)) + (got,)
    return pl.pallas_call(
        functools.partial(advance_kernel, first),
        out_shape=(f, f, jax.ShapeDtypeStruct((rows, LANE), BF), jax.ShapeDtypeStruct((down, LANE), BF)),
        in_specs=[VMEM] * len(args),
        out_specs=(VMEM,) * 4,
        compiler_params=pltpu.CompilerParams(vmem_limit_bytes=16 << 20),
        cost_estimate=pl.CostEstimate(flops=110_000_000, bytes_accessed=3_000_000, transcendentals=0),
        name="advance",
    )(*args)


def correct_kernel(
    first, matrix_ref, diagonal_ref, applied_ref, field_ref, next_ref, product_ref,
    from_x_ref, from_y_ref, block_x_ref, block_y_ref, *outs,
):
    rows = field_ref.shape[0]
    scale = 0.5 if first else 1.0
    total_ref = outs[-1]
    given = scale * from_y_ref[:rows, :].astype(F32)
    sent = scale * applied_ref[:, FY:FY + LANE].astype(BF).astype(F32)
    corner = scale * from_y_ref[2 * rows:3 * rows, :].astype(F32)
    tail = block_y_ref[3 * rows + LANE:3 * rows + LANE + SPLIT, :].astype(F32)
    their_diagonal = tail[0:1] + tail[1:2] + tail[2:3]
    their_y = (
        from_y_ref[rows:2 * rows, :].astype(F32)
        + mm(sent.astype(BF), block_y_ref[3 * rows:3 * rows + LANE, :])
        + sent * their_diagonal
    )
    their_x = from_x_ref[...].astype(F32) + mm(corner.astype(BF), block_x_ref[2 * rows:2 * rows + LANE, :])
    total_ref[...] = (
        product_ref[...] + mm(given.astype(BF), matrix_ref[FY:FY + LANE, :])
        - next_ref[...] - field_ref[...]
    )
    total_ref[:, FX:FX + LANE] += their_x
    total_ref[:, FY:FY + LANE] += their_y + given * (diagonal_ref[0:1, FY:FY + LANE] - 1.0)
    if first:
        middle_ref, second_ref, again_ref, pack_ref = outs[:-1]
        middle_ref[...] = next_ref[...]
        middle_ref[:, FY:FY + LANE] += given
        second = total_ref[...]
        second_ref[...] = second
        applied = apply_operator(second, matrix_ref, diagonal_ref)
        again_ref[...] = applied
        pack_faces(pack_ref, applied)
    else:
        outs[0][...] = total_ref[...].astype(BF)


def correct(first, matrix, diagonal, applied, field, ahead, product, from_x, from_y, block_x, block_y):
    rows, nodes = field.shape
    f = jax.ShapeDtypeStruct((rows, nodes), F32)
    outs = (f, f, f, jax.ShapeDtypeStruct((2 * rows, LANE), BF)) if first else (jax.ShapeDtypeStruct((rows, nodes), BF),)
    return pl.pallas_call(
        functools.partial(correct_kernel, first),
        out_shape=outs,
        in_specs=[VMEM] * 10,
        out_specs=(VMEM,) * len(outs),
        scratch_shapes=[pltpu.VMEM((rows, nodes), F32)],
        compiler_params=pltpu.CompilerParams(vmem_limit_bytes=16 << 20),
        cost_estimate=pl.CostEstimate(flops=150_000_000, bytes_accessed=3_000_000, transcendentals=0),
        name="correct",
    )(matrix, diagonal, applied, field, ahead, product, from_x, from_y, block_x, block_y)


def filter_pairs(matrix, diagonal, field, applied, pack):
    block_x = got = swap(pack, "dx")
    ahead, product, to_x, to_y = advance(matrix, diagonal, applied, field, None, got)
    block_y = swap(to_y, "dy")
    field, second, applied, pack = correct(
        True, matrix, diagonal, applied, field, ahead, product, swap(to_x, "dx"), block_y, block_x, block_y
    )
    got = swap(pack, "dx")
    ahead, product, to_x, to_y = advance(matrix, diagonal, applied, second, field, got)
    return correct(
        False, matrix, diagonal, applied, second, ahead, product, swap(to_x, "dx"), swap(to_y, "dy"), block_x, block_y
    )[0]


def from_behind(block, axis, distance):
    devices = range(lax.axis_size(axis))
    route = [(i - distance, i) for i in devices if i - distance in devices]
    return lax.ppermute(block, axis, route)


def on_device(waves, stiff, cell_scale, cell_pot, conn, counts, shared, rotation):
    width, nodes = waves.shape[0], waves.shape[3]
    cells, degree_nodes = conn.shape[2:]
    share = shared.shape[3]
    count_x, count_y = lax.axis_size("dx"), lax.axis_size("dy")
    bands = lax.axis_size("band")
    owned = nodes * count_x * count_y - share * (2 * count_x * count_y - count_x - count_y)
    paired = count_x == 2 and count_y == 2 and bands == 2 * count_x * count_y
    x = waves.reshape(width, nodes)
    spots = (0, LANE, 2 * LANE, 3 * LANE)

    def exchange(sends):
        return (
            from_behind(sends[1], "dx", 1), from_behind(sends[0], "dx", -1),
            from_behind(sends[3], "dy", 1), from_behind(sends[2], "dy", -1),
        )

    matrix, diagonal, perm, before, rest, *sends = build(
        spots, paired, counts, cell_scale.reshape(1, cells),
        conn.reshape(cells, degree_nodes), cell_pot.reshape(cells, degree_nodes),
        shared.reshape(4, share), stiff, x,
    )
    if paired:
        filtered = filter_pairs(matrix, diagonal, before, rest, sends[0])
    else:
        for degree_step in range(DEGREE - 1):
            factor = 0.5 if degree_step == 0 else 1.0
            received = exchange(sends)
            if degree_step < DEGREE - 2:
                field, rest, *sends = step(spots, factor, False, matrix, diagonal, rest, before, received)
                before = field
            else:
                rest, *sends = step(spots, factor, True, matrix, diagonal, rest, before, received)
        filtered = finish(spots, rest, exchange(sends))

    if paired:
        across = [(i, i ^ 1) for i in range(bands)]
        other = lax.ppermute(rotation, "band", across)
        hops = (3, 1, 2)
        routes = [[(i, i ^ (2 * k)) for i in range(bands)] for k in hops]
        columns = [lax.ppermute(filtered, "band", route) for route in routes[:2]]
        side = lax.ppermute(filtered, "band", across)
        columns.append(lax.ppermute(filtered, "band", routes[2]))
        mine, turn, keep, give = products(hops, filtered, side, rotation, other, columns)
        got = lax.ppermute(turn, "band", across)
        corner = [
            (2 * i + j, 2 * (i ^ 1) + (j ^ 1)) for i in range(bands) for j in range(count_y)
        ]
        half = keep + swap(give, "dx")
        own, below = half[0], half[1].astype(BF)
        aside, away = own.astype(BF), below
        rotated = rotated_of(mine, got, perm)
        below = swap(below, "dy")
        aside = lax.ppermute(aside, "band", across)
        away = lax.ppermute(away, ("band", "dy"), corner)
        own, rotated = lax.optimization_barrier((own, rotated))
        margin = margin_of(owned, own, away, aside, below)
    else:
        gathered = lax.all_gather(filtered, "band", axis=0, tiled=True)
        owner = owner_row(nodes, lax.axis_index("dx"), lax.axis_index("dy")).astype(BF)
        block = mm_nt(filtered * owner, gathered)
        block = lax.psum_scatter(block, ("dx", "dy"), scatter_dimension=1, tiled=True)
        margin = block * (1.0 / owned)
        rotated = mm_nt(mm(rotation, gathered).astype(BF), perm).astype(BF)
    return margin, rotated.reshape(width, 1, 1, nodes)


def solution(mesh):
    return jax.shard_map(
        on_device,
        mesh=mesh,
        in_specs=(
            P("band", "dx", "dy", None),
            P(),
            P("dx", "dy", None),
            P("dx", "dy", None, None),
            P("dx", "dy", None, None),
            P("dx", "dy"),
            P("dx", "dy", None, None),
            P("band", None),
        ),
        out_specs=(P("band", ("dx", "dy")), P("band", "dx", "dy", None)),
        check_vma=False,
    )
```

```python
import functools

import jax
import jax.numpy as jnp
from jax import lax
from jax.experimental import pallas as pl
from jax.experimental.pallas import tpu as pltpu
from jax.sharding import PartitionSpec as P

DEGREE = 4
LANE = 128
SHIFT_CENTER = 3.0
HALF_WIDTH = 6.0
BF = jnp.bfloat16
F32 = jnp.float32
NT = (((1,), (1,)), ((), ()))
FACE = 4 * LANE
FX, FY = 0, 2 * LANE
SPLIT = 16

VMEM = pl.BlockSpec(memory_space=pltpu.VMEM)
HBM = pl.BlockSpec(memory_space=pltpu.HBM)


def iota(shape, dim):
    return lax.broadcasted_iota(jnp.int32, shape, dim)


def hot(mask):
    return jnp.where(mask, 1.0, 0.0).astype(BF)


def hot16(mask):
    return jnp.where(mask, jnp.ones((), BF), jnp.zeros((), BF))


def mm(a, b):
    return jnp.dot(a, b, preferred_element_type=F32)


def mm_nt(a, b):
    return lax.dot_general(a, b, NT, preferred_element_type=F32)


def apply_operator(field, matrix_ref, diagonal_ref):
    return mm(field.astype(BF), matrix_ref[...]) + field * diagonal_ref[0:1, :]


def build_kernel(
    spots, paired,
    counts_hbm, scale_hbm, conn_hbm, pot_hbm, shared_hbm, stiff_hbm, x_hbm,
    matrix_ref, diagonal_ref, perm_ref, y0_ref, rest_ref, *outs_and_scratch,
):
    count_out = 1 if paired else len(spots)
    sends = outs_and_scratch[:count_out]
    (count, scale, conn, pot, shared, stiff, x, tcat, vcat, off, cell, table, links, sems) = outs_and_scratch[count_out:]
    copies = [
        pltpu.make_async_copy(src, dst, sems.at[i])
        for i, (src, dst) in enumerate(
            ((counts_hbm, count), (scale_hbm, scale), (shared_hbm, shared), (conn_hbm, conn),
             (pot_hbm, pot), (stiff_hbm, stiff), (x_hbm, x))
        )
    ]
    for copy in copies:
        copy.start()
    cells, degree_nodes = conn.shape
    nodes = x.shape[1]
    wide = off.shape[0]
    cell[...] = jnp.zeros_like(cell)
    table[...] = jnp.zeros_like(table)
    links[...] = jnp.full(links.shape, -1, jnp.int32)
    copies[2].wait()
    if paired:
        first_x = 1 - lax.axis_index("dx")
        first_y = 1 - lax.axis_index("dy")
        order = (first_x, 1 - first_x, 2 + first_y, 3 - first_y)
    else:
        order = (0, 1, 2, 3)
    node = iota((nodes, LANE), 0)
    lane = iota((nodes, LANE), 1)
    spot = jnp.zeros((nodes, LANE), F32)
    for i in range(4):
        hit = node == shared[pl.ds(order[i], 1), :]
        perm_ref[:, i * LANE:(i + 1) * LANE] = hot(hit)
        spot = spot + jnp.where(hit, (lane + (i * LANE + 1)).astype(F32), 0.0)
    spot = jnp.broadcast_to(jnp.sum(spot, axis=1, keepdims=True), (nodes, LANE))
    on_face = (spot > 0.0).astype(F32)
    inner = (1.0 - on_face).astype(BF)
    below = hot(iota((LANE, LANE), 1) < iota((LANE, LANE), 0))
    ranks = []
    seen = jnp.zeros((1, LANE), F32)
    for j in range(nodes // LANE):
        part = inner[j * LANE:(j + 1) * LANE]
        ranks.append(mm(below, part) + seen)
        seen = seen + jnp.sum(part.astype(F32), axis=0, keepdims=True)
    rank = jnp.concatenate(ranks, axis=0)
    spot = jnp.where(on_face > 0.5, spot, rank + (FACE + 1))
    rank = jnp.where(on_face > 0.5, -1.0, rank).astype(jnp.int32).astype(jnp.int16)
    narrow_lane = lane.astype(jnp.int16)
    for j in range((nodes - FACE) // LANE):
        perm_ref[:, FACE + j * LANE:FACE + (j + 1) * LANE] = hot16(rank == narrow_lane + jnp.int16(j * LANE))
    for i in (0, 1, 3, 4, 5, 6):
        copies[i].wait()
    matrix = stiff[...]
    eye = iota(matrix.shape, 0) == iota(matrix.shape, 1)
    cell[:degree_nodes, :degree_nodes] = jnp.where(eye, 0.0, matrix.astype(F32))
    table[cells:cells + 1, :degree_nodes] = jnp.sum(
        jnp.where(eye, matrix.astype(F32), 0.0), axis=0, keepdims=True
    )
    table[:cells, :degree_nodes] = pot[...]
    links[:cells, :degree_nodes] = conn[...]
    y0 = mm(x[...], perm_ref[...])
    wide_node = iota((nodes, wide), 0)
    narrow_node = wide_node.astype(jnp.int16)
    wide_spot = jnp.concatenate([spot] * (wide // LANE), axis=1)
    tail = degree_nodes + (-degree_nodes) % 16
    row = iota((16, wide), 0)
    diagonal = jnp.zeros((1, nodes), F32)
    for c in range(cells):
        share = jnp.where(c < count[0, 0], 2.0 / HALF_WIDTH, 0.0)
        weight = share * scale[0, c]
        link = links[c:c + 1, :]
        found = jnp.sum(jnp.where(wide_node == link, wide_spot, 0.0), axis=0, keepdims=True)
        where = found.astype(jnp.int32) - 1
        select = hot16(narrow_node == where.astype(jnp.int16))
        tcat[:, c * wide:(c + 1) * wide] = select
        value = weight * table[cells:cells + 1, :] + share * table[c:c + 1, :]
        high = value.astype(BF).astype(F32)
        middle = (value - high).astype(BF).astype(F32)
        low = value - high - middle
        off[...] = (weight * cell[...]).astype(BF)
        off[tail:tail + 16, :] = jnp.where(
            row == 0, high, jnp.where(row == 1, middle, jnp.where(row == 2, low, 0.0))
        ).astype(BF)
        moved = mm_nt(off[...], select)
        diagonal = diagonal + jnp.sum(moved[tail:tail + 16], axis=0, keepdims=True)
        vcat[c * wide:(c + 1) * wide, :] = moved.astype(BF)
    diagonal_ref[...] = jnp.broadcast_to(diagonal, diagonal_ref.shape)
    for low in range(0, nodes, 2 * LANE):
        high = min(low + 2 * LANE, nodes)
        matrix_ref[low:high, low:] = mm(tcat[low:high, :], vcat[:, low:]).astype(BF)
        if high < nodes:
            matrix_ref[high:, low:high] = matrix_ref[low:high, high:].T
    y0_ref[...] = y0
    applied = apply_operator(y0, matrix_ref, diagonal_ref)
    if paired:
        rows = x.shape[0]
        rest_ref[...] = applied
        pack_faces(sends[0], applied)
        sends[0][2 * rows:, :] = matrix_ref[FY:FY + LANE, FX:FX + LANE]
    else:
        rest_ref[...] = 0.5 * (applied - y0)
        for send, at in zip(sends, spots):
            send[...] = applied[:, at:at + LANE].astype(BF)


def pack_faces(out_ref, applied):
    rows = applied.shape[0]
    out_ref[:rows, :] = applied[:, FX:FX + LANE].astype(BF)
    out_ref[rows:2 * rows, :] = applied[:, FY:FY + LANE].astype(BF)


def build(spots, paired, counts, scale, conn, pot, shared, stiff, x):
    cells, degree_nodes = conn.shape
    rows, nodes = x.shape
    wide = -(-(degree_nodes + 32) // LANE) * LANE
    f = lambda *s: jax.ShapeDtypeStruct(s, F32)
    b = lambda *s: jax.ShapeDtypeStruct(s, BF)
    outs = (b(nodes, nodes), f(8, nodes), b(nodes, nodes), f(rows, nodes), f(rows, nodes))
    outs += (b(2 * rows + LANE, LANE),) if paired else (b(rows, LANE),) * len(spots)
    return pl.pallas_call(
        functools.partial(build_kernel, spots, paired),
        out_shape=outs,
        in_specs=[HBM] * 7,
        out_specs=(VMEM,) * len(outs),
        scratch_shapes=[
            pltpu.SMEM(counts.shape, counts.dtype),
            pltpu.SMEM(scale.shape, F32),
            pltpu.VMEM(conn.shape, jnp.int32),
            pltpu.VMEM(pot.shape, F32),
            pltpu.VMEM(shared.shape, jnp.int32),
            pltpu.VMEM(stiff.shape, BF),
            pltpu.VMEM(x.shape, BF),
            pltpu.VMEM((nodes, cells * wide), BF),
            pltpu.VMEM((cells * wide, nodes), BF),
            pltpu.VMEM((wide, wide), BF),
            pltpu.VMEM((wide, wide), F32),
            pltpu.VMEM((8, wide), F32),
            pltpu.VMEM((8, wide), jnp.int32),
            pltpu.SemaphoreType.DMA((7,)),
        ],
        compiler_params=pltpu.CompilerParams(vmem_limit_bytes=40 << 20),
        cost_estimate=pl.CostEstimate(flops=5_000_000_000, bytes_accessed=5_000_000, transcendentals=0),
        name="build",
    )(counts, *(pltpu.with_memory_space_constraint(v, pltpu.HBM) for v in (scale, conn, pot, shared, stiff, x)))


def step_kernel(spots, factor, last, matrix_ref, diagonal_ref, rest_ref, before_ref, *refs):
    count = len(spots)
    received = refs[:count]
    outs = refs[count:]
    field_ref, outs = (outs[-1], outs[:-1]) if last else (outs[0], outs[1:])
    field_ref[...] = rest_ref[...]
    for got, at in zip(received, spots):
        field_ref[:, at:at + LANE] += factor * got[...].astype(F32)
    field = field_ref[...]
    applied = apply_operator(field, matrix_ref, diagonal_ref)
    outs[0][...] = applied - field - before_ref[...]
    for send, at in zip(outs[1:], spots):
        send[...] = applied[:, at:at + LANE].astype(BF)


def step(spots, factor, last, matrix, diagonal, rest, before, received):
    rows, nodes = rest.shape
    field = jax.ShapeDtypeStruct((rows, nodes), F32)
    outs = (field,) * (1 if last else 2) + (jax.ShapeDtypeStruct((rows, LANE), BF),) * len(spots)
    return pl.pallas_call(
        functools.partial(step_kernel, spots, factor, last),
        out_shape=outs,
        in_specs=[VMEM] * (4 + len(spots)),
        out_specs=(VMEM,) * len(outs),
        scratch_shapes=[pltpu.VMEM((rows, nodes), F32)] if last else [],
        compiler_params=pltpu.CompilerParams(vmem_limit_bytes=16 << 20),
        cost_estimate=pl.CostEstimate(flops=110_000_000, bytes_accessed=3_000_000, transcendentals=0),
        name="step",
    )(matrix, diagonal, rest, before, *received)


def finish_kernel(spots, rest_ref, *refs):
    received, out_ref = refs[:-1], refs[-1]
    out_ref[...] = rest_ref[...].astype(BF)
    for got, at in zip(received, spots):
        out_ref[:, at:at + LANE] = (rest_ref[:, at:at + LANE] + got[...].astype(F32)).astype(BF)


def finish(spots, rest, received):
    return pl.pallas_call(
        functools.partial(finish_kernel, spots),
        out_shape=jax.ShapeDtypeStruct(rest.shape, BF),
        in_specs=[VMEM] * (1 + len(spots)),
        out_specs=VMEM,
        compiler_params=pltpu.CompilerParams(vmem_limit_bytes=8 << 20),
        name="finish",
    )(rest, *received)


def owner_row(nodes, place_x, place_y):
    lane = iota((1, nodes), 1)
    hidden = ((lane < LANE) & (place_x > 0)) | ((lane >= 2 * LANE) & (lane < 3 * LANE) & (place_y > 0))
    return jnp.where(hidden, 0.0, 1.0)


def products_kernel(hops, own_ref, side_ref, mine_ref, other_ref, *refs):
    zs = len(hops) + 1
    columns = refs[:zs - 1]
    rot_ref, turn_ref, keep_ref, give_ref, fields, pair, coef = refs[zs - 1:]
    width, nodes = own_ref.shape
    at = lax.axis_index("band")
    z, x = at // 2, at % 2
    fields[:, 1 - x] = jnp.zeros((zs, width, nodes), BF)
    fields[z, x] = own_ref[...]
    for k, column in zip(hops, columns):
        fields[z ^ k, x] = column[...]
    coef[:width] = mine_ref[...]
    coef[width:] = other_ref[...]
    turned = mm(coef[...], fields[...].reshape(zs * 2 * width, nodes))
    rot_ref[...] = turned[:width]
    turn_ref[...] = turned[width:].astype(BF)
    owner = owner_row(nodes, lax.axis_index("dx"), lax.axis_index("dy"))
    pair[:width] = (own_ref[...].astype(F32) * owner).astype(BF)
    pair[width:] = (side_ref[...].astype(F32) * owner).astype(BF)
    p = lax.axis_index("dx") * 2 + lax.axis_index("dy")
    for j, ref in enumerate((keep_ref, keep_ref, give_ref, give_ref)):
        ref[j % 2] = mm_nt(fields[p ^ j, x], pair[...])


def products(hops, own, side, mine, other, columns):
    width, nodes = own.shape
    zs = len(hops) + 1
    f = lambda *s: jax.ShapeDtypeStruct(s, F32)
    outs = (f(width, nodes), jax.ShapeDtypeStruct((width, nodes), BF),
            f(2, width, 2 * width), f(2, width, 2 * width))
    return pl.pallas_call(
        functools.partial(products_kernel, hops),
        out_shape=outs,
        in_specs=[VMEM] * (4 + len(columns)),
        out_specs=(VMEM,) * 4,
        scratch_shapes=[
            pltpu.VMEM((zs, 2, width, nodes), BF),
            pltpu.VMEM((2 * width, nodes), BF),
            pltpu.VMEM((2 * width, zs * 2 * width), BF),
        ],
        compiler_params=pltpu.CompilerParams(vmem_limit_bytes=16 << 20),
        cost_estimate=pl.CostEstimate(flops=200_000_000, bytes_accessed=2_000_000, transcendentals=0),
        name="products",
    )(own, side, mine, other, *columns)


def rotated_kernel(mine_ref, got_ref, perm_ref, out_ref):
    total = (mine_ref[...] + got_ref[...].astype(F32)).astype(BF)
    out_ref[...] = mm_nt(total, perm_ref[...]).astype(BF)


def rotated_of(mine, got, perm):
    return pl.pallas_call(
        rotated_kernel,
        out_shape=jax.ShapeDtypeStruct(mine.shape, BF),
        in_specs=[VMEM] * 3,
        out_specs=VMEM,
        compiler_params=pltpu.CompilerParams(vmem_limit_bytes=16 << 20),
        cost_estimate=pl.CostEstimate(flops=110_000_000, bytes_accessed=3_000_000, transcendentals=0),
        name="rotated",
    )(mine, got, perm)


def margin_kernel(owned, own_ref, corner_ref, side_ref, below_ref, out_ref):
    width = own_ref.shape[0]
    x = lax.axis_index("band") % 2
    here = (own_ref[...] + below_ref[...].astype(F32)).T[:width] * (1.0 / owned)
    there = (side_ref[...].astype(F32) + corner_ref[...].astype(F32)).T[width:] * (1.0 / owned)
    out_ref[:, :width] = jnp.where(x == 0, here, there)
    out_ref[:, width:] = jnp.where(x == 0, there, here)


def margin_of(owned, *parts):
    width = parts[0].shape[0]
    return pl.pallas_call(
        functools.partial(margin_kernel, owned),
        out_shape=jax.ShapeDtypeStruct((width, 2 * width), F32),
        in_specs=[VMEM] * len(parts),
        out_specs=VMEM,
        compiler_params=pltpu.CompilerParams(vmem_limit_bytes=8 << 20),
        name="margin",
    )(*parts)


def swap(value, axis):
    return lax.ppermute(value, axis, [(0, 1), (1, 0)])


def split3(value):
    high = value.astype(BF).astype(F32)
    middle = (value - high).astype(BF).astype(F32)
    return high, middle, value - high - middle


def advance_kernel(first, matrix_ref, diagonal_ref, applied_ref, field_ref, *refs):
    before_ref = None if first else refs[0]
    got_ref, next_ref, product_ref, to_x_ref, to_y_ref = refs[0 if first else 1:]
    rows = field_ref.shape[0]
    if first:
        next_ref[...] = 0.5 * (applied_ref[...] - field_ref[...])
        next_ref[:, FX:FX + LANE] += 0.5 * got_ref[:rows, :].astype(F32)
    else:
        next_ref[...] = applied_ref[...] - field_ref[...] - before_ref[...]
        next_ref[:, FX:FX + LANE] += got_ref[:rows, :].astype(F32)
    product = apply_operator(next_ref[...], matrix_ref, diagonal_ref)
    product_ref[...] = product
    to_x_ref[...] = product[:, FX:FX + LANE].astype(BF)
    to_y_ref[:rows, :] = applied_ref[:, FY:FY + LANE].astype(BF)
    to_y_ref[rows:2 * rows, :] = product[:, FY:FY + LANE].astype(BF)
    to_y_ref[2 * rows:3 * rows, :] = got_ref[rows:2 * rows, :]
    if first:
        to_y_ref[3 * rows:3 * rows + LANE, :] = matrix_ref[FY:FY + LANE, FY:FY + LANE]
        high, middle, low = split3(diagonal_ref[0:1, FY:FY + LANE])
        row = iota((SPLIT, LANE), 0)
        to_y_ref[3 * rows + LANE:, :] = jnp.where(
            row == 0, high, jnp.where(row == 1, middle, jnp.where(row == 2, low, 0.0))
        ).astype(BF)


def advance(matrix, diagonal, applied, field, before, got):
    first = before is None
    rows, nodes = field.shape
    f = jax.ShapeDtypeStruct((rows, nodes), F32)
    down = 3 * rows + (LANE + SPLIT if first else 0)
    args = (matrix, diagonal, applied, field) + (() if first else (before,)) + (got,)
    return pl.pallas_call(
        functools.partial(advance_kernel, first),
        out_shape=(f, f, jax.ShapeDtypeStruct((rows, LANE), BF), jax.ShapeDtypeStruct((down, LANE), BF)),
        in_specs=[VMEM] * len(args),
        out_specs=(VMEM,) * 4,
        compiler_params=pltpu.CompilerParams(vmem_limit_bytes=16 << 20),
        cost_estimate=pl.CostEstimate(flops=110_000_000, bytes_accessed=3_000_000, transcendentals=0),
        name="advance",
    )(*args)


def correct_kernel(
    first, matrix_ref, diagonal_ref, applied_ref, field_ref, next_ref, product_ref,
    from_x_ref, from_y_ref, block_x_ref, block_y_ref, *outs,
):
    rows = field_ref.shape[0]
    scale = 0.5 if first else 1.0
    total_ref = outs[-1]
    given = scale * from_y_ref[:rows, :].astype(F32)
    sent = scale * applied_ref[:, FY:FY + LANE].astype(BF).astype(F32)
    corner = scale * from_y_ref[2 * rows:3 * rows, :].astype(F32)
    tail = block_y_ref[3 * rows + LANE:3 * rows + LANE + SPLIT, :].astype(F32)
    their_diagonal = tail[0:1] + tail[1:2] + tail[2:3]
    their_y = (
        from_y_ref[rows:2 * rows, :].astype(F32)
        + mm(sent.astype(BF), block_y_ref[3 * rows:3 * rows + LANE, :])
        + sent * their_diagonal
    )
    their_x = from_x_ref[...].astype(F32) + mm(corner.astype(BF), block_x_ref[2 * rows:2 * rows + LANE, :])
    total_ref[...] = (
        product_ref[...] + mm(given.astype(BF), matrix_ref[FY:FY + LANE, :])
        - next_ref[...] - field_ref[...]
    )
    total_ref[:, FX:FX + LANE] += their_x
    total_ref[:, FY:FY + LANE] += their_y + given * (diagonal_ref[0:1, FY:FY + LANE] - 1.0)
    if first:
        middle_ref, second_ref, again_ref, pack_ref = outs[:-1]
        middle_ref[...] = next_ref[...]
        middle_ref[:, FY:FY + LANE] += given
        second = total_ref[...]
        second_ref[...] = second
        applied = apply_operator(second, matrix_ref, diagonal_ref)
        again_ref[...] = applied
        pack_faces(pack_ref, applied)
    else:
        outs[0][...] = total_ref[...].astype(BF)


def correct(first, matrix, diagonal, applied, field, ahead, product, from_x, from_y, block_x, block_y):
    rows, nodes = field.shape
    f = jax.ShapeDtypeStruct((rows, nodes), F32)
    outs = (f, f, f, jax.ShapeDtypeStruct((2 * rows, LANE), BF)) if first else (jax.ShapeDtypeStruct((rows, nodes), BF),)
    return pl.pallas_call(
        functools.partial(correct_kernel, first),
        out_shape=outs,
        in_specs=[VMEM] * 10,
        out_specs=(VMEM,) * len(outs),
        scratch_shapes=[pltpu.VMEM((rows, nodes), F32)],
        compiler_params=pltpu.CompilerParams(vmem_limit_bytes=16 << 20),
        cost_estimate=pl.CostEstimate(flops=150_000_000, bytes_accessed=3_000_000, transcendentals=0),
        name="correct",
    )(matrix, diagonal, applied, field, ahead, product, from_x, from_y, block_x, block_y)


def filter_pairs(matrix, diagonal, field, applied, pack):
    block_x = got = swap(pack, "dx")
    ahead, product, to_x, to_y = advance(matrix, diagonal, applied, field, None, got)
    block_y = swap(to_y, "dy")
    field, second, applied, pack = correct(
        True, matrix, diagonal, applied, field, ahead, product, swap(to_x, "dx"), block_y, block_x, block_y
    )
    got = swap(pack, "dx")
    ahead, product, to_x, to_y = advance(matrix, diagonal, applied, second, field, got)
    return correct(
        False, matrix, diagonal, applied, second, ahead, product, swap(to_x, "dx"), swap(to_y, "dy"), block_x, block_y
    )[0]


def from_behind(block, axis, distance):
    devices = range(lax.axis_size(axis))
    route = [(i - distance, i) for i in devices if i - distance in devices]
    return lax.ppermute(block, axis, route)


def on_device(waves, stiff, cell_scale, cell_pot, conn, counts, shared, rotation):
    width, nodes = waves.shape[0], waves.shape[3]
    cells, degree_nodes = conn.shape[2:]
    share = shared.shape[3]
    count_x, count_y = lax.axis_size("dx"), lax.axis_size("dy")
    bands = lax.axis_size("band")
    owned = nodes * count_x * count_y - share * (2 * count_x * count_y - count_x - count_y)
    paired = count_x == 2 and count_y == 2 and bands == 2 * count_x * count_y
    x = waves.reshape(width, nodes)
    spots = (0, LANE, 2 * LANE, 3 * LANE)

    def exchange(sends):
        return (
            from_behind(sends[1], "dx", 1), from_behind(sends[0], "dx", -1),
            from_behind(sends[3], "dy", 1), from_behind(sends[2], "dy", -1),
        )

    matrix, diagonal, perm, before, rest, *sends = build(
        spots, paired, counts, cell_scale.reshape(1, cells),
        conn.reshape(cells, degree_nodes), cell_pot.reshape(cells, degree_nodes),
        shared.reshape(4, share), stiff, x,
    )
    if paired:
        filtered = filter_pairs(matrix, diagonal, before, rest, sends[0])
    else:
        for degree_step in range(DEGREE - 1):
            factor = 0.5 if degree_step == 0 else 1.0
            received = exchange(sends)
            if degree_step < DEGREE - 2:
                field, rest, *sends = step(spots, factor, False, matrix, diagonal, rest, before, received)
                before = field
            else:
                rest, *sends = step(spots, factor, True, matrix, diagonal, rest, before, received)
        filtered = finish(spots, rest, exchange(sends))

    if paired:
        across = [(i, i ^ 1) for i in range(bands)]
        other = lax.ppermute(rotation, "band", across)
        hops = (3, 1, 2)
        routes = [[(i, i ^ (2 * k)) for i in range(bands)] for k in hops]
        columns = [lax.ppermute(filtered, "band", route) for route in routes[:2]]
        side = lax.ppermute(filtered, "band", across)
        columns.append(lax.ppermute(filtered, "band", routes[2]))
        mine, turn, keep, give = products(hops, filtered, side, rotation, other, columns)
        got = lax.ppermute(turn, "band", across)
        corner = [
            (2 * i + j, 2 * (i ^ 1) + (j ^ 1)) for i in range(bands) for j in range(count_y)
        ]
        half = keep + swap(give, "dx")
        own, below = half[0], half[1].astype(BF)
        aside, away = own.astype(BF), below
        rotated = rotated_of(mine, got, perm)
        below = swap(below, "dy")
        aside = lax.ppermute(aside, "band", across)
        away = lax.ppermute(away, ("band", "dy"), corner)
        own, rotated = lax.optimization_barrier((own, rotated))
        margin = margin_of(owned, own, away, aside, below)
    else:
        gathered = lax.all_gather(filtered, "band", axis=0, tiled=True)
        owner = owner_row(nodes, lax.axis_index("dx"), lax.axis_index("dy")).astype(BF)
        block = mm_nt(filtered * owner, gathered)
        block = lax.psum_scatter(block, ("dx", "dy"), scatter_dimension=1, tiled=True)
        margin = block * (1.0 / owned)
        rotated = mm_nt(mm(rotation, gathered).astype(BF), perm).astype(BF)
    return margin, rotated.reshape(width, 1, 1, nodes)


def solution(mesh):
    return jax.shard_map(
        on_device,
        mesh=mesh,
        in_specs=(
            P("band", "dx", "dy", None),
            P(),
            P("dx", "dy", None),
            P("dx", "dy", None, None),
            P("dx", "dy", None, None),
            P("dx", "dy"),
            P("dx", "dy", None, None),
            P("band", None),
        ),
        out_specs=(P("band", ("dx", "dy")), P("band", "dx", "dy", None)),
        check_vma=False,
    )
```

```python
import functools

import jax
import jax.numpy as jnp
from jax import lax
from jax.experimental import pallas as pl
from jax.experimental.pallas import tpu as pltpu
from jax.sharding import PartitionSpec as P

DEGREE = 4
LANE = 128
SHIFT_CENTER = 3.0
HALF_WIDTH = 6.0
BF = jnp.bfloat16
F32 = jnp.float32
NT = (((1,), (1,)), ((), ()))
FACE = 4 * LANE
FX, FY = 0, 2 * LANE
SPLIT = 16

VMEM = pl.BlockSpec(memory_space=pltpu.VMEM)
HBM = pl.BlockSpec(memory_space=pltpu.HBM)


def iota(shape, dim):
    return lax.broadcasted_iota(jnp.int32, shape, dim)


def hot(mask):
    return jnp.where(mask, 1.0, 0.0).astype(BF)


def hot16(mask):
    return jnp.where(mask, jnp.ones((), BF), jnp.zeros((), BF))


def mm(a, b):
    return jnp.dot(a, b, preferred_element_type=F32)


def mm_nt(a, b):
    return lax.dot_general(a, b, NT, preferred_element_type=F32)


def apply_operator(field, matrix_ref, diagonal_ref):
    return mm(field.astype(BF), matrix_ref[...]) + field * diagonal_ref[0:1, :]


def build_kernel(
    spots, paired,
    counts_hbm, scale_hbm, conn_hbm, pot_hbm, shared_hbm, stiff_hbm, x_hbm,
    matrix_ref, diagonal_ref, perm_ref, y0_ref, rest_ref, *outs_and_scratch,
):
    count_out = 1 if paired else len(spots)
    sends = outs_and_scratch[:count_out]
    (count, scale, conn, pot, shared, stiff, x, tcat, vcat, off, cell, table, links, sems) = outs_and_scratch[count_out:]
    copies = [
        pltpu.make_async_copy(src, dst, sems.at[i])
        for i, (src, dst) in enumerate(
            ((counts_hbm, count), (scale_hbm, scale), (shared_hbm, shared), (conn_hbm, conn),
             (pot_hbm, pot), (stiff_hbm, stiff), (x_hbm, x))
        )
    ]
    for copy in copies:
        copy.start()
    cells, degree_nodes = conn.shape
    nodes = x.shape[1]
    wide = off.shape[0]
    cell[...] = jnp.zeros_like(cell)
    table[...] = jnp.zeros_like(table)
    links[...] = jnp.full(links.shape, -1, jnp.int32)
    copies[2].wait()
    if paired:
        first_x = 1 - lax.axis_index("dx")
        first_y = 1 - lax.axis_index("dy")
        order = (first_x, 1 - first_x, 2 + first_y, 3 - first_y)
    else:
        order = (0, 1, 2, 3)
    node = iota((nodes, LANE), 0)
    lane = iota((nodes, LANE), 1)
    spot = jnp.zeros((nodes, LANE), F32)
    for i in range(4):
        hit = node == shared[pl.ds(order[i], 1), :]
        perm_ref[:, i * LANE:(i + 1) * LANE] = hot(hit)
        spot = spot + jnp.where(hit, (lane + (i * LANE + 1)).astype(F32), 0.0)
    spot = jnp.broadcast_to(jnp.sum(spot, axis=1, keepdims=True), (nodes, LANE))
    on_face = (spot > 0.0).astype(F32)
    inner = (1.0 - on_face).astype(BF)
    below = hot(iota((LANE, LANE), 1) < iota((LANE, LANE), 0))
    ranks = []
    seen = jnp.zeros((1, LANE), F32)
    for j in range(nodes // LANE):
        part = inner[j * LANE:(j + 1) * LANE]
        ranks.append(mm(below, part) + seen)
        seen = seen + jnp.sum(part.astype(F32), axis=0, keepdims=True)
    rank = jnp.concatenate(ranks, axis=0)
    spot = jnp.where(on_face > 0.5, spot, rank + (FACE + 1))
    rank = jnp.where(on_face > 0.5, -1.0, rank).astype(jnp.int32).astype(jnp.int16)
    narrow_lane = lane.astype(jnp.int16)
    for j in range((nodes - FACE) // LANE):
        perm_ref[:, FACE + j * LANE:FACE + (j + 1) * LANE] = hot16(rank == narrow_lane + jnp.int16(j * LANE))
    for i in (0, 1, 3, 4, 5, 6):
        copies[i].wait()
    matrix = stiff[...]
    eye = iota(matrix.shape, 0) == iota(matrix.shape, 1)
    cell[:degree_nodes, :degree_nodes] = jnp.where(eye, 0.0, matrix.astype(F32))
    table[cells:cells + 1, :degree_nodes] = jnp.sum(
        jnp.where(eye, matrix.astype(F32), 0.0), axis=0, keepdims=True
    )
    table[:cells, :degree_nodes] = pot[...]
    links[:cells, :degree_nodes] = conn[...]
    y0 = mm(x[...], perm_ref[...])
    wide_node = iota((nodes, wide), 0)
    narrow_node = wide_node.astype(jnp.int16)
    wide_spot = jnp.concatenate([spot] * (wide // LANE), axis=1)
    tail = degree_nodes + (-degree_nodes) % 16
    row = iota((16, wide), 0)
    diagonal = jnp.zeros((1, nodes), F32)
    for c in range(cells):
        share = jnp.where(c < count[0, 0], 2.0 / HALF_WIDTH, 0.0)
        weight = share * scale[0, c]
        link = links[c:c + 1, :]
        found = jnp.sum(jnp.where(wide_node == link, wide_spot, 0.0), axis=0, keepdims=True)
        where = found.astype(jnp.int32) - 1
        select = hot16(narrow_node == where.astype(jnp.int16))
        tcat[:, c * wide:(c + 1) * wide] = select
        value = weight * table[cells:cells + 1, :] + share * table[c:c + 1, :]
        high = value.astype(BF).astype(F32)
        middle = (value - high).astype(BF).astype(F32)
        low = value - high - middle
        off[...] = (weight * cell[...]).astype(BF)
        off[tail:tail + 16, :] = jnp.where(
            row == 0, high, jnp.where(row == 1, middle, jnp.where(row == 2, low, 0.0))
        ).astype(BF)
        moved = mm_nt(off[...], select)
        diagonal = diagonal + jnp.sum(moved[tail:tail + 16], axis=0, keepdims=True)
        vcat[c * wide:(c + 1) * wide, :] = moved.astype(BF)
    diagonal_ref[...] = jnp.broadcast_to(diagonal, diagonal_ref.shape)
    for low in range(0, nodes, 2 * LANE):
        high = min(low + 2 * LANE, nodes)
        matrix_ref[low:high, low:] = mm(tcat[low:high, :], vcat[:, low:]).astype(BF)
        if high < nodes:
            matrix_ref[high:, low:high] = matrix_ref[low:high, high:].T
    y0_ref[...] = y0
    applied = apply_operator(y0, matrix_ref, diagonal_ref)
    if paired:
        rows = x.shape[0]
        rest_ref[...] = applied
        pack_faces(sends[0], applied)
        sends[0][2 * rows:, :] = matrix_ref[FY:FY + LANE, FX:FX + LANE]
    else:
        rest_ref[...] = 0.5 * (applied - y0)
        for send, at in zip(sends, spots):
            send[...] = applied[:, at:at + LANE].astype(BF)


def pack_faces(out_ref, applied):
    rows = applied.shape[0]
    out_ref[:rows, :] = applied[:, FX:FX + LANE].astype(BF)
    out_ref[rows:2 * rows, :] = applied[:, FY:FY + LANE].astype(BF)


def build(spots, paired, counts, scale, conn, pot, shared, stiff, x):
    cells, degree_nodes = conn.shape
    rows, nodes = x.shape
    wide = -(-(degree_nodes + 32) // LANE) * LANE
    f = lambda *s: jax.ShapeDtypeStruct(s, F32)
    b = lambda *s: jax.ShapeDtypeStruct(s, BF)
    outs = (b(nodes, nodes), f(8, nodes), b(nodes, nodes), f(rows, nodes), f(rows, nodes))
    outs += (b(2 * rows + LANE, LANE),) if paired else (b(rows, LANE),) * len(spots)
    return pl.pallas_call(
        functools.partial(build_kernel, spots, paired),
        out_shape=outs,
        in_specs=[HBM] * 7,
        out_specs=(VMEM,) * len(outs),
        scratch_shapes=[
            pltpu.SMEM(counts.shape, counts.dtype),
            pltpu.SMEM(scale.shape, F32),
            pltpu.VMEM(conn.shape, jnp.int32),
            pltpu.VMEM(pot.shape, F32),
            pltpu.VMEM(shared.shape, jnp.int32),
            pltpu.VMEM(stiff.shape, BF),
            pltpu.VMEM(x.shape, BF),
            pltpu.VMEM((nodes, cells * wide), BF),
            pltpu.VMEM((cells * wide, nodes), BF),
            pltpu.VMEM((wide, wide), BF),
            pltpu.VMEM((wide, wide), F32),
            pltpu.VMEM((8, wide), F32),
            pltpu.VMEM((8, wide), jnp.int32),
            pltpu.SemaphoreType.DMA((7,)),
        ],
        compiler_params=pltpu.CompilerParams(vmem_limit_bytes=40 << 20),
        cost_estimate=pl.CostEstimate(flops=5_000_000_000, bytes_accessed=5_000_000, transcendentals=0),
        name="build",
    )(counts, *(pltpu.with_memory_space_constraint(v, pltpu.HBM) for v in (scale, conn, pot, shared, stiff, x)))


def step_kernel(spots, factor, last, matrix_ref, diagonal_ref, rest_ref, before_ref, *refs):
    count = len(spots)
    received = refs[:count]
    outs = refs[count:]
    field_ref, outs = (outs[-1], outs[:-1]) if last else (outs[0], outs[1:])
    field_ref[...] = rest_ref[...]
    for got, at in zip(received, spots):
        field_ref[:, at:at + LANE] += factor * got[...].astype(F32)
    field = field_ref[...]
    applied = apply_operator(field, matrix_ref, diagonal_ref)
    outs[0][...] = applied - field - before_ref[...]
    for send, at in zip(outs[1:], spots):
        send[...] = applied[:, at:at + LANE].astype(BF)


def step(spots, factor, last, matrix, diagonal, rest, before, received):
    rows, nodes = rest.shape
    field = jax.ShapeDtypeStruct((rows, nodes), F32)
    outs = (field,) * (1 if last else 2) + (jax.ShapeDtypeStruct((rows, LANE), BF),) * len(spots)
    return pl.pallas_call(
        functools.partial(step_kernel, spots, factor, last),
        out_shape=outs,
        in_specs=[VMEM] * (4 + len(spots)),
        out_specs=(VMEM,) * len(outs),
        scratch_shapes=[pltpu.VMEM((rows, nodes), F32)] if last else [],
        compiler_params=pltpu.CompilerParams(vmem_limit_bytes=16 << 20),
        cost_estimate=pl.CostEstimate(flops=110_000_000, bytes_accessed=3_000_000, transcendentals=0),
        name="step",
    )(matrix, diagonal, rest, before, *received)


def finish_kernel(spots, rest_ref, *refs):
    received, out_ref = refs[:-1], refs[-1]
    out_ref[...] = rest_ref[...].astype(BF)
    for got, at in zip(received, spots):
        out_ref[:, at:at + LANE] = (rest_ref[:, at:at + LANE] + got[...].astype(F32)).astype(BF)


def finish(spots, rest, received):
    return pl.pallas_call(
        functools.partial(finish_kernel, spots),
        out_shape=jax.ShapeDtypeStruct(rest.shape, BF),
        in_specs=[VMEM] * (1 + len(spots)),
        out_specs=VMEM,
        compiler_params=pltpu.CompilerParams(vmem_limit_bytes=8 << 20),
        name="finish",
    )(rest, *received)


def owner_row(nodes, place_x, place_y):
    lane = iota((1, nodes), 1)
    hidden = ((lane < LANE) & (place_x > 0)) | ((lane >= 2 * LANE) & (lane < 3 * LANE) & (place_y > 0))
    return jnp.where(hidden, 0.0, 1.0)


def products_kernel(hops, own_ref, side_ref, mine_ref, other_ref, *refs):
    zs = len(hops) + 1
    columns = refs[:zs - 1]
    rot_ref, turn_ref, keep_ref, give_ref, fields, pair, coef = refs[zs - 1:]
    width, nodes = own_ref.shape
    at = lax.axis_index("band")
    z, x = at // 2, at % 2
    fields[:, 1 - x] = jnp.zeros((zs, width, nodes), BF)
    fields[z, x] = own_ref[...]
    for k, column in zip(hops, columns):
        fields[z ^ k, x] = column[...]
    coef[:width] = mine_ref[...]
    coef[width:] = other_ref[...]
    turned = mm(coef[...], fields[...].reshape(zs * 2 * width, nodes))
    rot_ref[...] = turned[:width]
    turn_ref[...] = turned[width:].astype(BF)
    owner = owner_row(nodes, lax.axis_index("dx"), lax.axis_index("dy"))
    pair[:width] = (own_ref[...].astype(F32) * owner).astype(BF)
    pair[width:] = (side_ref[...].astype(F32) * owner).astype(BF)
    p = lax.axis_index("dx") * 2 + lax.axis_index("dy")
    for j, ref in enumerate((keep_ref, keep_ref, give_ref, give_ref)):
        ref[j % 2] = mm_nt(fields[p ^ j, x], pair[...]).astype(ref.dtype)


def products(hops, own, side, mine, other, columns):
    width, nodes = own.shape
    zs = len(hops) + 1
    f = lambda *s: jax.ShapeDtypeStruct(s, F32)
    outs = (f(width, nodes), jax.ShapeDtypeStruct((width, nodes), BF),
            f(2, width, 2 * width), jax.ShapeDtypeStruct((2, width, 2 * width), BF))
    return pl.pallas_call(
        functools.partial(products_kernel, hops),
        out_shape=outs,
        in_specs=[VMEM] * (4 + len(columns)),
        out_specs=(VMEM,) * 4,
        scratch_shapes=[
            pltpu.VMEM((zs, 2, width, nodes), BF),
            pltpu.VMEM((2 * width, nodes), BF),
            pltpu.VMEM((2 * width, zs * 2 * width), BF),
        ],
        compiler_params=pltpu.CompilerParams(vmem_limit_bytes=16 << 20),
        cost_estimate=pl.CostEstimate(flops=200_000_000, bytes_accessed=2_000_000, transcendentals=0),
        name="products",
    )(own, side, mine, other, *columns)


def rotated_kernel(mine_ref, got_ref, perm_ref, out_ref):
    total = (mine_ref[...] + got_ref[...].astype(F32)).astype(BF)
    out_ref[...] = mm_nt(total, perm_ref[...]).astype(BF)


def rotated_of(mine, got, perm):
    return pl.pallas_call(
        rotated_kernel,
        out_shape=jax.ShapeDtypeStruct(mine.shape, BF),
        in_specs=[VMEM] * 3,
        out_specs=VMEM,
        compiler_params=pltpu.CompilerParams(vmem_limit_bytes=16 << 20),
        cost_estimate=pl.CostEstimate(flops=110_000_000, bytes_accessed=3_000_000, transcendentals=0),
        name="rotated",
    )(mine, got, perm)


def margin_kernel(owned, own_ref, corner_ref, side_ref, below_ref, out_ref):
    width = own_ref.shape[0]
    x = lax.axis_index("band") % 2
    here = (own_ref[...] + below_ref[...].astype(F32)).T[:width] * (1.0 / owned)
    there = (side_ref[...].astype(F32) + corner_ref[...].astype(F32)).T[width:] * (1.0 / owned)
    out_ref[:, :width] = jnp.where(x == 0, here, there)
    out_ref[:, width:] = jnp.where(x == 0, there, here)


def margin_of(owned, *parts):
    width = parts[0].shape[0]
    return pl.pallas_call(
        functools.partial(margin_kernel, owned),
        out_shape=jax.ShapeDtypeStruct((width, 2 * width), F32),
        in_specs=[VMEM] * len(parts),
        out_specs=VMEM,
        compiler_params=pltpu.CompilerParams(vmem_limit_bytes=8 << 20),
        name="margin",
    )(*parts)


def swap(value, axis):
    return lax.ppermute(value, axis, [(0, 1), (1, 0)])


def split3(value):
    high = value.astype(BF).astype(F32)
    middle = (value - high).astype(BF).astype(F32)
    return high, middle, value - high - middle


def advance_kernel(first, matrix_ref, diagonal_ref, applied_ref, field_ref, *refs):
    before_ref = None if first else refs[0]
    got_ref, next_ref, product_ref, to_x_ref, to_y_ref = refs[0 if first else 1:]
    rows = field_ref.shape[0]
    if first:
        next_ref[...] = 0.5 * (applied_ref[...] - field_ref[...])
        next_ref[:, FX:FX + LANE] += 0.5 * got_ref[:rows, :].astype(F32)
    else:
        next_ref[...] = applied_ref[...] - field_ref[...] - before_ref[...]
        next_ref[:, FX:FX + LANE] += got_ref[:rows, :].astype(F32)
    product = apply_operator(next_ref[...], matrix_ref, diagonal_ref)
    product_ref[...] = product
    to_x_ref[...] = product[:, FX:FX + LANE].astype(BF)
    to_y_ref[:rows, :] = applied_ref[:, FY:FY + LANE].astype(BF)
    to_y_ref[rows:2 * rows, :] = product[:, FY:FY + LANE].astype(BF)
    to_y_ref[2 * rows:3 * rows, :] = got_ref[rows:2 * rows, :]
    if first:
        to_y_ref[3 * rows:3 * rows + LANE, :] = matrix_ref[FY:FY + LANE, FY:FY + LANE]
        high, middle, low = split3(diagonal_ref[0:1, FY:FY + LANE])
        row = iota((SPLIT, LANE), 0)
        to_y_ref[3 * rows + LANE:, :] = jnp.where(
            row == 0, high, jnp.where(row == 1, middle, jnp.where(row == 2, low, 0.0))
        ).astype(BF)


def advance(matrix, diagonal, applied, field, before, got):
    first = before is None
    rows, nodes = field.shape
    f = jax.ShapeDtypeStruct((rows, nodes), F32)
    down = 3 * rows + (LANE + SPLIT if first else 0)
    args = (matrix, diagonal, applied, field) + (() if first else (before,)) + (got,)
    return pl.pallas_call(
        functools.partial(advance_kernel, first),
        out_shape=(f, f, jax.ShapeDtypeStruct((rows, LANE), BF), jax.ShapeDtypeStruct((down, LANE), BF)),
        in_specs=[VMEM] * len(args),
        out_specs=(VMEM,) * 4,
        compiler_params=pltpu.CompilerParams(vmem_limit_bytes=16 << 20),
        cost_estimate=pl.CostEstimate(flops=110_000_000, bytes_accessed=3_000_000, transcendentals=0),
        name="advance",
    )(*args)


def correct_kernel(
    first, matrix_ref, diagonal_ref, applied_ref, field_ref, next_ref, product_ref,
    from_x_ref, from_y_ref, block_x_ref, block_y_ref, *outs,
):
    rows = field_ref.shape[0]
    scale = 0.5 if first else 1.0
    total_ref = outs[-1]
    given = scale * from_y_ref[:rows, :].astype(F32)
    sent = scale * applied_ref[:, FY:FY + LANE].astype(BF).astype(F32)
    corner = scale * from_y_ref[2 * rows:3 * rows, :].astype(F32)
    tail = block_y_ref[3 * rows + LANE:3 * rows + LANE + SPLIT, :].astype(F32)
    their_diagonal = tail[0:1] + tail[1:2] + tail[2:3]
    their_y = (
        from_y_ref[rows:2 * rows, :].astype(F32)
        + mm(sent.astype(BF), block_y_ref[3 * rows:3 * rows + LANE, :])
        + sent * their_diagonal
    )
    their_x = from_x_ref[...].astype(F32) + mm(corner.astype(BF), block_x_ref[2 * rows:2 * rows + LANE, :])
    total_ref[...] = (
        product_ref[...] + mm(given.astype(BF), matrix_ref[FY:FY + LANE, :])
        - next_ref[...] - field_ref[...]
    )
    total_ref[:, FX:FX + LANE] += their_x
    total_ref[:, FY:FY + LANE] += their_y + given * (diagonal_ref[0:1, FY:FY + LANE] - 1.0)
    if first:
        middle_ref, second_ref, again_ref, pack_ref = outs[:-1]
        middle_ref[...] = next_ref[...]
        middle_ref[:, FY:FY + LANE] += given
        second = total_ref[...]
        second_ref[...] = second
        applied = apply_operator(second, matrix_ref, diagonal_ref)
        again_ref[...] = applied
        pack_faces(pack_ref, applied)
    else:
        outs[0][...] = total_ref[...].astype(BF)


def correct(first, matrix, diagonal, applied, field, ahead, product, from_x, from_y, block_x, block_y):
    rows, nodes = field.shape
    f = jax.ShapeDtypeStruct((rows, nodes), F32)
    outs = (f, f, f, jax.ShapeDtypeStruct((2 * rows, LANE), BF)) if first else (jax.ShapeDtypeStruct((rows, nodes), BF),)
    return pl.pallas_call(
        functools.partial(correct_kernel, first),
        out_shape=outs,
        in_specs=[VMEM] * 10,
        out_specs=(VMEM,) * len(outs),
        scratch_shapes=[pltpu.VMEM((rows, nodes), F32)],
        compiler_params=pltpu.CompilerParams(vmem_limit_bytes=16 << 20),
        cost_estimate=pl.CostEstimate(flops=150_000_000, bytes_accessed=3_000_000, transcendentals=0),
        name="correct",
    )(matrix, diagonal, applied, field, ahead, product, from_x, from_y, block_x, block_y)


def filter_pairs(matrix, diagonal, field, applied, pack):
    block_x = got = swap(pack, "dx")
    ahead, product, to_x, to_y = advance(matrix, diagonal, applied, field, None, got)
    block_y = swap(to_y, "dy")
    field, second, applied, pack = correct(
        True, matrix, diagonal, applied, field, ahead, product, swap(to_x, "dx"), block_y, block_x, block_y
    )
    got = swap(pack, "dx")
    ahead, product, to_x, to_y = advance(matrix, diagonal, applied, second, field, got)
    return correct(
        False, matrix, diagonal, applied, second, ahead, product, swap(to_x, "dx"), swap(to_y, "dy"), block_x, block_y
    )[0]


def from_behind(block, axis, distance):
    devices = range(lax.axis_size(axis))
    route = [(i - distance, i) for i in devices if i - distance in devices]
    return lax.ppermute(block, axis, route)


def on_device(waves, stiff, cell_scale, cell_pot, conn, counts, shared, rotation):
    width, nodes = waves.shape[0], waves.shape[3]
    cells, degree_nodes = conn.shape[2:]
    share = shared.shape[3]
    count_x, count_y = lax.axis_size("dx"), lax.axis_size("dy")
    bands = lax.axis_size("band")
    owned = nodes * count_x * count_y - share * (2 * count_x * count_y - count_x - count_y)
    paired = count_x == 2 and count_y == 2 and bands == 2 * count_x * count_y
    x = waves.reshape(width, nodes)
    spots = (0, LANE, 2 * LANE, 3 * LANE)

    def exchange(sends):
        return (
            from_behind(sends[1], "dx", 1), from_behind(sends[0], "dx", -1),
            from_behind(sends[3], "dy", 1), from_behind(sends[2], "dy", -1),
        )

    matrix, diagonal, perm, before, rest, *sends = build(
        spots, paired, counts, cell_scale.reshape(1, cells),
        conn.reshape(cells, degree_nodes), cell_pot.reshape(cells, degree_nodes),
        shared.reshape(4, share), stiff, x,
    )
    if paired:
        filtered = filter_pairs(matrix, diagonal, before, rest, sends[0])
    else:
        for degree_step in range(DEGREE - 1):
            factor = 0.5 if degree_step == 0 else 1.0
            received = exchange(sends)
            if degree_step < DEGREE - 2:
                field, rest, *sends = step(spots, factor, False, matrix, diagonal, rest, before, received)
                before = field
            else:
                rest, *sends = step(spots, factor, True, matrix, diagonal, rest, before, received)
        filtered = finish(spots, rest, exchange(sends))

    if paired:
        across = [(i, i ^ 1) for i in range(bands)]
        other = lax.ppermute(rotation, "band", across)
        hops = (3, 1, 2)
        routes = [[(i, i ^ (2 * k)) for i in range(bands)] for k in hops]
        columns = [lax.ppermute(filtered, "band", route) for route in routes[:2]]
        side = lax.ppermute(filtered, "band", across)
        columns.append(lax.ppermute(filtered, "band", routes[2]))
        mine, turn, keep, give = products(hops, filtered, side, rotation, other, columns)
        got = lax.ppermute(turn, "band", across)
        corner = [
            (2 * i + j, 2 * (i ^ 1) + (j ^ 1)) for i in range(bands) for j in range(count_y)
        ]
        half = keep + swap(give, "dx").astype(F32)
        own, below = half[0], half[1].astype(BF)
        aside, away = own.astype(BF), below
        rotated = rotated_of(mine, got, perm)
        below = swap(below, "dy")
        aside = lax.ppermute(aside, "band", across)
        away = lax.ppermute(away, ("band", "dy"), corner)
        own, rotated = lax.optimization_barrier((own, rotated))
        margin = margin_of(owned, own, away, aside, below)
    else:
        gathered = lax.all_gather(filtered, "band", axis=0, tiled=True)
        owner = owner_row(nodes, lax.axis_index("dx"), lax.axis_index("dy")).astype(BF)
        block = mm_nt(filtered * owner, gathered)
        block = lax.psum_scatter(block, ("dx", "dy"), scatter_dimension=1, tiled=True)
        margin = block * (1.0 / owned)
        rotated = mm_nt(mm(rotation, gathered).astype(BF), perm).astype(BF)
    return margin, rotated.reshape(width, 1, 1, nodes)


def solution(mesh):
    return jax.shard_map(
        on_device,
        mesh=mesh,
        in_specs=(
            P("band", "dx", "dy", None),
            P(),
            P("dx", "dy", None),
            P("dx", "dy", None, None),
            P("dx", "dy", None, None),
            P("dx", "dy"),
            P("dx", "dy", None, None),
            P("band", None),
        ),
        out_specs=(P("band", ("dx", "dy")), P("band", "dx", "dy", None)),
        check_vma=False,
    )
```
